32 devices in a mesh: dp: 8 (over y, x, core), mp: 4 (over z).
Axes of the slice: x: 2, y: 2, z: 4, core: 2. Of those that a mesh axis runs over, the one named last changes fastest.
Arguments:
- tokens: bfloat16 [2, 8192, 2560], P(None, ('dp', 'mp')), may hold values from -6 to 6
- cotangent: bfloat16 [2, 8192, 2560], P(None, ('dp', 'mp')), may hold values from -6 to 6
- parents: int32 [2, 8, 8], P(None, 'dp'), may hold values from 0 to 6, as said below
- latent_weight: float32 [2560, 1056], P('dp', 'mp'), may hold values from -0.125 to 0.125
- latent_first: float32 [2560, 1056], P('dp', 'mp')
- latent_second: float32 [2560, 1056], P('dp', 'mp'), as said below
- latent_stat: float32 [160, 16, 16], P('dp'), as said below
- latent_basis: float32 [160, 16, 16], P('dp'), as said below
- query_weight: float32 [768, 3840], P('dp', 'mp'), may hold values from -0.3125 to 0.3125
- query_first: float32 [768, 3840], P('dp', 'mp')
- query_second: float32 [768, 3840], P('dp', 'mp'), as said below
- query_stat: float32 [48, 16, 16], P('dp'), as said below
- query_basis: float32 [48, 16, 16], P('dp'), as said below
- keyval_weight: float32 [256, 5120], P('dp', 'mp'), may hold values from -0.375 to 0.375
- keyval_first: float32 [256, 5120], P('dp', 'mp')
- keyval_second: float32 [256, 5120], P('dp', 'mp'), as said below
- keyval_stat: float32 [16, 16, 16], P('dp'), as said below
- keyval_basis: float32 [16, 16, 16], P('dp'), as said below
- project_weight: float32 [2560, 2560], P('dp', 'mp'), may hold values from -4 to 4
- project_first: float32 [2560, 2560], P('dp', 'mp')
- project_second: float32 [2560, 2560], P('dp', 'mp'), as said below
- project_stat: float32 [160, 16, 16], P('dp'), as said below
- project_basis: float32 [160, 16, 16], P('dp'), as said below
- gateup_weight: float32 [2560, 2, 6400], P('dp', None, 'mp'), may hold values from -0.125 to 0.125
- gateup_first: float32 [2560, 2, 6400], P('dp', None, 'mp')
- gateup_second: float32 [2560, 2, 6400], P('dp', None, 'mp'), as said below
- gateup_stat: float32 [160, 16, 16], P('dp'), as said below
- gateup_basis: float32 [160, 16, 16], P('dp'), as said below
- down_weight: float32 [2560, 6400], P('dp', 'mp'), may hold values from -0.8 to 0.8
- down_first: float32 [2560, 6400], P('dp', 'mp')
- down_second: float32 [2560, 6400], P('dp', 'mp'), as said below
- down_stat: float32 [160, 16, 16], P('dp'), as said below
- down_basis: float32 [160, 16, 16], P('dp'), as said below
- gains: float32 [6144], P('dp'), may hold values from 0.5 to 1.5
- gains_first: float32 [6144], P('dp')
- gains_second: float32 [6144], P('dp'), as said below
Outputs:
- layer_out: bfloat16 [2, 8192, 2560], P(None, ('dp', 'mp'))
- input_grad: float32 [2, 8192, 2560], P(None, ('dp', 'mp'))
- latent_new: float32 [2560, 1056], P('dp', 'mp')
- latent_copy: bfloat16 [2560, 1056], P('dp', 'mp')
- latent_first_new: float32 [2560, 1056], P('dp', 'mp')
- latent_second_new: float32 [2560, 1056], P('dp', 'mp')
- latent_stat_new: float32 [160, 16, 16], P('dp')
- latent_basis_new: float32 [160, 16, 16], P('dp')
- query_new: float32 [768, 3840], P('dp', 'mp')
- query_copy: bfloat16 [768, 3840], P('dp', 'mp')
- query_first_new: float32 [768, 3840], P('dp', 'mp')
- query_second_new: float32 [768, 3840], P('dp', 'mp')
- query_stat_new: float32 [48, 16, 16], P('dp')
- query_basis_new: float32 [48, 16, 16], P('dp')
- keyval_new: float32 [256, 5120], P('dp', 'mp')
- keyval_copy: bfloat16 [256, 5120], P('dp', 'mp')
- keyval_first_new: float32 [256, 5120], P('dp', 'mp')
- keyval_second_new: float32 [256, 5120], P('dp', 'mp')
- keyval_stat_new: float32 [16, 16, 16], P('dp')
- keyval_basis_new: float32 [16, 16, 16], P('dp')
- project_new: float32 [2560, 2560], P('dp', 'mp')
- project_copy: bfloat16 [2560, 2560], P('dp', 'mp')
- project_first_new: float32 [2560, 2560], P('dp', 'mp')
- project_second_new: float32 [2560, 2560], P('dp', 'mp')
- project_stat_new: float32 [160, 16, 16], P('dp')
- project_basis_new: float32 [160, 16, 16], P('dp')
- gateup_new: float32 [2560, 2, 6400], P('dp', None, 'mp')
- gateup_copy: bfloat16 [2560, 2, 6400], P('dp', None, 'mp')
- gateup_first_new: float32 [2560, 2, 6400], P('dp', None, 'mp')
- gateup_second_new: float32 [2560, 2, 6400], P('dp', None, 'mp')
- gateup_stat_new: float32 [160, 16, 16], P('dp')
- gateup_basis_new: float32 [160, 16, 16], P('dp')
- down_new: float32 [2560, 6400], P('dp', 'mp')
- down_copy: bfloat16 [2560, 6400], P('dp', 'mp')
- down_first_new: float32 [2560, 6400], P('dp', 'mp')
- down_second_new: float32 [2560, 6400], P('dp', 'mp')
- down_stat_new: float32 [160, 16, 16], P('dp')
- down_basis_new: float32 [160, 16, 16], P('dp')
- gains_new: float32 [6144], P('dp')
- gains_first_new: float32 [6144], P('dp')
- gains_second_new: float32 [6144], P('dp')
The draws below stay inside these ranges and needn't reach their ends.
Inputs may be any that keep to these rules, and one draw needn't show every extreme that they name: parents[m, d, 0] is 0 and parents[m, d, b] < b for b >= 1, so every block's path ends at block 0; the last block of every tree has block 6 as its parent. `latent_second`: positive. `latent_stat`: each block is symmetric positive definite. `latent_basis`: each block is orthogonal. `query_second`: positive. `query_stat`: each block is symmetric positive definite. `query_basis`: each block is orthogonal. `keyval_second`: positive. `keyval_stat`: each block is symmetric positive definite. `keyval_basis`: each block is orthogonal. `project_second`: positive. `project_stat`: each block is symmetric positive definite. `project_basis`: each block is orthogonal. `gateup_second`: positive. `gateup_stat`: each block is symmetric positive definite. `gateup_basis`: each block is orthogonal. `down_second`: positive. `down_stat`: each block is symmetric positive definite. `down_basis`: each block is orthogonal. `gains_second`: positive.
All inputs are finite; a program needn't handle non-finite values.
Results may differ from the reference program's by a relative error of at most 0.028.
Values may be sent and summed in bfloat16 or wider, within the bound.
No kernel may reach another device: no remote copies, remote signals or barrier semaphores. Data moves between devices by JAX's collectives and lax.ppermute only.
A program may use at most 512 MiB of HBM per device.

```python
import math
import jax
import jax.numpy as jnp
from jax import lax

WIDTH = 2560
HEADS = 40
QUERY_RANK = 768
LATENT_RANK = 256
NOPE_DIM = 64
ROPE_DIM = 32
VALUE_DIM = 64
FFN_WIDTH = 6400
BLOCK = 128
TREE_BLOCKS = 8
MICRO_BATCHES = 2
ROTATE_ROWS = 16
STEP_COUNT = 10
LATENT_ALL = 1056
SEQUENCE = 1024
TOKENS = 16384
GAIN_COUNT = 6144
N_DP = 8


def grad_scale(factor):
    return factor * math.sqrt(TOKENS)


def first_draw(key, shape, grad_size, tag):
    return 0.05 * grad_size * jax.random.normal(jax.random.fold_in(key, tag), shape, jnp.float32)


def second_draw(key, shape, grad_size, tag):
    spread = jnp.exp(jax.random.uniform(jax.random.fold_in(key, tag), shape, jnp.float32, math.log(0.5), math.log(8.0)))
    return 0.0526 * grad_size * grad_size * spread


def unit_rows(key, blocks):
    magnitude = jax.random.uniform(key, (blocks, ROTATE_ROWS), jnp.float32, 0.5, 1.5)
    signs = jnp.where(jax.random.bernoulli(jax.random.fold_in(key, 1), 0.5, (blocks, ROTATE_ROWS)), 1.0, -1.0)
    vector = magnitude * signs
    return vector * lax.rsqrt(jnp.sum(vector * vector, axis=-1, keepdims=True))


def stat_draw(key, row_count, grad_size, columns, tag):
    own_key = jax.random.fold_in(key, tag)
    blocks = row_count // ROTATE_ROWS
    level = jnp.exp(jax.random.uniform(own_key, (blocks, 1, 1), jnp.float32, 0.0, math.log(4.0)))
    noise = jax.random.uniform(jax.random.fold_in(own_key, 3), (blocks, ROTATE_ROWS, ROTATE_ROWS), jnp.float32, -0.015, 0.015)
    identity = jnp.eye(ROTATE_ROWS, dtype=jnp.float32)
    off_diagonal = (noise + jnp.swapaxes(noise, 1, 2)) * (1.0 - identity)
    first_dir = math.sqrt(2.0) * unit_rows(jax.random.fold_in(own_key, 5), blocks)
    second_dir = math.sqrt(2.0) * unit_rows(jax.random.fold_in(own_key, 6), blocks)
    outer = first_dir[:, :, None] * first_dir[:, None, :] + second_dir[:, :, None] * second_dir[:, None, :]
    return 0.75 * 0.0526 * columns * grad_size * grad_size * level * (identity + off_diagonal + outer)


def basis_draw(key, row_count, tag):
    own_key = jax.random.fold_in(key, tag)
    blocks = row_count // ROTATE_ROWS
    first_unit = unit_rows(jax.random.fold_in(own_key, 11), blocks)
    second_unit = unit_rows(jax.random.fold_in(own_key, 12), blocks)
    identity = jnp.eye(ROTATE_ROWS, dtype=jnp.float32)
    inner = jnp.sum(first_unit * second_unit, axis=-1)[:, None, None]
    return identity - 2.0 * first_unit[:, :, None] * first_unit[:, None, :] - 2.0 * second_unit[:, :, None] * second_unit[:, None, :] + 4.0 * inner * first_unit[:, :, None] * second_unit[:, None, :]


def draw_parents(key, part):
    upper = jnp.maximum(jnp.arange(TREE_BLOCKS), 1)
    drawn = jax.random.randint(key, (MICRO_BATCHES, N_DP, TREE_BLOCKS), 0, upper)
    last_block = jnp.arange(TREE_BLOCKS) == TREE_BLOCKS - 1
    fixed = jnp.where(last_block[None, None, :], TREE_BLOCKS - 2, drawn)
    return fixed.astype(jnp.int32)


def draw_latent_first(key, part):
    return first_draw(key, (WIDTH, LATENT_ALL), grad_scale(4.0), 200)


def draw_latent_second(key, part):
    return second_draw(key, (WIDTH, LATENT_ALL), grad_scale(4.0), 300)


def draw_latent_stat(key, part):
    return stat_draw(key, WIDTH, grad_scale(4.0), LATENT_ALL, 400)


def draw_latent_basis(key, part):
    return basis_draw(key, WIDTH, 100)


def draw_query_first(key, part):
    return first_draw(key, (QUERY_RANK, HEADS * (NOPE_DIM + ROPE_DIM)), grad_scale(0.9), 201)


def draw_query_second(key, part):
    return second_draw(key, (QUERY_RANK, HEADS * (NOPE_DIM + ROPE_DIM)), grad_scale(0.9), 301)


def draw_query_stat(key, part):
    return stat_draw(key, QUERY_RANK, grad_scale(0.9), HEADS * (NOPE_DIM + ROPE_DIM), 401)


def draw_query_basis(key, part):
    return basis_draw(key, QUERY_RANK, 101)


def draw_keyval_first(key, part):
    return first_draw(key, (LATENT_RANK, HEADS * (NOPE_DIM + VALUE_DIM)), grad_scale(1.2), 202)


def draw_keyval_second(key, part):
    return second_draw(key, (LATENT_RANK, HEADS * (NOPE_DIM + VALUE_DIM)), grad_scale(1.2), 302)


def draw_keyval_stat(key, part):
    return stat_draw(key, LATENT_RANK, grad_scale(1.2), HEADS * (NOPE_DIM + VALUE_DIM), 402)


def draw_keyval_basis(key, part):
    return basis_draw(key, LATENT_RANK, 102)


def draw_project_first(key, part):
    return first_draw(key, (WIDTH, HEADS * VALUE_DIM), grad_scale(0.028), 203)


def draw_project_second(key, part):
    return second_draw(key, (WIDTH, HEADS * VALUE_DIM), grad_scale(0.028), 303)


def draw_project_stat(key, part):
    return stat_draw(key, WIDTH, grad_scale(0.028), HEADS * VALUE_DIM, 403)


def draw_project_basis(key, part):
    return basis_draw(key, WIDTH, 103)


def draw_gateup_first(key, part):
    return first_draw(key, (WIDTH, 2, FFN_WIDTH), grad_scale(0.7), 204)


def draw_gateup_second(key, part):
    return second_draw(key, (WIDTH, 2, FFN_WIDTH), grad_scale(0.7), 304)


def draw_gateup_stat(key, part):
    return stat_draw(key, WIDTH, grad_scale(0.7), 2 * FFN_WIDTH, 404)


def draw_gateup_basis(key, part):
    return basis_draw(key, WIDTH, 104)


def draw_down_first(key, part):
    return first_draw(key, (WIDTH, FFN_WIDTH), grad_scale(0.11), 205)


def draw_down_second(key, part):
    return second_draw(key, (WIDTH, FFN_WIDTH), grad_scale(0.11), 305)


def draw_down_stat(key, part):
    return stat_draw(key, WIDTH, grad_scale(0.11), FFN_WIDTH, 405)


def draw_down_basis(key, part):
    return basis_draw(key, WIDTH, 105)


def draw_gains_first(key, part):
    return first_draw(key, (GAIN_COUNT,), grad_scale(3.0), 206)


def draw_gains_second(key, part):
    return second_draw(key, (GAIN_COUNT,), grad_scale(3.0), 306)


def block_scale(key, dims, split, smallest, largest):
    level, own = 1.0, jax.random.fold_in(key, 6)
    for axis_at, parts in split:
        steps = jnp.exp(jax.random.uniform(jax.random.fold_in(own, axis_at), (parts,), jnp.float32, smallest / len(split), largest / len(split)))
        level = level * jnp.repeat(steps, dims[axis_at] // parts).reshape([-1 if axis == axis_at else 1 for axis in range(len(dims))])
    return level


def bell_draw(key, dims, width, reach, pieces=(), kind=jnp.bfloat16):
    values = width * jax.random.normal(key, dims, jnp.float32)
    if pieces:
        values = values * block_scale(key, dims, pieces, -0.22, 0.18)
    return jnp.clip(values, -reach, reach).astype(kind)


def setup_inputs(seed: int = 0) -> dict:
    splits = jax.random.split(jax.random.key(seed), 37)
    return {
        "tokens": bell_draw(splits[0], (MICRO_BATCHES, N_DP * SEQUENCE, WIDTH), 1.0, 6.0, ((1, 32),)),
        "cotangent": bell_draw(splits[1], (MICRO_BATCHES, N_DP * SEQUENCE, WIDTH), 1.0, 6.0, ((1, 32),)),
        "parents": draw_parents(jax.random.fold_in(splits[36], 71), 0),
        "latent_weight": bell_draw(splits[3], (WIDTH, LATENT_ALL), WIDTH ** -0.5, 0.125, ((0, 8), (1, 4)), jnp.float32),
        "latent_first": draw_latent_first(jax.random.fold_in(splits[36], 71), 0),
        "latent_second": draw_latent_second(jax.random.fold_in(splits[36], 71), 0),
        "latent_stat": draw_latent_stat(jax.random.fold_in(splits[36], 71), 0),
        "latent_basis": draw_latent_basis(jax.random.fold_in(splits[36], 71), 0),
        "query_weight": bell_draw(splits[8], (QUERY_RANK, HEADS * (NOPE_DIM + ROPE_DIM)), (QUERY_RANK // 2) ** -0.5, 0.3125, ((0, 8), (1, 4)), jnp.float32),
        "query_first": draw_query_first(jax.random.fold_in(splits[36], 71), 0),
        "query_second": draw_query_second(jax.random.fold_in(splits[36], 71), 0),
        "query_stat": draw_query_stat(jax.random.fold_in(splits[36], 71), 0),
        "query_basis": draw_query_basis(jax.random.fold_in(splits[36], 71), 0),
        "keyval_weight": bell_draw(splits[13], (LATENT_RANK, HEADS * (NOPE_DIM + VALUE_DIM)), LATENT_RANK ** -0.5, 0.375, ((0, 8), (1, 4)), jnp.float32),
        "keyval_first": draw_keyval_first(jax.random.fold_in(splits[36], 71), 0),
        "keyval_second": draw_keyval_second(jax.random.fold_in(splits[36], 71), 0),
        "keyval_stat": draw_keyval_stat(jax.random.fold_in(splits[36], 71), 0),
        "keyval_basis": draw_keyval_basis(jax.random.fold_in(splits[36], 71), 0),
        "project_weight": bell_draw(splits[18], (WIDTH, HEADS * VALUE_DIM), 0.8, 4.0, ((0, 8), (1, 4)), jnp.float32),
        "project_first": draw_project_first(jax.random.fold_in(splits[36], 71), 0),
        "project_second": draw_project_second(jax.random.fold_in(splits[36], 71), 0),
        "project_stat": draw_project_stat(jax.random.fold_in(splits[36], 71), 0),
        "project_basis": draw_project_basis(jax.random.fold_in(splits[36], 71), 0),
        "gateup_weight": bell_draw(splits[23], (WIDTH, 2, FFN_WIDTH), WIDTH ** -0.5, 0.125, ((0, 8), (2, 4)), jnp.float32),
        "gateup_first": draw_gateup_first(jax.random.fold_in(splits[36], 71), 0),
        "gateup_second": draw_gateup_second(jax.random.fold_in(splits[36], 71), 0),
        "gateup_stat": draw_gateup_stat(jax.random.fold_in(splits[36], 71), 0),
        "gateup_basis": draw_gateup_basis(jax.random.fold_in(splits[36], 71), 0),
        "down_weight": bell_draw(splits[28], (WIDTH, FFN_WIDTH), 0.14, 0.8, ((0, 8), (1, 4)), jnp.float32),
        "down_first": draw_down_first(jax.random.fold_in(splits[36], 71), 0),
        "down_second": draw_down_second(jax.random.fold_in(splits[36], 71), 0),
        "down_stat": draw_down_stat(jax.random.fold_in(splits[36], 71), 0),
        "down_basis": draw_down_basis(jax.random.fold_in(splits[36], 71), 0),
        "gains": jnp.clip(1.0 + 0.1 * jax.random.normal(splits[33], (GAIN_COUNT,), jnp.float32), 0.5, 1.5),
        "gains_first": draw_gains_first(jax.random.fold_in(splits[36], 71), 0),
        "gains_second": draw_gains_second(jax.random.fold_in(splits[36], 71), 0),
    }


HIGHEST = lax.Precision.HIGHEST
NORM_EPS = 1e-05
RESIDUAL = 1.4 / math.sqrt(62.0)
ROPE_BASE = 10000.0
BETA_FIRST = 0.95
BETA_SECOND = 0.95
ADAM_EPS = 1e-08
DECAY = 0.01
RATES = (0.08, 0.2, 0.25, 3.2, 0.08, 0.56)
GAIN_RATE = 0.8

@jax.custom_vjp
def low(v):
    return lax.optimization_barrier(v.astype(jnp.bfloat16)).astype(jnp.float32)

@jax.custom_vjp
def low_back(v):
    return v

def low_keep(v):
    return (low(v), None)

def low_pass(kept, grad):
    return (grad,)

def back_keep(v):
    return (v, None)

def back_low(kept, grad):
    return (low(grad),)
low.defvjp(low_keep, low_pass)
low_back.defvjp(back_keep, back_low)

def rms_norm(values, scale_gain):
    return values * lax.rsqrt(lax.optimization_barrier(jnp.mean(values * values, axis=-1, keepdims=True)) + NORM_EPS) * scale_gain

def rotate(values, cosine, sine_part):
    half_dim = values.shape[-1] // 2
    first_half = values[..., :half_dim]
    second_half = values[..., half_dim:]
    return jnp.concatenate([first_half * cosine - second_half * sine_part, second_half * cosine + first_half * sine_part], axis=-1)

def tree_layout(parent):
    block_count = parent.shape[0]
    identity = jnp.eye(block_count, dtype=jnp.float32)
    blocks = jnp.arange(block_count)
    parent_of = ((parent[:, None] == blocks[None, :]) & (blocks[:, None] > 0)).astype(jnp.float32)
    reached = identity
    for unused in range(block_count):
        reached = jnp.minimum(1.0, identity + jnp.dot(parent_of, reached, precision=HIGHEST))
    depths = lax.optimization_barrier(jnp.sum(reached, axis=1)) - 1.0
    length = block_count * BLOCK
    ancestor = jnp.broadcast_to(reached[:, None, :, None], (block_count, BLOCK, block_count, BLOCK)).reshape(length, length) > 0.5
    tokens_at = jnp.arange(length)
    same_block = tokens_at[:, None] // BLOCK == tokens_at[None, :] // BLOCK
    visible = ancestor & (jnp.logical_not(same_block) | (tokens_at[None, :] <= tokens_at[:, None]))
    position = jnp.repeat(depths, BLOCK) * BLOCK + (tokens_at % BLOCK).astype(jnp.float32)
    frequency = ROPE_BASE ** (-(jnp.arange(ROPE_DIM // 2).astype(jnp.float32) * 2.0 / ROPE_DIM))
    angles = position[:, None] * frequency[None, :]
    return (visible, jnp.cos(angles), jnp.sin(angles))

def head_attention(queries, keys_all, values_all, visible):
    scores = low_back(jnp.dot(queries, keys_all.T, precision=HIGHEST) * queries.shape[-1] ** (-0.5))
    scores = jnp.where(visible, scores, -1e+30)
    row_top = lax.optimization_barrier(jnp.max(scores, axis=-1, keepdims=True))
    weights = jnp.exp(scores - row_top)
    probs = weights / lax.optimization_barrier(jnp.sum(weights, axis=-1, keepdims=True))
    return (jnp.dot(low(probs), values_all, precision=HIGHEST), jnp.max(row_top))

def forward(tokens, latent_weight, query_weight, keyval_weight, project_weight, gateup_weight, down_weight, gains, visible, cosine, sine_part):
    length = tokens.shape[0]
    gain_all = low(gains)
    gain_one = gain_all[:WIDTH]
    gain_two = gain_all[WIDTH:2 * WIDTH]
    gain_query = gain_all[2 * WIDTH:2 * WIDTH + QUERY_RANK]
    gain_keyval = gain_all[2 * WIDTH + QUERY_RANK:]
    normed = low(rms_norm(tokens, gain_one))
    latent = low(low_back(jnp.dot(normed, low(latent_weight), precision=HIGHEST)))
    query_latent = low(rms_norm(latent[:, :QUERY_RANK], gain_query))
    keyval_latent = low(rms_norm(latent[:, QUERY_RANK:QUERY_RANK + LATENT_RANK], gain_keyval))
    key_rope = latent[:, QUERY_RANK + LATENT_RANK:]
    query_all = low_back(jnp.dot(query_latent, low(query_weight), precision=HIGHEST)).reshape(length, HEADS, NOPE_DIM + ROPE_DIM)
    keyval = low_back(jnp.dot(keyval_latent, low(keyval_weight), precision=HIGHEST)).reshape(length, HEADS, NOPE_DIM + VALUE_DIM)
    queries = low(jnp.concatenate([query_all[..., :NOPE_DIM], rotate(query_all[..., NOPE_DIM:], cosine[:, None, :], sine_part[:, None, :])], axis=-1))
    shared = rotate(key_rope, cosine, sine_part)
    keys_all = low(jnp.concatenate([keyval[..., :NOPE_DIM], jnp.broadcast_to(shared[:, None, :], (length, HEADS, ROPE_DIM))], axis=-1))
    values_all = low(keyval[..., NOPE_DIM:])

    def one_head(head_items):
        return head_attention(head_items[0], head_items[1], head_items[2], visible)
    heads_out, head_tops = lax.map(jax.checkpoint(one_head), (jnp.transpose(queries, (1, 0, 2)), jnp.transpose(keys_all, (1, 0, 2)), jnp.transpose(values_all, (1, 0, 2))))
    attended = low(low_back(jnp.transpose(heads_out, (1, 0, 2)).reshape(length, HEADS * VALUE_DIM)))
    branch = low_back(jnp.dot(attended, low(project_weight).T, precision=HIGHEST))
    hidden = tokens + RESIDUAL * branch
    normed_two = low(rms_norm(hidden, gain_two))
    gateup = low_back(jnp.einsum('ld,dkf->lkf', normed_two, low(gateup_weight), precision=HIGHEST))
    activated = low(jax.nn.silu(gateup[:, 0]) * gateup[:, 1])
    mixed_out = low_back(jnp.dot(activated, low(down_weight).T, precision=HIGHEST))
    return (hidden + RESIDUAL * mixed_out, head_tops)

def renew(stat_m, basis_m):
    product = jnp.einsum('bij,bjk->bik', stat_m, basis_m, precision=HIGHEST)
    inner = jnp.einsum('bij,bik->bjk', product, product, precision=HIGHEST)
    factor = jnp.linalg.cholesky(inner)
    solved = jax.scipy.linalg.solve_triangular(factor, jnp.swapaxes(product, 1, 2), lower=True)
    return jnp.swapaxes(solved, 1, 2)

def soap_update(weight, grad_w, first_m, second_m, stat_m, basis_m, step_rate):
    blocks = grad_w.reshape(basis_m.shape[0], basis_m.shape[1], -1)
    turned = jnp.einsum('bij,bic->bjc', basis_m, blocks, precision=HIGHEST).reshape(grad_w.shape)
    new_first = BETA_FIRST * first_m + (1.0 - BETA_FIRST) * turned
    new_second = BETA_SECOND * second_m + (1.0 - BETA_SECOND) * turned * turned
    normal_step = new_first / (1.0 - BETA_FIRST ** STEP_COUNT) / (jnp.sqrt(new_second / (1.0 - BETA_SECOND ** STEP_COUNT)) + ADAM_EPS)
    rotated_back = jnp.einsum('bij,bjc->bic', basis_m, normal_step.reshape(blocks.shape), precision=HIGHEST).reshape(grad_w.shape)
    new_weight = weight - step_rate * (rotated_back + DECAY * weight)
    gram_sum = jnp.einsum('bic,bjc->bij', blocks, blocks, precision=HIGHEST)
    new_stat = BETA_SECOND * stat_m + (1.0 - BETA_SECOND) * gram_sum
    return (new_weight, new_first, new_second, new_stat, renew(new_stat, basis_m))

def adam_update(weight, grad_w, first_m, second_m):
    new_first = BETA_FIRST * first_m + (1.0 - BETA_FIRST) * grad_w
    new_second = BETA_SECOND * second_m + (1.0 - BETA_SECOND) * grad_w * grad_w
    normal_step = new_first / (1.0 - BETA_FIRST ** STEP_COUNT) / (jnp.sqrt(new_second / (1.0 - BETA_SECOND ** STEP_COUNT)) + ADAM_EPS)
    return (weight - GAIN_RATE * (normal_step + DECAY * weight), new_first, new_second)

def clip_columns(new_weight, clip_factor, head_width, rope_scaled):
    rows = new_weight.shape[0]
    root_factor = jnp.sqrt(clip_factor)
    tail_factor = clip_factor if rope_scaled else jnp.ones_like(clip_factor)
    column_scale = jnp.concatenate([jnp.broadcast_to(root_factor[:, None], (clip_factor.shape[0], NOPE_DIM)), jnp.broadcast_to(tail_factor[:, None], (clip_factor.shape[0], head_width - NOPE_DIM))], axis=1)
    return (new_weight.reshape(rows, clip_factor.shape[0], head_width) * column_scale[None]).reshape(new_weight.shape)

def reference(tokens, cotangent, parents, latent_weight, latent_first, latent_second, latent_stat, latent_basis, query_weight, query_first, query_second, query_stat, query_basis, keyval_weight, keyval_first, keyval_second, keyval_stat, keyval_basis, project_weight, project_first, project_second, project_stat, project_basis, gateup_weight, gateup_first, gateup_second, gateup_stat, gateup_basis, down_weight, down_first, down_second, down_stat, down_basis, gains, gains_first, gains_second):
    trees = MICRO_BATCHES * N_DP
    matrices = (latent_weight, query_weight, keyval_weight, project_weight, gateup_weight, down_weight)
    states = ((latent_first, latent_second, latent_stat, latent_basis), (query_first, query_second, query_stat, query_basis), (keyval_first, keyval_second, keyval_stat, keyval_basis), (project_first, project_second, project_stat, project_basis), (gateup_first, gateup_second, gateup_stat, gateup_basis), (down_first, down_second, down_stat, down_basis))
    params = matrices + (gains,)
    flat_tokens = tokens.astype(jnp.float32).reshape(trees, SEQUENCE, WIDTH)
    flat_cot = cotangent.astype(jnp.float32).reshape(trees, SEQUENCE, WIDTH)
    flat_parents = parents.reshape(trees, TREE_BLOCKS)

    def tree_step(carry, tree_items):
        running, peak_run = carry
        tree_tokens, tree_cot, tree_parent = tree_items
        visible, cosine, sine_part = tree_layout(tree_parent)

        def apply_layer(layer_in, *weights_in):
            return forward(layer_in, *weights_in, visible, cosine, sine_part)
        result, pullback, head_tops = jax.vjp(apply_layer, tree_tokens, *params, has_aux=True)
        gradients = pullback(tree_cot)
        new_running = tuple((sum_old + grad_in for sum_old, grad_in in zip(running, gradients[1:])))
        return ((new_running, jnp.maximum(peak_run, head_tops)), (result.astype(jnp.bfloat16), gradients[0]))
    zero_sums = tuple((jnp.zeros(weight_in.shape, jnp.float32) for weight_in in params))
    start_peak = jnp.full((HEADS,), -1e+30, jnp.float32)
    (sums_out, peaks), (outputs, input_grads) = lax.scan(tree_step, (zero_sums, start_peak), (flat_tokens, flat_cot, flat_parents))
    threshold = jnp.mean(peaks)
    clip_factor = jnp.minimum(1.0, threshold / jnp.maximum(peaks, 1.0))
    results = [outputs.reshape(MICRO_BATCHES, N_DP * SEQUENCE, WIDTH), input_grads.reshape(MICRO_BATCHES, N_DP * SEQUENCE, WIDTH)]
    for mat_index in range(6):
        first_m, second_m, stat_m, basis_m = states[mat_index]
        new_weight, new_first, new_second, new_stat, new_basis = soap_update(matrices[mat_index], sums_out[mat_index], first_m, second_m, stat_m, basis_m, RATES[mat_index])
        if mat_index == 1:
            new_weight = clip_columns(new_weight, clip_factor, NOPE_DIM + ROPE_DIM, True)
        if mat_index == 2:
            new_weight = clip_columns(new_weight, clip_factor, NOPE_DIM + VALUE_DIM, False)
        results.extend([new_weight, new_weight.astype(jnp.bfloat16), new_first, new_second, new_stat, new_basis])
    gains_new, gains_first_new, gains_second_new = adam_update(gains, sums_out[6], gains_first, gains_second)
    results.extend([gains_new, gains_first_new, gains_second_new])
    return (results[0], results[1], results[2], results[3], results[4], results[5], results[6], results[7], results[8], results[9], results[10], results[11], results[12], results[13], results[14], results[15], results[16], results[17], results[18], results[19], results[20], results[21], results[22], results[23], results[24], results[25], results[26], results[27], results[28], results[29], results[30], results[31], results[32], results[33], results[34], results[35], results[36], results[37], results[38], results[39], results[40])
```

```python
import functools
import math

import jax
import jax.numpy as jnp
from jax import lax
from jax.experimental import pallas as pl
from jax.experimental.pallas import tpu as pltpu
from jax.sharding import PartitionSpec as P

WIDTH = 2560
HEADS = 40
QUERY_RANK = 768
LATENT_RANK = 256
NOPE_DIM = 64
ROPE_DIM = 32
VALUE_DIM = 64
BLOCK = 128
ROTATE_ROWS = 16
STEP_COUNT = 10


HIGHEST = lax.Precision.HIGHEST
NORM_EPS = 1e-05
RESIDUAL = 1.4 / math.sqrt(62.0)
ROPE_BASE = 10000.0
BETA_FIRST = 0.95
BETA_SECOND = 0.95
ADAM_EPS = 1e-08
DECAY = 0.01
RATES = (0.08, 0.2, 0.25, 3.2, 0.08, 0.56)
GAIN_RATE = 0.8


def rms_parts(values, scale_gain):
    inverse = lax.rsqrt(jnp.mean(values * values, axis=-1, keepdims=True) + NORM_EPS)
    return (values * inverse * scale_gain, inverse)


def rms_back(values, inverse, scale_gain, upstream):
    weighted = upstream * scale_gain
    inner = jnp.mean(weighted * values, axis=-1, keepdims=True)
    return inverse * weighted - values * (inverse * inverse * inverse) * inner


def rotate(values, cosine, sine_part):
    half_dim = values.shape[-1] // 2
    first_half = values[..., :half_dim]
    second_half = values[..., half_dim:]
    return jnp.concatenate(
        [
            first_half * cosine - second_half * sine_part,
            second_half * cosine + first_half * sine_part,
        ],
        axis=-1,
    )


def rotate_back(grad_in, cosine, sine_part):
    half_dim = grad_in.shape[-1] // 2
    first_half = grad_in[..., :half_dim]
    second_half = grad_in[..., half_dim:]
    return jnp.concatenate(
        [
            first_half * cosine + second_half * sine_part,
            second_half * cosine - first_half * sine_part,
        ],
        axis=-1,
    )


def tree_layout(parent):
    block_count = parent.shape[0]
    identity = jnp.eye(block_count, dtype=jnp.float32)
    blocks = jnp.arange(block_count)
    parent_of = ((parent[:, None] == blocks[None, :]) & (blocks[:, None] > 0)).astype(jnp.float32)
    reached = identity
    for unused in range(block_count):
        reached = jnp.minimum(1.0, identity + jnp.dot(parent_of, reached, precision=HIGHEST))
    depths = jnp.sum(reached, axis=1) - 1.0
    length = block_count * BLOCK
    ancestor = (
        jnp.broadcast_to(
            reached[:, None, :, None], (block_count, BLOCK, block_count, BLOCK)
        ).reshape(length, length)
        > 0.5
    )
    tokens_at = jnp.arange(length)
    same_block = tokens_at[:, None] // BLOCK == tokens_at[None, :] // BLOCK
    visible = ancestor & (jnp.logical_not(same_block) | (tokens_at[None, :] <= tokens_at[:, None]))
    position = jnp.repeat(depths, BLOCK) * BLOCK + (tokens_at % BLOCK).astype(jnp.float32)
    frequency = ROPE_BASE ** (-(jnp.arange(ROPE_DIM // 2).astype(jnp.float32) * 2.0 / ROPE_DIM))
    angles = position[:, None] * frequency[None, :]
    return (visible, jnp.cos(angles), jnp.sin(angles))


def dot_first(first_arg, second_arg):
    return lax.dot_general(
        first_arg, second_arg, (((0,), (0,)), ((), ())), preferred_element_type=jnp.float32
    )


def dot_last(first_arg, second_arg):
    return lax.dot_general(
        first_arg, second_arg, (((1,), (1,)), ((), ())), preferred_element_type=jnp.float32
    )


def gram_of(grad_w):
    blocks = grad_w.reshape(grad_w.shape[0] // ROTATE_ROWS, ROTATE_ROWS, -1)
    return jnp.einsum("bic,bjc->bij", blocks, blocks, precision=HIGHEST)


def rotated_update(weight, grad_w, first_m, second_m, basis_m, step_rate):
    blocks = grad_w.reshape(basis_m.shape[0], basis_m.shape[1], -1)
    turned = jnp.einsum("bij,bic->bjc", basis_m, blocks, precision=HIGHEST).reshape(grad_w.shape)
    new_first = BETA_FIRST * first_m + (1.0 - BETA_FIRST) * turned
    new_second = BETA_SECOND * second_m + (1.0 - BETA_SECOND) * turned * turned
    normal_step = (
        new_first
        / (1.0 - BETA_FIRST**STEP_COUNT)
        / (jnp.sqrt(new_second / (1.0 - BETA_SECOND**STEP_COUNT)) + ADAM_EPS)
    )
    rotated_back = jnp.einsum(
        "bij,bjc->bic", basis_m, normal_step.reshape(blocks.shape), precision=HIGHEST
    ).reshape(grad_w.shape)
    new_weight = weight - step_rate * (rotated_back + DECAY * weight)
    return (new_weight, new_first, new_second)


def clip_columns(new_weight, clip_factor, head_width, rope_scaled):
    rows = new_weight.shape[0]
    root_factor = jnp.sqrt(clip_factor)
    tail_factor = clip_factor if rope_scaled else jnp.ones_like(clip_factor)
    column_scale = jnp.concatenate(
        [
            jnp.broadcast_to(root_factor[:, None], (clip_factor.shape[0], NOPE_DIM)),
            jnp.broadcast_to(tail_factor[:, None], (clip_factor.shape[0], head_width - NOPE_DIM)),
        ],
        axis=1,
    )
    return (
        new_weight.reshape(rows, clip_factor.shape[0], head_width) * column_scale[None]
    ).reshape(new_weight.shape)


def groups_of(data_count, group_size):
    near = [[start + i for i in range(group_size)] for start in range(0, data_count, group_size)]
    cross = [[i + start for start in range(0, data_count, group_size)] for i in range(group_size)]
    return near, cross


def to_trees(values, group_size, near):
    micro, count, width = values.shape
    parts = values.reshape(micro, group_size, count // group_size, width)
    parts = lax.all_to_all(parts, "dp", 1, 0, axis_index_groups=near)
    parts = parts.reshape(group_size * micro, count // group_size, width)
    return lax.all_to_all(parts, "mp", 0, 0, tiled=True)


def to_owners(values, group_size, near):
    planes, count, width = values.shape
    parts = lax.all_to_all(values, "mp", 0, 0, tiled=True)
    parts = parts.reshape(group_size, planes // group_size, count, width)
    parts = lax.all_to_all(parts, "dp", 0, 1, axis_index_groups=near)
    return parts.reshape(planes // group_size, group_size * count, width)


def spread(values, axis_name, count, groups=None):
    return lax.all_to_all(
        jnp.broadcast_to(values[None], (count,) + values.shape),
        axis_name,
        0,
        0,
        tiled=True,
        axis_index_groups=groups,
    )


def swap_bit(values, bit, data_count):
    return lax.ppermute(values, "dp", [(i, i ^ bit) for i in range(data_count)])


def bits_of(group_size, data_count):
    bits = []
    bit = group_size
    while bit < data_count:
        bits.append(bit)
        bit *= 2
    return bits


def gather_tokens(values, group_size, data_count):
    rows = values.shape[0] // 2
    bits = bits_of(group_size, data_count)
    pieces = {}
    for half in range(2):
        got = {0: values[half * rows : (half + 1) * rows]}
        for bit in bits if half == 0 else bits[::-1]:
            for index in sorted(got):
                got[index ^ bit] = swap_bit(got[index], bit, data_count)
        for index in sorted(got):
            pieces[(index, half)] = got[index]
            for near in range(1, group_size):
                pieces[(index ^ near, half)] = swap_bit(got[index], near, data_count)
    return pieces


def add_low(first_arg, second_arg):
    return (first_arg.astype(jnp.float32) + second_arg.astype(jnp.float32)).astype(jnp.bfloat16)


def scatter_tokens(pieces, group_size, data_count):
    bits = bits_of(group_size, data_count)
    halves = []
    for half in range(2):
        held = {}
        for index in range(0, data_count, group_size):
            total = pieces[(index, half)]
            for near in range(1, group_size):
                total = add_low(total, swap_bit(pieces[(index ^ near, half)], near, data_count))
            held[index] = total
        for bit in bits if half == 0 else bits[::-1]:
            for index in sorted(held):
                if not index & bit:
                    held[index] = add_low(held[index], swap_bit(held[index ^ bit], bit, data_count))
            held = {index: held[index] for index in held if not index & bit}
        halves.append(held[0])
    return jnp.concatenate(halves, axis=0)


def gather_far(block, group_size, data_count, data_index):
    far_count = data_count // group_size
    rows = block.shape[0] // 2
    own = data_index // group_size
    bits = bits_of(group_size, data_count)
    out = jnp.zeros((far_count,) + block.shape, block.dtype)
    for half in range(2):
        got = {0: block[half * rows : (half + 1) * rows]}
        for bit in bits if half == 0 else bits[::-1]:
            for index in sorted(got):
                got[index ^ bit] = swap_bit(got[index], bit, data_count)
        for index in sorted(got):
            out = lax.dynamic_update_slice(
                out, got[index][None], (own ^ (index // group_size), half * rows, 0)
            )
    return out


def gather_rows(block, group_size, data_count, data_index):
    far = gather_far(block, group_size, data_count, data_index)
    own = data_index % group_size
    out = jnp.zeros((far.shape[0], group_size) + block.shape, block.dtype)
    for near in range(group_size):
        part = far if near == 0 else swap_bit(far, near, data_count)
        out = lax.dynamic_update_slice(out, part[:, None], (0, own ^ near, 0, 0))
    return out.reshape((data_count * block.shape[0],) + block.shape[1:])


def after(values, *others):
    return lax.optimization_barrier((values,) + others)[0]


def scatter_rows(grad_w, group_size, data_count, near, cross):
    far_count = data_count // group_size
    rows = grad_w.shape[0] // data_count
    parts = grad_w.astype(jnp.bfloat16).reshape(far_count, group_size, rows, -1)
    parts = lax.all_to_all(parts, "dp", 1, 0, axis_index_groups=near)
    parts = jnp.sum(parts.astype(jnp.float32), axis=0).astype(jnp.bfloat16)
    parts = lax.all_to_all(parts, "dp", 0, 0, tiled=True, axis_index_groups=cross)
    return jnp.sum(parts.astype(jnp.float32), axis=0)


def scatter_columns(grad_w, model_count):
    rows, width = grad_w.shape
    parts = grad_w.astype(jnp.bfloat16).reshape(rows, model_count, width // model_count)
    parts = lax.all_to_all(jnp.swapaxes(parts, 0, 1), "mp", 0, 0, tiled=True)
    return jnp.sum(parts.astype(jnp.float32), axis=0)


def basis_kernel(stat_ref, basis_ref, out_ref):
    size = stat_ref.shape[0]
    columns = jnp.zeros(stat_ref.shape, jnp.float32)
    for j in range(size):
        columns = columns + basis_ref[j][:, None, :] * stat_ref[j][None, :, :]
    for j in range(size):
        column = columns[j]
        norm = jnp.sum(column * column, axis=0, keepdims=True)
        column = column * lax.rsqrt(norm)
        out_ref[j] = column
        shares = jnp.sum(columns * column[None], axis=1, keepdims=True)
        columns = columns - shares * column[None]


def renew_all(stats, bases):
    counts = [stat_m.shape[0] for stat_m in stats]
    total = sum(counts)
    padded = -(-total // 128) * 128
    stat_t = jnp.concatenate([jnp.transpose(s, (2, 1, 0)) for s in stats], axis=2)
    basis_t = jnp.concatenate([jnp.transpose(b, (1, 2, 0)) for b in bases], axis=2)
    pad = ((0, 0), (0, 0), (0, padded - total))
    stat_t = jnp.pad(stat_t, pad, constant_values=1.0)
    basis_t = jnp.pad(basis_t, pad, constant_values=1.0)
    out = pl.pallas_call(
        basis_kernel,
        out_shape=jax.ShapeDtypeStruct((ROTATE_ROWS, ROTATE_ROWS, padded), jnp.float32),
    )(stat_t, basis_t)
    results = []
    start = 0
    for count in counts:
        results.append(jnp.transpose(out[:, :, start : start + count], (2, 1, 0)))
        start += count
    return results


LOG2E = 1.4426950408889634


def exp_rows(query, keys, bias, scale):
    scores = lax.dot_general(
        query, keys, (((1,), (1,)), ((), ())), preferred_element_type=jnp.float32
    )
    scores = scores * (scale * LOG2E) + bias
    top = jnp.max(scores, axis=-1, keepdims=True)
    raised = jnp.exp2(scores - top)
    return raised, top, 1.0 / jnp.sum(raised, axis=-1, keepdims=True)


def attend_kernel(
    scale,
    rows,
    query_latent_ref,
    keyval_latent_ref,
    query_w_ref,
    keyval_w_ref,
    key_ref,
    bias_ref,
    cos_ref,
    left_ref,
    right_ref,
    out_ref,
    query_ref,
    keyval_ref,
    peak_ref,
):
    bf16 = jnp.bfloat16
    length = key_ref.shape[0]
    raw = jnp.dot(query_latent_ref[...], query_w_ref[...], preferred_element_type=jnp.float32)
    both = jnp.dot(keyval_latent_ref[...], keyval_w_ref[...], preferred_element_type=jnp.float32)
    keyval_ref[...] = both.astype(bf16)
    lane = lax.broadcasted_iota(jnp.int32, (1, 128), 1)
    for head in range(2):
        at = slice(head * 128, head * 128 + 128)
        part = raw[:, at]
        query_ref[:, at] = (
            part * cos_ref[...]
            + pltpu.roll(part, 128 - ROPE_DIM // 2, 1) * left_ref[...]
            + pltpu.roll(part, ROPE_DIM // 2, 1) * right_ref[...]
        ).astype(bf16)
    for first in range(0, length, rows):
        last = first + rows
        outs = []
        for head in range(2):
            at = slice(head * 128, head * 128 + 128)
            keyval = keyval_ref[:last, at]
            keys = jnp.where(lane < NOPE_DIM, keyval, key_ref[:last, :])
            raised, top, inverse = exp_rows(
                query_ref[first:last, at], keys, bias_ref[first:last, :last], scale
            )
            outs.append(
                jnp.dot(raised.astype(bf16), keyval, preferred_element_type=jnp.float32) * inverse
            )
            tops = jnp.max(top) * (1.0 / LOG2E)
            spot = slice(head * 8, head * 8 + 8)
            if first == 0:
                peak_ref[0, spot, :] = jnp.full((8, 128), tops, jnp.float32)
            else:
                peak_ref[0, spot, :] = jnp.maximum(peak_ref[0, spot, :], tops)
        out_ref[first:last, :] = jnp.where(
            lane < VALUE_DIM, pltpu.roll(outs[0], VALUE_DIM, 1), outs[1]
        ).astype(bf16)


def attend_back_kernel(
    scale,
    rows,
    query_ref,
    keyval_ref,
    grad_ref,
    key_ref,
    bias_ref,
    cos_ref,
    left_ref,
    right_ref,
    query_out_ref,
    keyval_out_ref,
    shared_out_ref,
    pair_ref,
    total_ref,
):
    bf16 = jnp.bfloat16
    length = key_ref.shape[0]
    lane = lax.broadcasted_iota(jnp.int32, (1, 128), 1)
    low_lanes = lane < NOPE_DIM

    @pl.when(pl.program_id(0) == 0)
    def clear():
        total_ref[...] = jnp.zeros_like(total_ref)

    for head in range(2):
        at = slice(head * 128, head * 128 + 128)
        pair_ref[...] = jnp.zeros_like(pair_ref)
        for first in range(0, length, rows):
            last = first + rows
            keyval = keyval_ref[:last, at]
            keys = jnp.where(low_lanes, keyval, key_ref[:last, :])
            query = query_ref[first:last, at]
            grad = grad_ref[first:last, :].astype(jnp.float32)
            if head == 0:
                grad = pltpu.roll(grad, VALUE_DIM, 1)
            grad = jnp.where(low_lanes, 0.0, grad).astype(bf16)
            raised, _, inverse = exp_rows(query, keys, bias_ref[first:last, :last], scale)
            probs = raised * inverse
            grad_probs = lax.dot_general(
                grad, keyval, (((1,), (1,)), ((), ())), preferred_element_type=jnp.float32
            )
            inner = jnp.sum(probs * grad_probs, axis=-1, keepdims=True)
            grad_scores = (probs * (grad_probs - inner)).astype(bf16)
            part = jnp.dot(grad_scores, keys, preferred_element_type=jnp.float32) * scale
            query_out_ref[first:last, at] = (
                part * cos_ref[first:last, :]
                - pltpu.roll(part, 128 - ROPE_DIM // 2, 1) * left_ref[first:last, :]
                - pltpu.roll(part, ROPE_DIM // 2, 1) * right_ref[first:last, :]
            ).astype(bf16)
            zero = jnp.zeros_like(query)
            left = jnp.concatenate([grad_scores, probs.astype(bf16)], axis=0)
            right = jnp.concatenate(
                [
                    jnp.concatenate(
                        [jnp.where(low_lanes, query, zero), jnp.where(low_lanes, zero, query)],
                        axis=1,
                    ),
                    jnp.concatenate([grad, zero], axis=1),
                ],
                axis=0,
            )
            both = lax.dot_general(
                left, right, (((0,), (0,)), ((), ())), preferred_element_type=jnp.float32
            )
            pair_ref[:last, :] += both[:, :128]
            total_ref[:last, :] += both[:, 128:]
        keyval_out_ref[:, at] = (pair_ref[...] * jnp.where(low_lanes, scale, 1.0)).astype(bf16)

    @pl.when(pl.program_id(0) == pl.num_programs(0) - 1)
    def finish():
        shared_out_ref[...] = total_ref[...] * scale


def resident(shape):
    return pl.BlockSpec(shape, lambda step: (0,) * len(shape))


def attend(query_latent, keyval_latent, query_w, keyval_w, key_lanes, bias, tables, scale, rows):
    length = bias.shape[0]
    steps = query_w.shape[1] // 256
    wide = jax.ShapeDtypeStruct((length, steps * 256), jnp.bfloat16)
    column = lambda width: pl.BlockSpec((length, width), lambda step: (0, step))
    return pl.pallas_call(
        functools.partial(attend_kernel, scale, rows),
        grid=(steps,),
        in_specs=[
            resident(query_latent.shape),
            resident(keyval_latent.shape),
            pl.BlockSpec((query_w.shape[0], 256), lambda step: (0, step)),
            pl.BlockSpec((keyval_w.shape[0], 256), lambda step: (0, step)),
            resident(key_lanes.shape),
            resident(bias.shape),
        ]
        + [resident(table.shape) for table in tables],
        out_specs=[
            column(128),
            column(256),
            column(256),
            pl.BlockSpec((1, 16, 128), lambda step: (step, 0, 0)),
        ],
        out_shape=[
            jax.ShapeDtypeStruct((length, steps * 128), jnp.bfloat16),
            wide,
            wide,
            jax.ShapeDtypeStruct((steps, 16, 128), jnp.float32),
        ],
        compiler_params=pltpu.CompilerParams(vmem_limit_bytes=56 * 1024 * 1024),
    )(query_latent, keyval_latent, query_w, keyval_w, key_lanes, bias, *tables)


def attend_back(queries, keyval, grad, key_lanes, bias, tables, scale, rows):
    length = bias.shape[0]
    steps = queries.shape[1] // 256
    wide = jax.ShapeDtypeStruct(queries.shape, jnp.bfloat16)
    column = lambda width: pl.BlockSpec((length, width), lambda step: (0, step))
    return pl.pallas_call(
        functools.partial(attend_back_kernel, scale, rows),
        grid=(steps,),
        in_specs=[
            column(256),
            column(256),
            column(128),
            resident(key_lanes.shape),
            resident(bias.shape),
        ]
        + [resident(table.shape) for table in tables],
        out_specs=[column(256), column(256), resident((length, 128))],
        out_shape=[wide, wide, jax.ShapeDtypeStruct((length, 128), jnp.float32)],
        scratch_shapes=[
            pltpu.VMEM((length, 128), jnp.float32),
            pltpu.VMEM((length, 128), jnp.float32),
        ],
        compiler_params=pltpu.CompilerParams(vmem_limit_bytes=56 * 1024 * 1024),
    )(queries, keyval, grad, key_lanes, bias, *tables)


def on_device(
    tokens,
    cotangent,
    parents,
    latent_weight,
    latent_first,
    latent_second,
    latent_stat,
    latent_basis,
    query_weight,
    query_first,
    query_second,
    query_stat,
    query_basis,
    keyval_weight,
    keyval_first,
    keyval_second,
    keyval_stat,
    keyval_basis,
    project_weight,
    project_first,
    project_second,
    project_stat,
    project_basis,
    gateup_weight,
    gateup_first,
    gateup_second,
    gateup_stat,
    gateup_basis,
    down_weight,
    down_first,
    down_second,
    down_stat,
    down_basis,
    gains,
    gains_first,
    gains_second,
):
    matrices = (
        latent_weight,
        query_weight,
        keyval_weight,
        project_weight,
        gateup_weight,
        down_weight,
    )
    states = (
        (latent_first, latent_second, latent_stat, latent_basis),
        (query_first, query_second, query_stat, query_basis),
        (keyval_first, keyval_second, keyval_stat, keyval_basis),
        (project_first, project_second, project_stat, project_basis),
        (gateup_first, gateup_second, gateup_stat, gateup_basis),
        (down_first, down_second, down_stat, down_basis),
    )
    bf16 = jnp.bfloat16
    data_count = lax.axis_size("dp")
    model_count = lax.axis_size("mp")
    micro, share, _ = tokens.shape
    group = model_count // micro
    near, cross = groups_of(data_count, group)
    data_index = lax.axis_index("dp")
    model_index = lax.axis_index("mp")
    own_part = data_index % group
    length = share * model_count
    heads = HEADS // group
    scale_attn = float(NOPE_DIM + ROPE_DIM) ** (-0.5)
    rows_attn = min(512, length)
    own_heads = query_weight.shape[1] // (NOPE_DIM + ROPE_DIM)
    latent_all = latent_weight.shape[1] * model_count

    gain_all = spread(gains.astype(bf16), "dp", data_count).reshape(-1).astype(jnp.float32)
    gain_one = gain_all[:WIDTH]
    gain_two = gain_all[WIDTH : 2 * WIDTH]
    gain_query = gain_all[2 * WIDTH : 2 * WIDTH + QUERY_RANK]
    gain_keyval = gain_all[2 * WIDTH + QUERY_RANK :]

    def columns(weight):
        return lax.all_gather(weight.astype(bf16), "mp", axis=1, tiled=True)

    def head_part(weight, width):
        rows = columns(weight)
        parts = rows.reshape(rows.shape[0], group, -1)
        parts = lax.all_to_all(parts, "dp", 1, 0, axis_index_groups=near)
        parts = parts.reshape(group * rows.shape[0], -1)
        full = gather_far(parts, group, data_count, data_index)
        full = full.reshape(data_count * rows.shape[0], heads, width)
        return jnp.pad(full, ((0, 0), (0, 0), (0, 128 - width))).reshape(full.shape[0], -1)

    lat_w = gather_rows(columns(latent_weight), group, data_count, data_index)
    query_w = head_part(query_weight, NOPE_DIM + ROPE_DIM)
    keyval_w = head_part(keyval_weight, NOPE_DIM + VALUE_DIM)
    output_w = gather_rows(columns(project_weight), group, data_count, data_index)

    unit_count = down_weight.shape[1] // data_count
    hidden_units = unit_count * model_count
    padded = -(-hidden_units // 128) * 128
    gate_t = gateup_weight.astype(bf16).reshape(-1, 2, data_count, unit_count)
    gate_t = lax.all_to_all(jnp.transpose(gate_t, (2, 1, 3, 0)), "dp", 0, 0, tiled=True)
    gate_t = jnp.transpose(gate_t, (1, 2, 0, 3)).reshape(2 * unit_count, WIDTH)
    gate_t = lax.all_gather(gate_t, "mp", axis=0)
    gate_t = jnp.transpose(gate_t.reshape(model_count, 2, unit_count, WIDTH), (1, 0, 2, 3))
    gate_t = gate_t.reshape(2, hidden_units, WIDTH)
    gate_t = jnp.pad(gate_t, ((0, 0), (0, padded - hidden_units), (0, 0))).reshape(-1, WIDTH)
    down_t = down_weight.astype(bf16).reshape(-1, data_count, unit_count)
    down_t = lax.all_to_all(jnp.transpose(down_t, (1, 2, 0)), "dp", 0, 0, tiled=True)
    down_t = jnp.transpose(down_t, (1, 0, 2)).reshape(unit_count, WIDTH)
    down_t = lax.all_gather(down_t, "mp", axis=0).reshape(hidden_units, WIDTH)
    down_t = jnp.pad(down_t, ((0, padded - hidden_units), (0, 0)))

    tok = tokens.reshape(micro * share, WIDTH).astype(jnp.float32)
    normed, inverse_one = rms_parts(tok, gain_one)
    normed = normed.astype(bf16)
    latent = jnp.dot(normed, lat_w, preferred_element_type=jnp.float32).astype(bf16)
    latent = latent.astype(jnp.float32)
    query_raw = latent[:, :QUERY_RANK]
    keyval_raw = latent[:, QUERY_RANK : QUERY_RANK + LATENT_RANK]
    key_rope = latent[:, QUERY_RANK + LATENT_RANK :]
    query_normed, inverse_query = rms_parts(query_raw, gain_query)
    keyval_normed, inverse_keyval = rms_parts(keyval_raw, gain_keyval)
    sent = jnp.concatenate([query_normed, keyval_normed, key_rope], axis=1).astype(bf16)

    mid = to_trees(sent.reshape(micro, share, latent_all), group, near)
    tree = spread(mid, "dp", group, near)
    tree = jnp.swapaxes(tree, 0, 1).reshape(length, latent_all)
    tree_parents = spread(parents[:, 0], "dp", group, near).reshape(group * micro, -1)
    visible, cosine, sine_part = tree_layout(
        lax.dynamic_index_in_dim(tree_parents, model_index, 0, keepdims=False)
    )
    query_latent = tree[:, :QUERY_RANK]
    keyval_latent = tree[:, QUERY_RANK : QUERY_RANK + LATENT_RANK]
    shared = rotate(
        tree[:, QUERY_RANK + LATENT_RANK :].astype(jnp.float32), cosine, sine_part
    )
    key_lanes = jnp.pad(shared, ((0, 0), (NOPE_DIM, 128 - NOPE_DIM - ROPE_DIM))).astype(bf16)
    bias = jnp.where(visible, 0.0, -1e30).astype(jnp.float32)
    half_rope = ROPE_DIM // 2
    tail_lanes = 128 - NOPE_DIM - ROPE_DIM
    tables = (
        jnp.concatenate(
            [jnp.ones((length, NOPE_DIM)), cosine, cosine, jnp.zeros((length, tail_lanes))], axis=1
        ).astype(jnp.float32),
        jnp.pad(-sine_part, ((0, 0), (NOPE_DIM, half_rope + tail_lanes))),
        jnp.pad(sine_part, ((0, 0), (NOPE_DIM + half_rope, tail_lanes))),
    )
    attended, queries, keyval, peaks = attend(
        query_latent, keyval_latent, query_w, keyval_w, key_lanes, bias, tables, scale_attn, rows_attn
    )
    peak_own = peaks.reshape(heads, 8, 128)[:, 0, 0]

    def heads_out(values):
        parts = values.reshape(model_count, group, share // group, -1)
        parts = lax.all_to_all(parts, "dp", 1, 2, axis_index_groups=near)
        return to_owners(
            parts.reshape(model_count, share // group, -1), group, near
        ).reshape(micro * share, -1)

    def heads_in(values):
        parts = to_trees(values.reshape(micro, share, -1), group, near)
        parts = parts.reshape(model_count, share // group, group, -1)
        parts = lax.all_to_all(parts, "dp", 2, 1, axis_index_groups=near)
        return parts.reshape(length, -1)

    attended_own = heads_out(attended)
    branch = dot_last(attended_own, output_w)
    hidden = tok + RESIDUAL * branch
    normed_two, inverse_two = rms_parts(hidden, gain_two)
    normed_two = normed_two.astype(bf16)

    far_count = data_count // group
    half_rows = micro * share // 2
    order = [
        [(far * group + place, half) for place in range(group) for half in range(2)]
        for far in range(far_count)
    ]

    def joined(values):
        pieces = gather_tokens(values, group, data_count)
        return [jnp.concatenate([pieces[key] for key in keys], axis=0) for keys in order]

    def parted(blocks):
        pieces = {}
        for keys, block in zip(order, blocks):
            for at, key in enumerate(keys):
                pieces[key] = block[at * half_rows : (at + 1) * half_rows]
        return scatter_tokens(pieces, group, data_count).astype(jnp.float32)

    grad_out = cotangent.reshape(micro * share, WIDTH).astype(jnp.float32)
    mixed_blocks = joined(after((RESIDUAL * grad_out).astype(bf16), tree))
    normed_blocks = joined(normed_two)
    active_blocks = []
    grad_gateup_blocks = []
    for mixed_block, normed_block in zip(mixed_blocks, normed_blocks):
        gateup = dot_last(normed_block, gate_t)
        gate_part = gateup[:, :padded]
        up_part = gateup[:, padded:]
        sigmoid_gate = jax.nn.sigmoid(gate_part)
        silu_gate = gate_part * sigmoid_gate
        active_blocks.append((silu_gate * up_part).astype(bf16))
        grad_act = dot_last(mixed_block, down_t)
        grad_gate = grad_act * up_part * sigmoid_gate * (1.0 + gate_part * (1.0 - sigmoid_gate))
        grad_up = grad_act * silu_gate
        grad_gateup_blocks.append(jnp.concatenate([grad_gate, grad_up], axis=1).astype(bf16))
    grad_normed_blocks = [
        jnp.dot(block, gate_t, preferred_element_type=jnp.float32).astype(bf16)
        for block in grad_gateup_blocks
    ]
    grad_normed_two = parted(grad_normed_blocks)
    activated = jnp.concatenate(active_blocks, axis=0)
    grad_down_t = dot_first(activated, jnp.concatenate(mixed_blocks, axis=0)).astype(bf16)
    grad_gate_t = dot_first(
        jnp.concatenate(grad_gateup_blocks, axis=0), jnp.concatenate(normed_blocks, axis=0)
    ).astype(bf16)
    active_late = [after(block, grad_normed_two) for block in active_blocks]
    mixed_out = parted(
        [
            jnp.dot(block, down_t, preferred_element_type=jnp.float32).astype(bf16)
            for block in active_late
        ]
    )
    layer_out = (hidden + RESIDUAL * mixed_out).astype(bf16)
    grad_down_t = grad_down_t[:hidden_units]

    down_sum = lax.psum_scatter(
        grad_down_t.reshape(model_count, unit_count, WIDTH), "mp", scatter_dimension=0, tiled=True
    )
    down_sum = jnp.transpose(down_sum.reshape(unit_count, data_count, -1), (1, 0, 2))
    down_sum = lax.all_to_all(down_sum, "dp", 0, 0, tiled=True)
    down_sum = jnp.transpose(down_sum, (2, 0, 1)).reshape(down_weight.shape)
    gate_sum = grad_gate_t.reshape(2, padded, WIDTH)[:, :hidden_units]
    gate_sum = jnp.transpose(
        gate_sum.reshape(2, model_count, unit_count, WIDTH), (1, 0, 2, 3)
    ).reshape(model_count, 2 * unit_count, WIDTH)
    gate_sum = lax.psum_scatter(gate_sum, "mp", scatter_dimension=0, tiled=True)
    gate_sum = jnp.transpose(gate_sum.reshape(2 * unit_count, data_count, -1), (1, 0, 2))
    gate_sum = lax.all_to_all(gate_sum, "dp", 0, 0, tiled=True)
    gate_sum = jnp.transpose(
        gate_sum.reshape(data_count, 2, unit_count, -1), (3, 1, 0, 2)
    ).reshape(gateup_weight.shape)

    grad_hidden = grad_out + rms_back(hidden, inverse_two, gain_two, grad_normed_two)
    grad_gain_two = jnp.sum(grad_normed_two * hidden * inverse_two, axis=0)
    grad_branch = (RESIDUAL * grad_hidden).astype(bf16)
    grad_branch = after(grad_branch, grad_gate_t, grad_down_t)
    grad_attended = heads_in(
        jnp.dot(grad_branch, output_w, preferred_element_type=jnp.float32).astype(bf16)
    )
    grad_project = dot_first(grad_branch, attended_own)
    grad_query_all, grad_keyval, grad_shared = attend_back(
        queries, keyval, grad_attended, key_lanes, bias, tables, scale_attn, rows_attn
    )
    grad_shared = rotate_back(
        grad_shared[:, NOPE_DIM : NOPE_DIM + ROPE_DIM], cosine, sine_part
    )
    latent_terms = jnp.concatenate(
        [dot_last(grad_query_all, query_w), dot_last(grad_keyval, keyval_w), grad_shared], axis=1
    ).astype(bf16)
    parts = latent_terms.reshape(model_count, group, share // group, latent_all)
    parts = lax.all_to_all(parts, "dp", 1, 0, axis_index_groups=near)
    parts = jnp.sum(parts.astype(jnp.float32), axis=0).astype(bf16)
    grad_latent_all = (
        to_owners(parts, group, near).reshape(micro * share, latent_all).astype(jnp.float32)
    )
    grad_query_w = dot_first(query_latent, grad_query_all)
    grad_keyval_w = dot_first(keyval_latent, grad_keyval)

    grad_query_up = grad_latent_all[:, :QUERY_RANK]
    grad_keyval_up = grad_latent_all[:, QUERY_RANK : QUERY_RANK + LATENT_RANK]
    grad_latent = jnp.concatenate(
        [
            rms_back(query_raw, inverse_query, gain_query, grad_query_up),
            rms_back(keyval_raw, inverse_keyval, gain_keyval, grad_keyval_up),
            grad_latent_all[:, QUERY_RANK + LATENT_RANK :],
        ],
        axis=1,
    ).astype(bf16)
    grad_gain_query = jnp.sum(grad_query_up * query_raw * inverse_query, axis=0)
    grad_gain_keyval = jnp.sum(grad_keyval_up * keyval_raw * inverse_keyval, axis=0)
    grad_normed = dot_last(grad_latent, lat_w)
    grad_latent_w = dot_first(normed, grad_latent)
    input_grad = grad_hidden + rms_back(tok, inverse_one, gain_one, grad_normed)
    grad_gain_one = jnp.sum(grad_normed * tok * inverse_one, axis=0)
    grad_gains = jnp.concatenate(
        [grad_gain_one, grad_gain_two, grad_gain_query, grad_gain_keyval]
    )

    def head_grads(grad_w):
        rows = grad_w.shape[0] // data_count
        parts = grad_w.astype(bf16).reshape(data_count // group, group * rows, -1)
        parts = lax.all_to_all(parts, "dp", 0, 0, tiled=True, axis_index_groups=cross)
        parts = jnp.sum(parts.astype(jnp.float32), axis=0).astype(bf16)
        parts = lax.all_to_all(
            parts.reshape(group, rows, -1), "dp", 0, 1, axis_index_groups=near
        )
        return scatter_columns(parts.reshape(rows, -1), model_count)

    reduced = [
        scatter_columns(
            scatter_rows(grad_latent_w, group, data_count, near, cross), model_count
        ),
        head_grads(grad_query_w)
        .reshape(query_weight.shape[0], own_heads, 128)[:, :, : NOPE_DIM + ROPE_DIM]
        .reshape(query_weight.shape),
        head_grads(grad_keyval_w),
        scatter_columns(
            scatter_rows(grad_project, group, data_count, near, cross), model_count
        ),
        gate_sum.astype(jnp.float32),
        down_sum.astype(jnp.float32),
    ]
    gain_parts = lax.all_to_all(
        grad_gains.reshape(data_count, -1), "dp", 0, 0, tiled=True
    )
    gain_parts = jnp.sum(gain_parts, axis=0)
    gains_grad = jnp.sum(spread(gain_parts, "mp", model_count), axis=0)

    peak_all = jnp.max(spread(peak_own, "mp", model_count), axis=0)
    peak_all = jnp.max(spread(peak_all, "dp", data_count // group, cross), axis=0)
    all_peaks = spread(peak_all, "dp", group, near).reshape(HEADS)
    threshold = jnp.mean(all_peaks)
    clip_all = jnp.minimum(1.0, threshold / jnp.maximum(all_peaks, 1.0))
    clip_own = lax.dynamic_slice_in_dim(clip_all, model_index * own_heads, own_heads, 0)

    grams = jnp.concatenate([gram_of(grad_w) for grad_w in reduced], axis=0)
    grams = jnp.sum(spread(grams, "mp", model_count), axis=0)
    results = [
        layer_out.reshape(tokens.shape),
        input_grad.reshape(tokens.shape),
    ]
    new_stats = []
    start = 0
    for mat_index in range(6):
        stat_m = states[mat_index][2]
        gram_sum = grams[start : start + stat_m.shape[0]]
        start += stat_m.shape[0]
        new_stats.append(BETA_SECOND * stat_m + (1.0 - BETA_SECOND) * gram_sum)
    new_bases = renew_all(new_stats, [state[3] for state in states])
    for mat_index in range(6):
        first_m, second_m, stat_m, basis_m = states[mat_index]
        new_weight, new_first, new_second = rotated_update(
            matrices[mat_index],
            reduced[mat_index],
            first_m,
            second_m,
            basis_m,
            RATES[mat_index],
        )
        if mat_index == 1:
            new_weight = clip_columns(new_weight, clip_own, NOPE_DIM + ROPE_DIM, True)
        if mat_index == 2:
            new_weight = clip_columns(new_weight, clip_own, NOPE_DIM + VALUE_DIM, False)
        results.extend(
            [
                new_weight,
                new_weight.astype(jnp.bfloat16),
                new_first,
                new_second,
                new_stats[mat_index],
                new_bases[mat_index],
            ]
        )
    gains_first_new = BETA_FIRST * gains_first + (1.0 - BETA_FIRST) * gains_grad
    gains_second_new = BETA_SECOND * gains_second + (1.0 - BETA_SECOND) * gains_grad * gains_grad
    gains_step = (
        gains_first_new
        / (1.0 - BETA_FIRST**STEP_COUNT)
        / (jnp.sqrt(gains_second_new / (1.0 - BETA_SECOND**STEP_COUNT)) + ADAM_EPS)
    )
    results.extend(
        [gains - GAIN_RATE * (gains_step + DECAY * gains), gains_first_new, gains_second_new]
    )
    return tuple(results)


def solution(mesh):
    placed = (
        P(None, ("dp", "mp"), None),
        P(None, ("dp", "mp"), None),
        P(None, "dp", None),
        P("dp", "mp"),
        P("dp", "mp"),
        P("dp", "mp"),
        P("dp", None, None),
        P("dp", None, None),
        P("dp", "mp"),
        P("dp", "mp"),
        P("dp", "mp"),
        P("dp", None, None),
        P("dp", None, None),
        P("dp", "mp"),
        P("dp", "mp"),
        P("dp", "mp"),
        P("dp", None, None),
        P("dp", None, None),
        P("dp", "mp"),
        P("dp", "mp"),
        P("dp", "mp"),
        P("dp", None, None),
        P("dp", None, None),
        P("dp", None, "mp"),
        P("dp", None, "mp"),
        P("dp", None, "mp"),
        P("dp", None, None),
        P("dp", None, None),
        P("dp", "mp"),
        P("dp", "mp"),
        P("dp", "mp"),
        P("dp", None, None),
        P("dp", None, None),
        P("dp"),
        P("dp"),
        P("dp"),
    )
    return jax.shard_map(
        on_device,
        mesh=mesh,
        in_specs=placed,
        out_specs=(
            P(None, ("dp", "mp"), None),
            P(None, ("dp", "mp"), None),
            P("dp", "mp"),
            P("dp", "mp"),
            P("dp", "mp"),
            P("dp", "mp"),
            P("dp", None, None),
            P("dp", None, None),
            P("dp", "mp"),
            P("dp", "mp"),
            P("dp", "mp"),
            P("dp", "mp"),
            P("dp", None, None),
            P("dp", None, None),
            P("dp", "mp"),
            P("dp", "mp"),
            P("dp", "mp"),
            P("dp", "mp"),
            P("dp", None, None),
            P("dp", None, None),
            P("dp", "mp"),
            P("dp", "mp"),
            P("dp", "mp"),
            P("dp", "mp"),
            P("dp", None, None),
            P("dp", None, None),
            P("dp", None, "mp"),
            P("dp", None, "mp"),
            P("dp", None, "mp"),
            P("dp", None, "mp"),
            P("dp", None, None),
            P("dp", None, None),
            P("dp", "mp"),
            P("dp", "mp"),
            P("dp", "mp"),
            P("dp", "mp"),
            P("dp", None, None),
            P("dp", None, None),
            P("dp"),
            P("dp"),
            P("dp"),
        ),
        check_vma=False,
    )
```

```python
import functools
import math

import jax
import jax.numpy as jnp
from jax import lax
from jax.experimental import pallas as pl
from jax.experimental.layout import Layout, with_layout_constraint
from jax.experimental.pallas import tpu as pltpu
from jax.sharding import PartitionSpec as P

WIDTH = 2560
HEADS = 40
QUERY_RANK = 768
LATENT_RANK = 256
NOPE_DIM = 64
ROPE_DIM = 32
VALUE_DIM = 64
BLOCK = 128
ROTATE_ROWS = 16
STEP_COUNT = 10


HIGHEST = lax.Precision.HIGHEST
NORM_EPS = 1e-05
RESIDUAL = 1.4 / math.sqrt(62.0)
ROPE_BASE = 10000.0
BETA_FIRST = 0.95
BETA_SECOND = 0.95
ADAM_EPS = 1e-08
DECAY = 0.01
RATES = (0.08, 0.2, 0.25, 3.2, 0.08, 0.56)
GAIN_RATE = 0.8


def rms_parts(values, scale_gain):
    inverse = lax.rsqrt(jnp.mean(values * values, axis=-1, keepdims=True) + NORM_EPS)
    return (values * inverse * scale_gain, inverse)


def rms_back(values, inverse, scale_gain, upstream):
    weighted = upstream * scale_gain
    inner = jnp.mean(weighted * values, axis=-1, keepdims=True)
    return inverse * weighted - values * (inverse * inverse * inverse) * inner


def rotate(values, cosine, sine_part):
    half_dim = values.shape[-1] // 2
    first_half = values[..., :half_dim]
    second_half = values[..., half_dim:]
    return jnp.concatenate(
        [
            first_half * cosine - second_half * sine_part,
            second_half * cosine + first_half * sine_part,
        ],
        axis=-1,
    )


def rotate_back(grad_in, cosine, sine_part):
    half_dim = grad_in.shape[-1] // 2
    first_half = grad_in[..., :half_dim]
    second_half = grad_in[..., half_dim:]
    return jnp.concatenate(
        [
            first_half * cosine + second_half * sine_part,
            second_half * cosine - first_half * sine_part,
        ],
        axis=-1,
    )


def tree_layout(parent):
    block_count = parent.shape[0]
    identity = jnp.eye(block_count, dtype=jnp.float32)
    blocks = jnp.arange(block_count)
    parent_of = ((parent[:, None] == blocks[None, :]) & (blocks[:, None] > 0)).astype(jnp.float32)
    reached = identity
    for unused in range(block_count):
        reached = jnp.minimum(1.0, identity + jnp.dot(parent_of, reached, precision=HIGHEST))
    depths = jnp.sum(reached, axis=1) - 1.0
    length = block_count * BLOCK
    ancestor = (
        jnp.broadcast_to(
            reached[:, None, :, None], (block_count, BLOCK, block_count, BLOCK)
        ).reshape(length, length)
        > 0.5
    )
    tokens_at = jnp.arange(length)
    same_block = tokens_at[:, None] // BLOCK == tokens_at[None, :] // BLOCK
    visible = ancestor & (jnp.logical_not(same_block) | (tokens_at[None, :] <= tokens_at[:, None]))
    position = jnp.repeat(depths, BLOCK) * BLOCK + (tokens_at % BLOCK).astype(jnp.float32)
    frequency = ROPE_BASE ** (-(jnp.arange(ROPE_DIM // 2).astype(jnp.float32) * 2.0 / ROPE_DIM))
    angles = position[:, None] * frequency[None, :]
    return (visible, jnp.cos(angles), jnp.sin(angles))


def dot_first(first_arg, second_arg):
    return lax.dot_general(
        first_arg, second_arg, (((0,), (0,)), ((), ())), preferred_element_type=jnp.float32
    )


def dot_last(first_arg, second_arg):
    return lax.dot_general(
        first_arg, second_arg, (((1,), (1,)), ((), ())), preferred_element_type=jnp.float32
    )


def gram_of(grad_w):
    blocks = grad_w.reshape(grad_w.shape[0] // ROTATE_ROWS, ROTATE_ROWS, -1)
    return jnp.einsum("bic,bjc->bij", blocks, blocks, precision=HIGHEST)


def rotated_update(weight, grad_w, first_m, second_m, basis_m, step_rate):
    blocks = grad_w.reshape(basis_m.shape[0], basis_m.shape[1], -1)
    turned = jnp.einsum("bij,bic->bjc", basis_m, blocks, precision=HIGHEST).reshape(grad_w.shape)
    new_first = BETA_FIRST * first_m + (1.0 - BETA_FIRST) * turned
    new_second = BETA_SECOND * second_m + (1.0 - BETA_SECOND) * turned * turned
    normal_step = (
        new_first
        / (1.0 - BETA_FIRST**STEP_COUNT)
        / (jnp.sqrt(new_second / (1.0 - BETA_SECOND**STEP_COUNT)) + ADAM_EPS)
    )
    rotated_back = jnp.einsum(
        "bij,bjc->bic", basis_m, normal_step.reshape(blocks.shape), precision=HIGHEST
    ).reshape(grad_w.shape)
    new_weight = weight - step_rate * (rotated_back + DECAY * weight)
    return (new_weight, new_first, new_second)


def clip_columns(new_weight, clip_factor, head_width, rope_scaled):
    rows = new_weight.shape[0]
    root_factor = jnp.sqrt(clip_factor)
    tail_factor = clip_factor if rope_scaled else jnp.ones_like(clip_factor)
    column_scale = jnp.concatenate(
        [
            jnp.broadcast_to(root_factor[:, None], (clip_factor.shape[0], NOPE_DIM)),
            jnp.broadcast_to(tail_factor[:, None], (clip_factor.shape[0], head_width - NOPE_DIM)),
        ],
        axis=1,
    )
    return (
        new_weight.reshape(rows, clip_factor.shape[0], head_width) * column_scale[None]
    ).reshape(new_weight.shape)


def groups_of(data_count, group_size):
    near = [[start + i for i in range(group_size)] for start in range(0, data_count, group_size)]
    cross = [[i + start for start in range(0, data_count, group_size)] for i in range(group_size)]
    return near, cross


def near_parts(values, group_size, near):
    micro, count, width = values.shape
    parts = values.reshape(micro, group_size, count // group_size, width)
    parts = lax.all_to_all(parts, "dp", 1, 0, axis_index_groups=near)
    return parts.reshape(group_size * micro, count // group_size, width)


def to_trees(values, group_size, near):
    return lax.all_to_all(near_parts(values, group_size, near), "mp", 0, 0, tiled=True)


def to_owners(values, group_size, near):
    planes, count, width = values.shape
    parts = values.reshape(group_size, planes // group_size, count, width)
    parts = lax.all_to_all(parts, "dp", 0, 1, axis_index_groups=near)
    return parts.reshape(planes // group_size, group_size * count, width)


def spread(values, axis_name, count, groups=None):
    return lax.all_to_all(
        jnp.broadcast_to(values[None], (count,) + values.shape),
        axis_name,
        0,
        0,
        tiled=True,
        axis_index_groups=groups,
    )


def swap_bit(values, bit, data_count):
    return lax.ppermute(values, "dp", [(i, i ^ bit) for i in range(data_count)])


def bits_of(group_size, data_count):
    bits = []
    bit = group_size
    while bit < data_count:
        bits.append(bit)
        bit *= 2
    return bits


def gather_tokens(values, group_size, data_count):
    rows = values.shape[0] // 2
    bits = bits_of(group_size, data_count)
    pieces = {}
    for half in range(2):
        got = {0: values[half * rows : (half + 1) * rows]}
        for bit in bits if half == 0 else bits[::-1]:
            for index in sorted(got):
                got[index ^ bit] = swap_bit(got[index], bit, data_count)
        for index in sorted(got):
            pieces[(index, half)] = got[index]
            for near in range(1, group_size):
                pieces[(index ^ near, half)] = swap_bit(got[index], near, data_count)
    return pieces


def add_low(first_arg, second_arg):
    return (first_arg.astype(jnp.float32) + second_arg.astype(jnp.float32)).astype(jnp.bfloat16)


def scatter_tokens(pieces, group_size, data_count, near_count):
    bits = bits_of(group_size, data_count)
    halves = []
    for half in range(2):
        held = {}
        for index in range(0, data_count, group_size):
            total = pieces[(index, half)]
            for near in range(1, near_count):
                total = add_low(total, swap_bit(pieces[(index ^ near, half)], near, data_count))
            held[index] = total
        for bit in bits if half == 0 else bits[::-1]:
            for index in sorted(held):
                if not index & bit:
                    held[index] = add_low(held[index], swap_bit(held[index ^ bit], bit, data_count))
            held = {index: held[index] for index in held if not index & bit}
        halves.append(held[0])
    return jnp.concatenate(halves, axis=0)


def spread_planes(values, model_count, model_index):
    out = jnp.zeros((model_count,) + values.shape, values.dtype)
    for shift in range(model_count):
        part = values
        if shift:
            part = lax.ppermute(
                values, "mp", [(i, (i + shift) % model_count) for i in range(model_count)]
            )
        place = (model_index + model_count - shift) % model_count
        out = lax.dynamic_update_slice(out, part[None], (place,) + (0,) * values.ndim)
    return out


def row_major(values):
    return with_layout_constraint(values, Layout(major_to_minor=tuple(range(values.ndim))))


def far_parts(block, group_size, data_count):
    return [block] + [
        swap_bit(block, far, data_count) for far in range(group_size, data_count, group_size)
    ]


def in_order(parts, own):
    out = jnp.zeros((len(parts),) + parts[0].shape, parts[0].dtype)
    for index, part in enumerate(parts):
        out = lax.dynamic_update_slice(out, part[None], (own ^ index,) + (0,) * part.ndim)
    return row_major(out)


def rows_of(parts, group_size, data_count, data_index):
    far = in_order(parts, data_index // group_size)
    own = data_index % group_size
    out = jnp.zeros((len(parts), group_size) + parts[0].shape, far.dtype)
    for near in range(group_size):
        part = far if near == 0 else swap_bit(far, near, data_count)
        out = lax.dynamic_update_slice(out, part[:, None], (0, own ^ near, 0, 0))
    return out.reshape((data_count * parts[0].shape[0],) + parts[0].shape[1:])


def blocks_of(parts, group_size, data_count):
    blocks = []
    for part in parts:
        blocks.append(part)
        for near in range(1, group_size):
            blocks.append(swap_bit(part, near, data_count))
    return jnp.concatenate(blocks, axis=0)


def scatter_blocks(values, group_size, data_count):
    parts = values.reshape(data_count // group_size, group_size, -1, values.shape[-1])
    total = parts[:, 0].astype(jnp.float32)
    for near in range(1, group_size):
        total = total + swap_bit(parts[:, near], near, data_count).astype(jnp.float32)
    total = total.astype(jnp.bfloat16)
    result = total[0].astype(jnp.float32)
    for far in range(1, data_count // group_size):
        result = result + swap_bit(total[far], far * group_size, data_count).astype(jnp.float32)
    return result


def tie(*values):
    return lax.optimization_barrier(values)


def far_sum(parts, group_size, data_count, data_index):
    own = data_index // group_size

    def part_of(far):
        return lax.dynamic_index_in_dim(parts, own ^ far, 0, keepdims=False)

    total = part_of(0).astype(jnp.float32)
    for far in range(1, data_count // group_size):
        total = total + swap_bit(part_of(far), far * group_size, data_count).astype(jnp.float32)
    return total


def near_sum(grad_w, group_size, data_count, data_index):
    own = data_index % group_size
    parts = grad_w.astype(jnp.bfloat16).reshape(
        data_count // group_size, group_size, -1, grad_w.shape[-1]
    )

    def part_of(near):
        return lax.dynamic_index_in_dim(parts, own ^ near, 1, keepdims=False)

    total = part_of(0).astype(jnp.float32)
    for near in range(1, group_size):
        total = total + swap_bit(part_of(near), near, data_count).astype(jnp.float32)
    return total.astype(jnp.bfloat16)


def scatter_columns(grad_w, model_count):
    rows, width = grad_w.shape
    parts = grad_w.astype(jnp.bfloat16).reshape(rows, model_count, width // model_count)
    parts = lax.all_to_all(jnp.swapaxes(parts, 0, 1), "mp", 0, 0, tiled=True)
    return jnp.sum(parts.astype(jnp.float32), axis=0)


def basis_kernel(stat_ref, basis_ref, out_ref):
    size = stat_ref.shape[0]
    columns = jnp.zeros(stat_ref.shape, jnp.float32)
    for j in range(size):
        columns = columns + basis_ref[j][:, None, :] * stat_ref[j][None, :, :]
    for j in range(size):
        column = columns[j]
        norm = jnp.sum(column * column, axis=0, keepdims=True)
        column = column * lax.rsqrt(norm)
        out_ref[j] = column
        shares = jnp.sum(columns * column[None], axis=1, keepdims=True)
        columns = columns - shares * column[None]


def renew_all(stats, bases):
    counts = [stat_m.shape[0] for stat_m in stats]
    total = sum(counts)
    padded = -(-total // 128) * 128
    stat_t = jnp.concatenate([jnp.transpose(s, (2, 1, 0)) for s in stats], axis=2)
    basis_t = jnp.concatenate([jnp.transpose(b, (1, 2, 0)) for b in bases], axis=2)
    pad = ((0, 0), (0, 0), (0, padded - total))
    stat_t = jnp.pad(stat_t, pad, constant_values=1.0)
    basis_t = jnp.pad(basis_t, pad, constant_values=1.0)
    out = pl.pallas_call(
        basis_kernel,
        out_shape=jax.ShapeDtypeStruct((ROTATE_ROWS, ROTATE_ROWS, padded), jnp.float32),
    )(stat_t, basis_t)
    results = []
    start = 0
    for count in counts:
        results.append(jnp.transpose(out[:, :, start : start + count], (2, 1, 0)))
        start += count
    return results


LOG2E = 1.4426950408889634


def exp_rows(query, keys, bias, scale):
    scores = lax.dot_general(
        query, keys, (((1,), (1,)), ((), ())), preferred_element_type=jnp.float32
    )
    scores = scores * (scale * LOG2E) + bias
    top = jnp.max(scores, axis=-1, keepdims=True)
    raised = jnp.exp2(scores - top)
    return raised, top, 1.0 / jnp.sum(raised, axis=-1, keepdims=True)


def attend_kernel(
    scale,
    rows,
    query_latent_ref,
    keyval_latent_ref,
    query_w_ref,
    keyval_w_ref,
    key_ref,
    bias_ref,
    cos_ref,
    left_ref,
    right_ref,
    out_ref,
    query_ref,
    keyval_ref,
    peak_ref,
):
    bf16 = jnp.bfloat16
    length = key_ref.shape[0]
    raw = jnp.dot(query_latent_ref[...], query_w_ref[...], preferred_element_type=jnp.float32)
    both = jnp.dot(keyval_latent_ref[...], keyval_w_ref[...], preferred_element_type=jnp.float32)
    keyval_ref[...] = both.astype(bf16)
    lane = lax.broadcasted_iota(jnp.int32, (1, 128), 1)
    for head in range(2):
        at = slice(head * 128, head * 128 + 128)
        part = raw[:, at]
        query_ref[:, at] = (
            part * cos_ref[...]
            + pltpu.roll(part, 128 - ROPE_DIM // 2, 1) * left_ref[...]
            + pltpu.roll(part, ROPE_DIM // 2, 1) * right_ref[...]
        ).astype(bf16)
    for first in range(0, length, rows):
        last = first + rows
        outs = []
        for head in range(2):
            at = slice(head * 128, head * 128 + 128)
            keyval = keyval_ref[:last, at]
            keys = jnp.where(lane < NOPE_DIM, keyval, key_ref[:last, :])
            raised, top, inverse = exp_rows(
                query_ref[first:last, at], keys, bias_ref[first:last, :last], scale
            )
            outs.append(
                jnp.dot(raised.astype(bf16), keyval, preferred_element_type=jnp.float32) * inverse
            )
            tops = jnp.max(top) * (1.0 / LOG2E)
            spot = slice(head * 8, head * 8 + 8)
            if first == 0:
                peak_ref[0, spot, :] = jnp.full((8, 128), tops, jnp.float32)
            else:
                peak_ref[0, spot, :] = jnp.maximum(peak_ref[0, spot, :], tops)
        out_ref[first:last, :] = jnp.where(
            lane < VALUE_DIM, pltpu.roll(outs[0], VALUE_DIM, 1), outs[1]
        ).astype(bf16)


def attend_back_kernel(
    scale,
    rows,
    query_ref,
    keyval_ref,
    grad_ref,
    key_ref,
    bias_ref,
    cos_ref,
    left_ref,
    right_ref,
    query_out_ref,
    keyval_out_ref,
    shared_out_ref,
    pair_ref,
    total_ref,
):
    bf16 = jnp.bfloat16
    length = key_ref.shape[0]
    lane = lax.broadcasted_iota(jnp.int32, (1, 128), 1)
    low_lanes = lane < NOPE_DIM

    @pl.when(pl.program_id(0) == 0)
    def clear():
        total_ref[...] = jnp.zeros_like(total_ref)

    for head in range(2):
        at = slice(head * 128, head * 128 + 128)
        pair_ref[...] = jnp.zeros_like(pair_ref)
        for first in range(0, length, rows):
            last = first + rows
            keyval = keyval_ref[:last, at]
            keys = jnp.where(low_lanes, keyval, key_ref[:last, :])
            query = query_ref[first:last, at]
            grad = grad_ref[first:last, :].astype(jnp.float32)
            if head == 0:
                grad = pltpu.roll(grad, VALUE_DIM, 1)
            grad = jnp.where(low_lanes, 0.0, grad).astype(bf16)
            raised, _, inverse = exp_rows(query, keys, bias_ref[first:last, :last], scale)
            probs = raised * inverse
            grad_probs = lax.dot_general(
                grad, keyval, (((1,), (1,)), ((), ())), preferred_element_type=jnp.float32
            )
            inner = jnp.sum(probs * grad_probs, axis=-1, keepdims=True)
            grad_scores = (probs * (grad_probs - inner)).astype(bf16)
            part = jnp.dot(grad_scores, keys, preferred_element_type=jnp.float32) * scale
            query_out_ref[first:last, at] = (
                part * cos_ref[first:last, :]
                - pltpu.roll(part, 128 - ROPE_DIM // 2, 1) * left_ref[first:last, :]
                - pltpu.roll(part, ROPE_DIM // 2, 1) * right_ref[first:last, :]
            ).astype(bf16)
            zero = jnp.zeros_like(query)
            left = jnp.concatenate([grad_scores, probs.astype(bf16)], axis=0)
            right = jnp.concatenate(
                [
                    jnp.concatenate(
                        [jnp.where(low_lanes, query, zero), jnp.where(low_lanes, zero, query)],
                        axis=1,
                    ),
                    jnp.concatenate([grad, zero], axis=1),
                ],
                axis=0,
            )
            both = lax.dot_general(
                left, right, (((0,), (0,)), ((), ())), preferred_element_type=jnp.float32
            )
            pair_ref[:last, :] += both[:, :128]
            total_ref[:last, :] += both[:, 128:]
        keyval_out_ref[:, at] = (pair_ref[...] * jnp.where(low_lanes, scale, 1.0)).astype(bf16)

    @pl.when(pl.program_id(0) == pl.num_programs(0) - 1)
    def finish():
        shared_out_ref[...] = total_ref[...] * scale


def attend_cost(length, steps, products):
    return pl.CostEstimate(
        flops=int(products * 2 * steps * 2 * length * length * 256),
        bytes_accessed=steps * length * 256 * 8,
        transcendentals=steps * 2 * length * length,
    )


def resident(shape):
    return pl.BlockSpec(shape, lambda step: (0,) * len(shape))


def attend(query_latent, keyval_latent, query_w, keyval_w, key_lanes, bias, tables, scale, rows):
    length = bias.shape[0]
    steps = query_w.shape[1] // 256
    wide = jax.ShapeDtypeStruct((length, steps * 256), jnp.bfloat16)
    column = lambda width: pl.BlockSpec((length, width), lambda step: (0, step))
    return pl.pallas_call(
        functools.partial(attend_kernel, scale, rows),
        grid=(steps,),
        in_specs=[
            resident(query_latent.shape),
            resident(keyval_latent.shape),
            pl.BlockSpec((query_w.shape[0], 256), lambda step: (0, step)),
            pl.BlockSpec((keyval_w.shape[0], 256), lambda step: (0, step)),
            resident(key_lanes.shape),
            resident(bias.shape),
        ]
        + [resident(table.shape) for table in tables],
        out_specs=[
            column(128),
            column(256),
            column(256),
            pl.BlockSpec((1, 16, 128), lambda step: (step, 0, 0)),
        ],
        out_shape=[
            jax.ShapeDtypeStruct((length, steps * 128), jnp.bfloat16),
            wide,
            wide,
            jax.ShapeDtypeStruct((steps, 16, 128), jnp.float32),
        ],
        compiler_params=pltpu.CompilerParams(vmem_limit_bytes=56 * 1024 * 1024),
        cost_estimate=attend_cost(length, steps, 2.0),
    )(query_latent, keyval_latent, query_w, keyval_w, key_lanes, bias, *tables)


def attend_back(queries, keyval, grad, key_lanes, bias, tables, scale, rows):
    length = bias.shape[0]
    steps = queries.shape[1] // 256
    wide = jax.ShapeDtypeStruct(queries.shape, jnp.bfloat16)
    column = lambda width: pl.BlockSpec((length, width), lambda step: (0, step))
    return pl.pallas_call(
        functools.partial(attend_back_kernel, scale, rows),
        grid=(steps,),
        in_specs=[
            column(256),
            column(256),
            column(128),
            resident(key_lanes.shape),
            resident(bias.shape),
        ]
        + [resident(table.shape) for table in tables],
        out_specs=[column(256), column(256), resident((length, 128))],
        out_shape=[wide, wide, jax.ShapeDtypeStruct((length, 128), jnp.float32)],
        scratch_shapes=[
            pltpu.VMEM((length, 128), jnp.float32),
            pltpu.VMEM((length, 128), jnp.float32),
        ],
        compiler_params=pltpu.CompilerParams(vmem_limit_bytes=56 * 1024 * 1024),
        cost_estimate=attend_cost(length, steps, 4.0),
    )(queries, keyval, grad, key_lanes, bias, *tables)


def on_device(
    tokens,
    cotangent,
    parents,
    latent_weight,
    latent_first,
    latent_second,
    latent_stat,
    latent_basis,
    query_weight,
    query_first,
    query_second,
    query_stat,
    query_basis,
    keyval_weight,
    keyval_first,
    keyval_second,
    keyval_stat,
    keyval_basis,
    project_weight,
    project_first,
    project_second,
    project_stat,
    project_basis,
    gateup_weight,
    gateup_first,
    gateup_second,
    gateup_stat,
    gateup_basis,
    down_weight,
    down_first,
    down_second,
    down_stat,
    down_basis,
    gains,
    gains_first,
    gains_second,
):
    matrices = (
        latent_weight,
        query_weight,
        keyval_weight,
        project_weight,
        gateup_weight,
        down_weight,
    )
    states = (
        (latent_first, latent_second, latent_stat, latent_basis),
        (query_first, query_second, query_stat, query_basis),
        (keyval_first, keyval_second, keyval_stat, keyval_basis),
        (project_first, project_second, project_stat, project_basis),
        (gateup_first, gateup_second, gateup_stat, gateup_basis),
        (down_first, down_second, down_stat, down_basis),
    )
    bf16 = jnp.bfloat16
    data_count = lax.axis_size("dp")
    model_count = lax.axis_size("mp")
    micro, share, _ = tokens.shape
    group = model_count // micro
    near, cross = groups_of(data_count, group)
    data_index = lax.axis_index("dp")
    model_index = lax.axis_index("mp")
    own_part = data_index % group
    length = share * model_count
    heads = HEADS // group
    scale_attn = float(NOPE_DIM + ROPE_DIM) ** (-0.5)
    rows_attn = min(512, length)
    own_heads = query_weight.shape[1] // (NOPE_DIM + ROPE_DIM)
    latent_all = latent_weight.shape[1] * model_count

    def columns(far):
        return jnp.swapaxes(far, 0, 1).reshape(far.shape[1], -1)

    def exchange_units(values):
        return lax.all_to_all(values, "dp", 0, 0, tiled=True)

    query_rows = query_weight.shape[0]
    keyval_rows = keyval_weight.shape[0]
    unit_count = down_weight.shape[1] // data_count
    hidden_units = unit_count * model_count
    padded = -(-hidden_units // 128) * 128
    gain_all = spread(gains.astype(bf16), "dp", data_count)
    output_w = lax.all_gather(project_weight.astype(bf16), "mp", axis=0)
    lat_w = spread_planes(row_major(latent_weight.astype(bf16)), model_count, model_index)
    query_pad = jnp.pad(
        query_weight.astype(bf16).reshape(query_rows, own_heads, NOPE_DIM + ROPE_DIM),
        ((0, 0), (0, 0), (0, 128 - NOPE_DIM - ROPE_DIM)),
    ).reshape(query_rows, own_heads * 128)
    both_w = jnp.concatenate([query_pad, keyval_weight.astype(bf16)], axis=0)
    both_w, lat_w = tie(row_major(both_w), lat_w)
    both_w = spread_planes(both_w, model_count, model_index)
    units = jnp.concatenate(
        [
            jnp.transpose(
                gateup_weight.astype(bf16).reshape(-1, 2, data_count, unit_count), (2, 1, 3, 0)
            ),
            jnp.transpose(
                down_weight.astype(bf16).reshape(-1, 1, data_count, unit_count), (2, 1, 3, 0)
            ),
        ],
        axis=1,
    )
    units, gain_all = tie(units, gain_all)
    units = exchange_units(units)
    lat_w = far_parts(row_major(columns(lat_w)), group, data_count)
    both_w, *lat_w = tie(both_w, *lat_w)
    lat_w = rows_of(lat_w, group, data_count, data_index)
    both_w = columns(both_w).reshape(query_rows + keyval_rows, group, -1)
    both_w = lax.all_to_all(both_w, "dp", 1, 0, axis_index_groups=near)
    both_w = in_order(far_parts(row_major(both_w), group, data_count), data_index // group)
    gain_all = gain_all.reshape(-1).astype(jnp.float32)
    gain_one = gain_all[:WIDTH]
    gain_two = gain_all[WIDTH : 2 * WIDTH]
    gain_query = gain_all[2 * WIDTH : 2 * WIDTH + QUERY_RANK]
    gain_keyval = gain_all[2 * WIDTH + QUERY_RANK :]

    tok = tokens.reshape(micro * share, WIDTH).astype(jnp.float32)
    normed, inverse_one = rms_parts(tok, gain_one)
    normed = normed.astype(bf16)
    latent = jnp.dot(normed, lat_w, preferred_element_type=jnp.float32).astype(bf16)
    latent = latent.astype(jnp.float32)
    query_raw = latent[:, :QUERY_RANK]
    keyval_raw = latent[:, QUERY_RANK : QUERY_RANK + LATENT_RANK]
    key_rope = latent[:, QUERY_RANK + LATENT_RANK :]
    query_normed, inverse_query = rms_parts(query_raw, gain_query)
    keyval_normed, inverse_keyval = rms_parts(keyval_raw, gain_keyval)
    sent = jnp.concatenate([query_normed, keyval_normed, key_rope], axis=1).astype(bf16)

    mid, units = tie(
        near_parts(sent.reshape(micro, share, latent_all), group, near), units
    )
    mid = lax.all_to_all(mid, "mp", 0, 0, tiled=True)
    units = jnp.transpose(units, (1, 2, 0, 3)).reshape(3, unit_count, WIDTH)
    gate_first = lax.all_gather(units[0], "mp", axis=0)
    gate_pad = jnp.zeros((padded - hidden_units, WIDTH), bf16)
    tree = spread(mid, "dp", group, near)
    tree, both_w, output_w = tie(tree, both_w, output_w)
    tree, gate_first = tie(tree, gate_first)
    query_w = both_w[:, :, :query_rows].reshape(data_count * query_rows, -1)
    keyval_w = both_w[:, :, query_rows:].reshape(data_count * keyval_rows, -1)
    gate_halves = [gate_first, lax.all_gather(units[1], "mp", axis=0)]
    output_parts = far_parts(row_major(columns(output_w)), group, data_count)
    tree = jnp.swapaxes(tree, 0, 1).reshape(length, latent_all)
    tree_parents = jnp.zeros((group, micro, parents.shape[2]), parents.dtype)
    own_parents, normed = tie(parents[:, 0], normed)
    for place in range(group):
        part = own_parents if place == 0 else swap_bit(own_parents, place, data_count)
        tree_parents = lax.dynamic_update_slice(
            tree_parents, part[None], (own_part ^ place, 0, 0)
        )
    tree_parents = tree_parents.reshape(group * micro, -1)
    visible, cosine, sine_part = tree_layout(
        lax.dynamic_index_in_dim(tree_parents, model_index, 0, keepdims=False)
    )
    query_latent = tree[:, :QUERY_RANK]
    keyval_latent = tree[:, QUERY_RANK : QUERY_RANK + LATENT_RANK]
    shared = rotate(
        tree[:, QUERY_RANK + LATENT_RANK :].astype(jnp.float32), cosine, sine_part
    )
    key_lanes = jnp.pad(shared, ((0, 0), (NOPE_DIM, 128 - NOPE_DIM - ROPE_DIM))).astype(bf16)
    bias = jnp.where(visible, 0.0, -1e30).astype(jnp.float32)
    half_rope = ROPE_DIM // 2
    tail_lanes = 128 - NOPE_DIM - ROPE_DIM
    tables = (
        jnp.concatenate(
            [jnp.ones((length, NOPE_DIM)), cosine, cosine, jnp.zeros((length, tail_lanes))], axis=1
        ).astype(jnp.float32),
        jnp.pad(-sine_part, ((0, 0), (NOPE_DIM, half_rope + tail_lanes))),
        jnp.pad(sine_part, ((0, 0), (NOPE_DIM + half_rope, tail_lanes))),
    )
    attended, queries, keyval, peaks = attend(
        query_latent, keyval_latent, query_w, keyval_w, key_lanes, bias, tables, scale_attn, rows_attn
    )
    peak_own = peaks.reshape(heads, 8, 128)[:, 0, 0]

    def heads_near(values):
        parts = values.reshape(model_count, group, share // group, -1)
        parts = lax.all_to_all(parts, "dp", 1, 2, axis_index_groups=near)
        return parts.reshape(model_count, share // group, -1)

    def heads_in(values):
        parts = values.reshape(model_count, share // group, group, -1)
        parts = lax.all_to_all(parts, "dp", 2, 1, axis_index_groups=near)
        return parts.reshape(length, -1)

    grad_out = cotangent.reshape(micro * share, WIDTH).astype(jnp.float32)
    mixed_own, attended, *output_parts = tie(
        (RESIDUAL * grad_out).astype(bf16), attended, *output_parts
    )
    output_w = rows_of(output_parts, group, data_count, data_index)
    mixed_parts = [mixed_own] + [
        swap_bit(mixed_own, bit, data_count) for bit in bits_of(group, data_count)
    ]
    attended, gate_halves[1] = tie(attended, gate_halves[1])
    attended = heads_near(attended)
    attended = lax.all_to_all(attended, "mp", 0, 0, tiled=True)
    down_t, attended, *mixed_parts = tie(units[2], attended, *mixed_parts)
    down_t = lax.all_gather(down_t, "mp", axis=0).reshape(hidden_units, WIDTH)
    attended_own = to_owners(attended, group, near).reshape(micro * share, -1)
    branch = dot_last(attended_own, output_w)
    hidden = tok + RESIDUAL * branch
    normed_two, inverse_two = rms_parts(hidden, gain_two)
    normed_two = normed_two.astype(bf16)

    far_count = data_count // group
    half_rows = micro * share // 2
    order = [
        [(far * group + place, half) for place in range(group) for half in range(2)]
        for far in range(far_count)
    ]

    def joined(values):
        pieces = gather_tokens(values, group, data_count)
        return jnp.concatenate([pieces[key] for keys in order for key in keys], axis=0)

    def parted(values):
        pieces = {}
        for at, key in enumerate([key for keys in order for key in keys]):
            pieces[key] = values[at * half_rows : (at + 1) * half_rows]
        return scatter_tokens(pieces, group, data_count, group).astype(jnp.float32)

    down_t = jnp.concatenate([down_t, gate_pad], axis=0)
    normed_full, *mixed_parts = tie(joined(normed_two), *mixed_parts)
    early = [0] + [bit // group for bit in bits_of(group, data_count)]
    mixed_parts = [
        mixed_parts[early.index(far)]
        if far in early
        else swap_bit(mixed_parts[0], far * group, data_count)
        for far in range(far_count)
    ]
    mixed_full = blocks_of(mixed_parts, group, data_count)
    gate_t = jnp.concatenate(
        [
            gate_halves[0].reshape(hidden_units, WIDTH),
            gate_pad,
            gate_halves[1].reshape(hidden_units, WIDTH),
            gate_pad,
        ],
        axis=0,
    )
    gateup = dot_last(normed_full, gate_t)
    gate_part = gateup[:, :padded]
    up_part = gateup[:, padded:]
    grad_act = dot_last(mixed_full, down_t)
    sigmoid_gate = jax.nn.sigmoid(gate_part)
    silu_gate = gate_part * sigmoid_gate
    activated = (silu_gate * up_part).astype(bf16)
    grad_gate = grad_act * up_part * sigmoid_gate * (1.0 + gate_part * (1.0 - sigmoid_gate))
    grad_up = grad_act * silu_gate
    grad_gateup = jnp.concatenate([grad_gate, grad_up], axis=1).astype(bf16)
    grad_normed_two = parted(
        jnp.dot(grad_gateup, gate_t, preferred_element_type=jnp.float32).astype(bf16)
    )
    grad_down_t = dot_first(activated, mixed_full).astype(bf16)
    grad_gate_t = dot_first(grad_gateup, normed_full).astype(bf16)
    grad_down_t = grad_down_t[:hidden_units]

    down_sum = lax.psum_scatter(
        grad_down_t.reshape(model_count, unit_count, WIDTH), "mp", scatter_dimension=0, tiled=True
    )

    grad_hidden = grad_out + rms_back(hidden, inverse_two, gain_two, grad_normed_two)
    grad_gain_two = jnp.sum(grad_normed_two * hidden * inverse_two, axis=0)
    grad_branch, grad_gate_t = tie((RESIDUAL * grad_hidden).astype(bf16), grad_gate_t)
    gate_sum = grad_gate_t.reshape(2, padded, WIDTH)[:, :hidden_units]
    gate_sum = jnp.transpose(
        gate_sum.reshape(2, model_count, unit_count, WIDTH), (1, 0, 2, 3)
    ).reshape(model_count, 2 * unit_count, WIDTH)
    gate_sum = lax.psum_scatter(gate_sum, "mp", scatter_dimension=0, tiled=True)
    grad_attended = jnp.dot(grad_branch, output_w, preferred_element_type=jnp.float32)
    grad_attended = near_parts(
        grad_attended.astype(bf16).reshape(micro, share, -1), group, near
    )
    tail = grad_attended.shape[1] // 2
    early = lax.all_to_all(grad_attended[:, :tail], "mp", 0, 0, tiled=True)
    late, early, activated = tie(grad_attended[:, tail:], early, activated)
    late = lax.all_to_all(late, "mp", 0, 0, tiled=True)
    mixed_out = jnp.dot(activated, down_t, preferred_element_type=jnp.float32).astype(bf16)
    mixed_out = lax.psum_scatter(
        in_order(list(mixed_out.reshape(data_count, -1, WIDTH)), data_index),
        "dp",
        scatter_dimension=0,
        tiled=True,
    ).reshape(hidden.shape)
    project_sum = near_sum(
        dot_first(grad_branch, attended_own), group, data_count, data_index
    )
    grad_attended = heads_in(jnp.concatenate([early, late], axis=1))
    grad_attended, project_sum = tie(grad_attended, project_sum)
    project_sum = far_sum(project_sum, group, data_count, data_index)
    grad_query_all, grad_keyval, grad_shared = attend_back(
        queries, keyval, grad_attended, key_lanes, bias, tables, scale_attn, rows_attn
    )
    grad_shared = rotate_back(
        grad_shared[:, NOPE_DIM : NOPE_DIM + ROPE_DIM], cosine, sine_part
    )
    latent_terms = jnp.concatenate(
        [dot_last(grad_query_all, query_w), dot_last(grad_keyval, keyval_w), grad_shared], axis=1
    ).astype(bf16)
    down_sum = jnp.transpose(down_sum.reshape(unit_count, data_count, -1), (1, 0, 2))
    down_sum = lax.all_to_all(down_sum, "dp", 0, 0, tiled=True)
    gate_sum = jnp.transpose(gate_sum.reshape(2 * unit_count, data_count, -1), (1, 0, 2))
    gate_sum = lax.all_to_all(gate_sum, "dp", 0, 0, tiled=True)
    latent_terms, project_sum, down_sum, gate_sum = tie(
        latent_terms, project_sum, down_sum, gate_sum
    )
    down_sum = jnp.transpose(down_sum, (2, 0, 1)).reshape(down_weight.shape)
    gate_sum = jnp.transpose(
        gate_sum.reshape(data_count, 2, unit_count, -1), (3, 1, 0, 2)
    ).reshape(gateup_weight.shape)

    layer_out = (hidden + RESIDUAL * mixed_out).astype(bf16)
    parts = latent_terms.reshape(model_count, group, share // group, latent_all)
    parts = lax.all_to_all(parts, "dp", 1, 0, axis_index_groups=near)
    parts = jnp.sum(parts.astype(jnp.float32), axis=0).astype(bf16)
    grad_both = jnp.concatenate(
        [
            dot_first(query_latent, grad_query_all)
            .astype(bf16)
            .reshape(data_count // group, group, query_rows, -1),
            dot_first(keyval_latent, grad_keyval)
            .astype(bf16)
            .reshape(data_count // group, group, keyval_rows, -1),
        ],
        axis=2,
    )
    parts, grad_both = tie(lax.all_to_all(parts, "mp", 0, 0, tiled=True), grad_both)
    grad_both = far_sum(
        grad_both.reshape(data_count // group, group * (query_rows + keyval_rows), -1),
        group,
        data_count,
        data_index,
    )
    grad_latent_all = (
        to_owners(parts, group, near).reshape(micro * share, latent_all).astype(jnp.float32)
    )

    grad_query_up = grad_latent_all[:, :QUERY_RANK]
    grad_keyval_up = grad_latent_all[:, QUERY_RANK : QUERY_RANK + LATENT_RANK]
    grad_latent = jnp.concatenate(
        [
            rms_back(query_raw, inverse_query, gain_query, grad_query_up),
            rms_back(keyval_raw, inverse_keyval, gain_keyval, grad_keyval_up),
            grad_latent_all[:, QUERY_RANK + LATENT_RANK :],
        ],
        axis=1,
    ).astype(bf16)
    grad_gain_query = jnp.sum(grad_query_up * query_raw * inverse_query, axis=0)
    grad_gain_keyval = jnp.sum(grad_keyval_up * keyval_raw * inverse_keyval, axis=0)
    grad_normed = dot_last(grad_latent, lat_w)
    latent_sum = near_sum(dot_first(normed, grad_latent), group, data_count, data_index)
    input_grad = grad_hidden + rms_back(tok, inverse_one, gain_one, grad_normed)
    grad_gain_one = jnp.sum(grad_normed * tok * inverse_one, axis=0)
    grad_gains = jnp.concatenate(
        [grad_gain_one, grad_gain_two, grad_gain_query, grad_gain_keyval]
    )

    grad_both = lax.all_to_all(
        grad_both.astype(bf16).reshape(group, query_rows + keyval_rows, -1),
        "dp",
        0,
        1,
        axis_index_groups=near,
    )
    grad_both = scatter_columns(
        grad_both.reshape(query_rows + keyval_rows, -1), model_count
    )
    reduced = [
        scatter_columns(
            far_sum(latent_sum, group, data_count, data_index), model_count
        ),
        grad_both[:query_rows]
        .reshape(query_rows, own_heads, 128)[:, :, : NOPE_DIM + ROPE_DIM]
        .reshape(query_weight.shape),
        grad_both[query_rows:],
        scatter_columns(project_sum, model_count),
        gate_sum.astype(jnp.float32),
        down_sum.astype(jnp.float32),
    ]

    peak_row = lax.dynamic_update_slice(
        jnp.full((HEADS,), -1e30, jnp.float32), peak_own, (own_part * heads,)
    )
    small = jnp.concatenate(
        [
            grad_gains.reshape(data_count, -1),
            jnp.broadcast_to(peak_row[None], (data_count, HEADS)),
        ],
        axis=1,
    )
    small = lax.all_to_all(small, "dp", 0, 0, tiled=True)
    gain_count = gains.shape[0]
    small = jnp.concatenate(
        [jnp.sum(small[:, :gain_count], axis=0), jnp.max(small[:, gain_count:], axis=0)]
    )
    cells = ROTATE_ROWS * ROTATE_ROWS
    small = jnp.pad(small, (0, -(gain_count + HEADS) % cells)).reshape(-1, cells)
    grams = jnp.concatenate([gram_of(grad_w) for grad_w in reduced], axis=0)
    gram_count = grams.shape[0]
    packed = spread(
        jnp.concatenate([grams.reshape(gram_count, cells), small], axis=0), "mp", model_count
    )
    grams = jnp.sum(packed[:, :gram_count], axis=0).reshape(grams.shape)
    small = packed[:, gram_count:].reshape(model_count, -1)
    gains_grad = jnp.sum(small[:, :gain_count], axis=0)
    all_peaks = jnp.max(small[:, gain_count : gain_count + HEADS], axis=0)
    threshold = jnp.mean(all_peaks)
    clip_all = jnp.minimum(1.0, threshold / jnp.maximum(all_peaks, 1.0))
    clip_own = lax.dynamic_slice_in_dim(clip_all, model_index * own_heads, own_heads, 0)

    results = [
        layer_out.reshape(tokens.shape),
        input_grad.reshape(tokens.shape),
    ]
    new_stats = []
    start = 0
    for mat_index in range(6):
        stat_m = states[mat_index][2]
        gram_sum = grams[start : start + stat_m.shape[0]]
        start += stat_m.shape[0]
        new_stats.append(BETA_SECOND * stat_m + (1.0 - BETA_SECOND) * gram_sum)
    new_bases = renew_all(new_stats, [state[3] for state in states])
    for mat_index in range(6):
        first_m, second_m, stat_m, basis_m = states[mat_index]
        new_weight, new_first, new_second = rotated_update(
            matrices[mat_index],
            reduced[mat_index],
            first_m,
            second_m,
            basis_m,
            RATES[mat_index],
        )
        if mat_index == 1:
            new_weight = clip_columns(new_weight, clip_own, NOPE_DIM + ROPE_DIM, True)
        if mat_index == 2:
            new_weight = clip_columns(new_weight, clip_own, NOPE_DIM + VALUE_DIM, False)
        results.extend(
            [
                new_weight,
                new_weight.astype(jnp.bfloat16),
                new_first,
                new_second,
                new_stats[mat_index],
                new_bases[mat_index],
            ]
        )
    gains_first_new = BETA_FIRST * gains_first + (1.0 - BETA_FIRST) * gains_grad
    gains_second_new = BETA_SECOND * gains_second + (1.0 - BETA_SECOND) * gains_grad * gains_grad
    gains_step = (
        gains_first_new
        / (1.0 - BETA_FIRST**STEP_COUNT)
        / (jnp.sqrt(gains_second_new / (1.0 - BETA_SECOND**STEP_COUNT)) + ADAM_EPS)
    )
    results.extend(
        [gains - GAIN_RATE * (gains_step + DECAY * gains), gains_first_new, gains_second_new]
    )
    return tuple(results)


def solution(mesh):
    placed = (
        P(None, ("dp", "mp"), None),
        P(None, ("dp", "mp"), None),
        P(None, "dp", None),
        P("dp", "mp"),
        P("dp", "mp"),
        P("dp", "mp"),
        P("dp", None, None),
        P("dp", None, None),
        P("dp", "mp"),
        P("dp", "mp"),
        P("dp", "mp"),
        P("dp", None, None),
        P("dp", None, None),
        P("dp", "mp"),
        P("dp", "mp"),
        P("dp", "mp"),
        P("dp", None, None),
        P("dp", None, None),
        P("dp", "mp"),
        P("dp", "mp"),
        P("dp", "mp"),
        P("dp", None, None),
        P("dp", None, None),
        P("dp", None, "mp"),
        P("dp", None, "mp"),
        P("dp", None, "mp"),
        P("dp", None, None),
        P("dp", None, None),
        P("dp", "mp"),
        P("dp", "mp"),
        P("dp", "mp"),
        P("dp", None, None),
        P("dp", None, None),
        P("dp"),
        P("dp"),
        P("dp"),
    )
    return jax.shard_map(
        on_device,
        mesh=mesh,
        in_specs=placed,
        out_specs=(
            P(None, ("dp", "mp"), None),
            P(None, ("dp", "mp"), None),
            P("dp", "mp"),
            P("dp", "mp"),
            P("dp", "mp"),
            P("dp", "mp"),
            P("dp", None, None),
            P("dp", None, None),
            P("dp", "mp"),
            P("dp", "mp"),
            P("dp", "mp"),
            P("dp", "mp"),
            P("dp", None, None),
            P("dp", None, None),
            P("dp", "mp"),
            P("dp", "mp"),
            P("dp", "mp"),
            P("dp", "mp"),
            P("dp", None, None),
            P("dp", None, None),
            P("dp", "mp"),
            P("dp", "mp"),
            P("dp", "mp"),
            P("dp", "mp"),
            P("dp", None, None),
            P("dp", None, None),
            P("dp", None, "mp"),
            P("dp", None, "mp"),
            P("dp", None, "mp"),
            P("dp", None, "mp"),
            P("dp", None, None),
            P("dp", None, None),
            P("dp", "mp"),
            P("dp", "mp"),
            P("dp", "mp"),
            P("dp", "mp"),
            P("dp", None, None),
            P("dp", None, None),
            P("dp"),
            P("dp"),
            P("dp"),
        ),
        check_vma=False,
    )
```

```python
import functools
import math

import jax
import jax.numpy as jnp
from jax import lax
from jax.experimental import pallas as pl
from jax.experimental.layout import Layout, with_layout_constraint
from jax.experimental.pallas import tpu as pltpu
from jax.sharding import PartitionSpec as P

WIDTH = 2560
HEADS = 40
QUERY_RANK = 768
LATENT_RANK = 256
NOPE_DIM = 64
ROPE_DIM = 32
VALUE_DIM = 64
BLOCK = 128
ROTATE_ROWS = 16
STEP_COUNT = 10


HIGHEST = lax.Precision.HIGHEST
NORM_EPS = 1e-05
RESIDUAL = 1.4 / math.sqrt(62.0)
ROPE_BASE = 10000.0
BETA_FIRST = 0.95
BETA_SECOND = 0.95
ADAM_EPS = 1e-08
DECAY = 0.01
RATES = (0.08, 0.2, 0.25, 3.2, 0.08, 0.56)
GAIN_RATE = 0.8


def rms_parts(values, scale_gain):
    inverse = lax.rsqrt(jnp.mean(values * values, axis=-1, keepdims=True) + NORM_EPS)
    return (values * inverse * scale_gain, inverse)


def rms_back(values, inverse, scale_gain, upstream):
    weighted = upstream * scale_gain
    inner = jnp.mean(weighted * values, axis=-1, keepdims=True)
    return inverse * weighted - values * (inverse * inverse * inverse) * inner


def rotate(values, cosine, sine_part):
    half_dim = values.shape[-1] // 2
    first_half = values[..., :half_dim]
    second_half = values[..., half_dim:]
    return jnp.concatenate(
        [
            first_half * cosine - second_half * sine_part,
            second_half * cosine + first_half * sine_part,
        ],
        axis=-1,
    )


def rotate_back(grad_in, cosine, sine_part):
    half_dim = grad_in.shape[-1] // 2
    first_half = grad_in[..., :half_dim]
    second_half = grad_in[..., half_dim:]
    return jnp.concatenate(
        [
            first_half * cosine + second_half * sine_part,
            second_half * cosine - first_half * sine_part,
        ],
        axis=-1,
    )


def tree_layout(parent):
    block_count = parent.shape[0]
    identity = jnp.eye(block_count, dtype=jnp.float32)
    blocks = jnp.arange(block_count)
    parent_of = ((parent[:, None] == blocks[None, :]) & (blocks[:, None] > 0)).astype(jnp.float32)
    reached = identity
    for unused in range(block_count):
        reached = jnp.minimum(1.0, identity + jnp.dot(parent_of, reached, precision=HIGHEST))
    depths = jnp.sum(reached, axis=1) - 1.0
    length = block_count * BLOCK
    ancestor = (
        jnp.broadcast_to(
            reached[:, None, :, None], (block_count, BLOCK, block_count, BLOCK)
        ).reshape(length, length)
        > 0.5
    )
    tokens_at = jnp.arange(length)
    same_block = tokens_at[:, None] // BLOCK == tokens_at[None, :] // BLOCK
    visible = ancestor & (jnp.logical_not(same_block) | (tokens_at[None, :] <= tokens_at[:, None]))
    position = jnp.repeat(depths, BLOCK) * BLOCK + (tokens_at % BLOCK).astype(jnp.float32)
    frequency = ROPE_BASE ** (-(jnp.arange(ROPE_DIM // 2).astype(jnp.float32) * 2.0 / ROPE_DIM))
    angles = position[:, None] * frequency[None, :]
    return (visible, jnp.cos(angles), jnp.sin(angles))


def dot_first(first_arg, second_arg):
    return lax.dot_general(
        first_arg, second_arg, (((0,), (0,)), ((), ())), preferred_element_type=jnp.float32
    )


def dot_last(first_arg, second_arg):
    return lax.dot_general(
        first_arg, second_arg, (((1,), (1,)), ((), ())), preferred_element_type=jnp.float32
    )


def gram_of(grad_w):
    blocks = grad_w.reshape(grad_w.shape[0] // ROTATE_ROWS, ROTATE_ROWS, -1)
    return jnp.einsum("bic,bjc->bij", blocks, blocks, precision=HIGHEST)


def rotated_update(weight, grad_w, first_m, second_m, basis_m, step_rate):
    blocks = grad_w.reshape(basis_m.shape[0], basis_m.shape[1], -1)
    turned = jnp.einsum("bij,bic->bjc", basis_m, blocks, precision=HIGHEST).reshape(grad_w.shape)
    new_first = BETA_FIRST * first_m + (1.0 - BETA_FIRST) * turned
    new_second = BETA_SECOND * second_m + (1.0 - BETA_SECOND) * turned * turned
    normal_step = (
        new_first
        / (1.0 - BETA_FIRST**STEP_COUNT)
        / (jnp.sqrt(new_second / (1.0 - BETA_SECOND**STEP_COUNT)) + ADAM_EPS)
    )
    rotated_back = jnp.einsum(
        "bij,bjc->bic", basis_m, normal_step.reshape(blocks.shape), precision=HIGHEST
    ).reshape(grad_w.shape)
    new_weight = weight - step_rate * (rotated_back + DECAY * weight)
    return (new_weight, new_first, new_second)


def clip_columns(new_weight, clip_factor, head_width, rope_scaled):
    rows = new_weight.shape[0]
    root_factor = jnp.sqrt(clip_factor)
    tail_factor = clip_factor if rope_scaled else jnp.ones_like(clip_factor)
    column_scale = jnp.concatenate(
        [
            jnp.broadcast_to(root_factor[:, None], (clip_factor.shape[0], NOPE_DIM)),
            jnp.broadcast_to(tail_factor[:, None], (clip_factor.shape[0], head_width - NOPE_DIM)),
        ],
        axis=1,
    )
    return (
        new_weight.reshape(rows, clip_factor.shape[0], head_width) * column_scale[None]
    ).reshape(new_weight.shape)


def groups_of(data_count, group_size):
    near = [[start + i for i in range(group_size)] for start in range(0, data_count, group_size)]
    cross = [[i + start for start in range(0, data_count, group_size)] for i in range(group_size)]
    return near, cross


def near_parts(values, group_size, near):
    micro, count, width = values.shape
    parts = values.reshape(micro, group_size, count // group_size, width)
    parts = lax.all_to_all(parts, "dp", 1, 0, axis_index_groups=near)
    return parts.reshape(group_size * micro, count // group_size, width)


def to_trees(values, group_size, near):
    return lax.all_to_all(near_parts(values, group_size, near), "mp", 0, 0, tiled=True)


def to_owners(values, group_size, near):
    planes, count, width = values.shape
    parts = values.reshape(group_size, planes // group_size, count, width)
    parts = lax.all_to_all(parts, "dp", 0, 1, axis_index_groups=near)
    return parts.reshape(planes // group_size, group_size * count, width)


def spread(values, axis_name, count, groups=None):
    return lax.all_to_all(
        jnp.broadcast_to(values[None], (count,) + values.shape),
        axis_name,
        0,
        0,
        tiled=True,
        axis_index_groups=groups,
    )


def swap_bit(values, bit, data_count):
    return lax.ppermute(values, "dp", [(i, i ^ bit) for i in range(data_count)])


def bits_of(group_size, data_count):
    bits = []
    bit = group_size
    while bit < data_count:
        bits.append(bit)
        bit *= 2
    return bits


def gather_tokens(values, group_size, data_count):
    rows = values.shape[0] // 2
    bits = bits_of(group_size, data_count)
    pieces = {}
    for half in range(2):
        got = {0: values[half * rows : (half + 1) * rows]}
        for bit in bits if half == 0 else bits[::-1]:
            for index in sorted(got):
                got[index ^ bit] = swap_bit(got[index], bit, data_count)
        for index in sorted(got):
            pieces[(index, half)] = got[index]
            for near in range(1, group_size):
                pieces[(index ^ near, half)] = swap_bit(got[index], near, data_count)
    return pieces


def add_low(first_arg, second_arg):
    return (first_arg.astype(jnp.float32) + second_arg.astype(jnp.float32)).astype(jnp.bfloat16)


def scatter_tokens(pieces, group_size, data_count, near_count, fillers):
    bits = bits_of(group_size, data_count)
    fillers = list(fillers)
    held = [{}, {}]
    far = range(0, data_count, group_size)
    sent = {
        (index, half, near): swap_bit(pieces[(index ^ near, half)], near, data_count)
        for half in range(2)
        for index in far
        for near in range(1, near_count)
    }
    keys = sorted(sent)
    fillers[0], *arrived = tie(fillers[0], *[sent[key] for key in keys])
    sent = dict(zip(keys, arrived))
    for half in range(2):
        for index in far:
            total = pieces[(index, half)]
            for near in range(1, near_count):
                total = add_low(total, sent[(index, half, near)])
            held[half][index] = total
    for step in range(len(bits)):
        sent = {}
        for half in range(2):
            bit = bits[step] if half == 0 else bits[::-1][step]
            for index in held[half]:
                if not index & bit:
                    sent[(index, half)] = swap_bit(held[half][index ^ bit], bit, data_count)
        keys = sorted(sent)
        if step + 1 < len(fillers):
            fillers[step + 1], *arrived = tie(fillers[step + 1], *[sent[key] for key in keys])
            sent = dict(zip(keys, arrived))
        held = [
            {
                index: add_low(held[half][index], sent[(index, half)])
                for index in held[half]
                if (index, half) in sent
            }
            for half in range(2)
        ]
    return jnp.concatenate([held[half][0] for half in range(2)], axis=0), fillers


def spread_planes(values, model_count, model_index):
    out = jnp.zeros((model_count,) + values.shape, values.dtype)
    for shift in range(model_count):
        part = values
        if shift:
            part = lax.ppermute(
                values, "mp", [(i, (i + shift) % model_count) for i in range(model_count)]
            )
        place = (model_index + model_count - shift) % model_count
        out = lax.dynamic_update_slice(out, part[None], (place,) + (0,) * values.ndim)
    return out


def row_major(values):
    return with_layout_constraint(values, Layout(major_to_minor=tuple(range(values.ndim))))


def far_parts(block, group_size, data_count):
    return [block] + [
        swap_bit(block, far, data_count) for far in range(group_size, data_count, group_size)
    ]


def in_order(parts, own):
    out = jnp.zeros((len(parts),) + parts[0].shape, parts[0].dtype)
    for index, part in enumerate(parts):
        out = lax.dynamic_update_slice(out, part[None], (own ^ index,) + (0,) * part.ndim)
    return row_major(out)


def rows_of(parts, group_size, data_count, data_index):
    far = in_order(parts, data_index // group_size)
    own = data_index % group_size
    out = jnp.zeros((len(parts), group_size) + parts[0].shape, far.dtype)
    for near in range(group_size):
        part = far if near == 0 else swap_bit(far, near, data_count)
        out = lax.dynamic_update_slice(out, part[:, None], (0, own ^ near, 0, 0))
    return out.reshape((data_count * parts[0].shape[0],) + parts[0].shape[1:])


def blocks_of(parts, group_size, data_count):
    blocks = []
    for part in parts:
        blocks.append(part)
        for near in range(1, group_size):
            blocks.append(swap_bit(part, near, data_count))
    return jnp.concatenate(blocks, axis=0)


def scatter_blocks(values, group_size, data_count):
    parts = values.reshape(data_count // group_size, group_size, -1, values.shape[-1])
    total = parts[:, 0].astype(jnp.float32)
    for near in range(1, group_size):
        total = total + swap_bit(parts[:, near], near, data_count).astype(jnp.float32)
    total = total.astype(jnp.bfloat16)
    result = total[0].astype(jnp.float32)
    for far in range(1, data_count // group_size):
        result = result + swap_bit(total[far], far * group_size, data_count).astype(jnp.float32)
    return result


def tie(*values):
    return lax.optimization_barrier(values)


def far_sum(parts, group_size, data_count, data_index):
    own = data_index // group_size

    def part_of(far):
        return lax.dynamic_index_in_dim(parts, own ^ far, 0, keepdims=False)

    total = part_of(0).astype(jnp.float32)
    for far in range(1, data_count // group_size):
        total = total + swap_bit(part_of(far), far * group_size, data_count).astype(jnp.float32)
    return total


def near_sum(grad_w, group_size, data_count, data_index):
    own = data_index % group_size
    parts = grad_w.astype(jnp.bfloat16).reshape(
        data_count // group_size, group_size, -1, grad_w.shape[-1]
    )

    def part_of(near):
        return lax.dynamic_index_in_dim(parts, own ^ near, 1, keepdims=False)

    total = part_of(0).astype(jnp.float32)
    for near in range(1, group_size):
        total = total + swap_bit(part_of(near), near, data_count).astype(jnp.float32)
    return total.astype(jnp.bfloat16)


def scatter_columns(grad_w, model_count):
    rows, width = grad_w.shape
    parts = grad_w.astype(jnp.bfloat16).reshape(rows, model_count, width // model_count)
    parts = lax.all_to_all(jnp.swapaxes(parts, 0, 1), "mp", 0, 0, tiled=True)
    return jnp.sum(parts.astype(jnp.float32), axis=0)


def basis_kernel(stat_ref, basis_ref, out_ref):
    size = stat_ref.shape[0]
    columns = jnp.zeros(stat_ref.shape, jnp.float32)
    for j in range(size):
        columns = columns + basis_ref[j][:, None, :] * stat_ref[j][None, :, :]
    for j in range(size):
        column = columns[j]
        norm = jnp.sum(column * column, axis=0, keepdims=True)
        column = column * lax.rsqrt(norm)
        out_ref[j] = column
        shares = jnp.sum(columns * column[None], axis=1, keepdims=True)
        columns = columns - shares * column[None]


def renew_all(stats, bases):
    counts = [stat_m.shape[0] for stat_m in stats]
    total = sum(counts)
    padded = -(-total // 128) * 128
    stat_t = jnp.concatenate([jnp.transpose(s, (2, 1, 0)) for s in stats], axis=2)
    basis_t = jnp.concatenate([jnp.transpose(b, (1, 2, 0)) for b in bases], axis=2)
    pad = ((0, 0), (0, 0), (0, padded - total))
    stat_t = jnp.pad(stat_t, pad, constant_values=1.0)
    basis_t = jnp.pad(basis_t, pad, constant_values=1.0)
    out = pl.pallas_call(
        basis_kernel,
        out_shape=jax.ShapeDtypeStruct((ROTATE_ROWS, ROTATE_ROWS, padded), jnp.float32),
    )(stat_t, basis_t)
    results = []
    start = 0
    for count in counts:
        results.append(jnp.transpose(out[:, :, start : start + count], (2, 1, 0)))
        start += count
    return results


LOG2E = 1.4426950408889634


def exp_rows(query, keys, bias, scale):
    scores = lax.dot_general(
        query, keys, (((1,), (1,)), ((), ())), preferred_element_type=jnp.float32
    )
    scores = scores * (scale * LOG2E) + bias
    top = jnp.max(scores, axis=-1, keepdims=True)
    raised = jnp.exp2(scores - top)
    return raised, top, 1.0 / jnp.sum(raised, axis=-1, keepdims=True)


def attend_kernel(
    scale,
    rows,
    query_latent_ref,
    keyval_latent_ref,
    query_w_ref,
    keyval_w_ref,
    key_ref,
    bias_ref,
    cos_ref,
    left_ref,
    right_ref,
    out_ref,
    query_ref,
    keyval_ref,
    peak_ref,
):
    bf16 = jnp.bfloat16
    length = key_ref.shape[0]
    raw = jnp.dot(query_latent_ref[...], query_w_ref[...], preferred_element_type=jnp.float32)
    both = jnp.dot(keyval_latent_ref[...], keyval_w_ref[...], preferred_element_type=jnp.float32)
    keyval_ref[...] = both.astype(bf16)
    lane = lax.broadcasted_iota(jnp.int32, (1, 128), 1)
    for head in range(2):
        at = slice(head * 128, head * 128 + 128)
        part = raw[:, at]
        query_ref[:, at] = (
            part * cos_ref[...]
            + pltpu.roll(part, 128 - ROPE_DIM // 2, 1) * left_ref[...]
            + pltpu.roll(part, ROPE_DIM // 2, 1) * right_ref[...]
        ).astype(bf16)
    for first in range(0, length, rows):
        last = first + rows
        outs = []
        for head in range(2):
            at = slice(head * 128, head * 128 + 128)
            keyval = keyval_ref[:last, at]
            keys = jnp.where(lane < NOPE_DIM, keyval, key_ref[:last, :])
            raised, top, inverse = exp_rows(
                query_ref[first:last, at], keys, bias_ref[first:last, :last], scale
            )
            outs.append(
                jnp.dot(raised.astype(bf16), keyval, preferred_element_type=jnp.float32) * inverse
            )
            tops = jnp.max(top) * (1.0 / LOG2E)
            spot = slice(head * 8, head * 8 + 8)
            if first == 0:
                peak_ref[0, spot, :] = jnp.full((8, 128), tops, jnp.float32)
            else:
                peak_ref[0, spot, :] = jnp.maximum(peak_ref[0, spot, :], tops)
        out_ref[first:last, :] = jnp.where(
            lane < VALUE_DIM, pltpu.roll(outs[0], VALUE_DIM, 1), outs[1]
        ).astype(bf16)


def attend_back_kernel(
    scale,
    rows,
    query_ref,
    keyval_ref,
    grad_ref,
    key_ref,
    bias_ref,
    cos_ref,
    left_ref,
    right_ref,
    query_out_ref,
    keyval_out_ref,
    shared_out_ref,
    pair_ref,
    total_ref,
):
    bf16 = jnp.bfloat16
    length = key_ref.shape[0]
    lane = lax.broadcasted_iota(jnp.int32, (1, 128), 1)
    low_lanes = lane < NOPE_DIM

    @pl.when(pl.program_id(0) == 0)
    def clear():
        total_ref[...] = jnp.zeros_like(total_ref)

    for head in range(2):
        at = slice(head * 128, head * 128 + 128)
        pair_ref[...] = jnp.zeros_like(pair_ref)
        for first in range(0, length, rows):
            last = first + rows
            keyval = keyval_ref[:last, at]
            keys = jnp.where(low_lanes, keyval, key_ref[:last, :])
            query = query_ref[first:last, at]
            grad = grad_ref[first:last, :].astype(jnp.float32)
            if head == 0:
                grad = pltpu.roll(grad, VALUE_DIM, 1)
            grad = jnp.where(low_lanes, 0.0, grad).astype(bf16)
            raised, _, inverse = exp_rows(query, keys, bias_ref[first:last, :last], scale)
            probs = raised * inverse
            grad_probs = lax.dot_general(
                grad, keyval, (((1,), (1,)), ((), ())), preferred_element_type=jnp.float32
            )
            inner = jnp.sum(probs * grad_probs, axis=-1, keepdims=True)
            grad_scores = (probs * (grad_probs - inner)).astype(bf16)
            part = jnp.dot(grad_scores, keys, preferred_element_type=jnp.float32) * scale
            query_out_ref[first:last, at] = (
                part * cos_ref[first:last, :]
                - pltpu.roll(part, 128 - ROPE_DIM // 2, 1) * left_ref[first:last, :]
                - pltpu.roll(part, ROPE_DIM // 2, 1) * right_ref[first:last, :]
            ).astype(bf16)
            zero = jnp.zeros_like(query)
            left = jnp.concatenate([grad_scores, probs.astype(bf16)], axis=0)
            right = jnp.concatenate(
                [
                    jnp.concatenate(
                        [jnp.where(low_lanes, query, zero), jnp.where(low_lanes, zero, query)],
                        axis=1,
                    ),
                    jnp.concatenate([grad, zero], axis=1),
                ],
                axis=0,
            )
            both = lax.dot_general(
                left, right, (((0,), (0,)), ((), ())), preferred_element_type=jnp.float32
            )
            pair_ref[:last, :] += both[:, :128]
            total_ref[:last, :] += both[:, 128:]
        keyval_out_ref[:, at] = (pair_ref[...] * jnp.where(low_lanes, scale, 1.0)).astype(bf16)

    @pl.when(pl.program_id(0) == pl.num_programs(0) - 1)
    def finish():
        shared_out_ref[...] = total_ref[...] * scale


def attend_cost(length, steps, products):
    return pl.CostEstimate(
        flops=int(products * 2 * steps * 2 * length * length * 256),
        bytes_accessed=steps * length * 256 * 8,
        transcendentals=steps * 2 * length * length,
    )


def resident(shape):
    return pl.BlockSpec(shape, lambda step: (0,) * len(shape))


def attend(query_latent, keyval_latent, query_w, keyval_w, key_lanes, bias, tables, scale, rows):
    length = bias.shape[0]
    steps = query_w.shape[1] // 256
    wide = jax.ShapeDtypeStruct((length, steps * 256), jnp.bfloat16)
    column = lambda width: pl.BlockSpec((length, width), lambda step: (0, step))
    return pl.pallas_call(
        functools.partial(attend_kernel, scale, rows),
        grid=(steps,),
        in_specs=[
            resident(query_latent.shape),
            resident(keyval_latent.shape),
            pl.BlockSpec((query_w.shape[0], 256), lambda step: (0, step)),
            pl.BlockSpec((keyval_w.shape[0], 256), lambda step: (0, step)),
            resident(key_lanes.shape),
            resident(bias.shape),
        ]
        + [resident(table.shape) for table in tables],
        out_specs=[
            column(128),
            column(256),
            column(256),
            pl.BlockSpec((1, 16, 128), lambda step: (step, 0, 0)),
        ],
        out_shape=[
            jax.ShapeDtypeStruct((length, steps * 128), jnp.bfloat16),
            wide,
            wide,
            jax.ShapeDtypeStruct((steps, 16, 128), jnp.float32),
        ],
        compiler_params=pltpu.CompilerParams(vmem_limit_bytes=56 * 1024 * 1024),
        cost_estimate=attend_cost(length, steps, 2.0),
    )(query_latent, keyval_latent, query_w, keyval_w, key_lanes, bias, *tables)


def attend_back(queries, keyval, grad, key_lanes, bias, tables, scale, rows):
    length = bias.shape[0]
    steps = queries.shape[1] // 256
    wide = jax.ShapeDtypeStruct(queries.shape, jnp.bfloat16)
    column = lambda width: pl.BlockSpec((length, width), lambda step: (0, step))
    return pl.pallas_call(
        functools.partial(attend_back_kernel, scale, rows),
        grid=(steps,),
        in_specs=[
            column(256),
            column(256),
            column(128),
            resident(key_lanes.shape),
            resident(bias.shape),
        ]
        + [resident(table.shape) for table in tables],
        out_specs=[column(256), column(256), resident((length, 128))],
        out_shape=[wide, wide, jax.ShapeDtypeStruct((length, 128), jnp.float32)],
        scratch_shapes=[
            pltpu.VMEM((length, 128), jnp.float32),
            pltpu.VMEM((length, 128), jnp.float32),
        ],
        compiler_params=pltpu.CompilerParams(vmem_limit_bytes=56 * 1024 * 1024),
        cost_estimate=attend_cost(length, steps, 4.0),
    )(queries, keyval, grad, key_lanes, bias, *tables)


def on_device(
    tokens,
    cotangent,
    parents,
    latent_weight,
    latent_first,
    latent_second,
    latent_stat,
    latent_basis,
    query_weight,
    query_first,
    query_second,
    query_stat,
    query_basis,
    keyval_weight,
    keyval_first,
    keyval_second,
    keyval_stat,
    keyval_basis,
    project_weight,
    project_first,
    project_second,
    project_stat,
    project_basis,
    gateup_weight,
    gateup_first,
    gateup_second,
    gateup_stat,
    gateup_basis,
    down_weight,
    down_first,
    down_second,
    down_stat,
    down_basis,
    gains,
    gains_first,
    gains_second,
):
    matrices = (
        latent_weight,
        query_weight,
        keyval_weight,
        project_weight,
        gateup_weight,
        down_weight,
    )
    states = (
        (latent_first, latent_second, latent_stat, latent_basis),
        (query_first, query_second, query_stat, query_basis),
        (keyval_first, keyval_second, keyval_stat, keyval_basis),
        (project_first, project_second, project_stat, project_basis),
        (gateup_first, gateup_second, gateup_stat, gateup_basis),
        (down_first, down_second, down_stat, down_basis),
    )
    bf16 = jnp.bfloat16
    data_count = lax.axis_size("dp")
    model_count = lax.axis_size("mp")
    micro, share, _ = tokens.shape
    group = model_count // micro
    near, cross = groups_of(data_count, group)
    data_index = lax.axis_index("dp")
    model_index = lax.axis_index("mp")
    own_part = data_index % group
    length = share * model_count
    heads = HEADS // group
    scale_attn = float(NOPE_DIM + ROPE_DIM) ** (-0.5)
    rows_attn = min(512, length)
    own_heads = query_weight.shape[1] // (NOPE_DIM + ROPE_DIM)
    latent_all = latent_weight.shape[1] * model_count

    def columns(far):
        return jnp.swapaxes(far, 0, 1).reshape(far.shape[1], -1)

    def exchange_units(values):
        return lax.all_to_all(values, "dp", 0, 0, tiled=True)

    query_rows = query_weight.shape[0]
    keyval_rows = keyval_weight.shape[0]
    unit_count = down_weight.shape[1] // data_count
    hidden_units = unit_count * model_count
    padded = -(-hidden_units // 128) * 128
    gain_all = spread(gains.astype(bf16), "dp", data_count)
    output_w = lax.all_gather(project_weight.astype(bf16), "mp", axis=0)
    lat_w = spread_planes(row_major(latent_weight.astype(bf16)), model_count, model_index)
    query_pad = jnp.pad(
        query_weight.astype(bf16).reshape(query_rows, own_heads, NOPE_DIM + ROPE_DIM),
        ((0, 0), (0, 0), (0, 128 - NOPE_DIM - ROPE_DIM)),
    ).reshape(query_rows, own_heads * 128)
    both_w = jnp.concatenate([query_pad, keyval_weight.astype(bf16)], axis=0)
    both_w, lat_w = tie(row_major(both_w), lat_w)
    both_w = spread_planes(both_w, model_count, model_index)
    units = jnp.concatenate(
        [
            jnp.transpose(
                gateup_weight.astype(bf16).reshape(-1, 2, data_count, unit_count), (2, 1, 3, 0)
            ),
            jnp.transpose(
                down_weight.astype(bf16).reshape(-1, 1, data_count, unit_count), (2, 1, 3, 0)
            ),
        ],
        axis=1,
    )
    units = exchange_units(units)
    lat_w = far_parts(row_major(columns(lat_w)), group, data_count)
    both_w, *lat_w = tie(columns(both_w), *lat_w)
    both_w = both_w.reshape(query_rows + keyval_rows, group, -1)
    both_w = lax.all_to_all(both_w, "dp", 1, 0, axis_index_groups=near)
    both_w, units = tie(row_major(both_w), units)
    both_parts = far_parts(both_w, group, data_count)
    lat_w = rows_of(lat_w, group, data_count, data_index)
    gain_all = gain_all.reshape(-1).astype(jnp.float32)
    gain_one = gain_all[:WIDTH]
    gain_two = gain_all[WIDTH : 2 * WIDTH]
    gain_query = gain_all[2 * WIDTH : 2 * WIDTH + QUERY_RANK]
    gain_keyval = gain_all[2 * WIDTH + QUERY_RANK :]

    tok = tokens.reshape(micro * share, WIDTH).astype(jnp.float32)
    normed, inverse_one = rms_parts(tok, gain_one)
    normed = normed.astype(bf16)
    latent = jnp.dot(normed, lat_w, preferred_element_type=jnp.float32).astype(bf16)
    latent = latent.astype(jnp.float32)
    query_raw = latent[:, :QUERY_RANK]
    keyval_raw = latent[:, QUERY_RANK : QUERY_RANK + LATENT_RANK]
    key_rope = latent[:, QUERY_RANK + LATENT_RANK :]
    query_normed, inverse_query = rms_parts(query_raw, gain_query)
    keyval_normed, inverse_keyval = rms_parts(keyval_raw, gain_keyval)
    sent = jnp.concatenate([query_normed, keyval_normed, key_rope], axis=1).astype(bf16)

    mid = near_parts(sent.reshape(micro, share, latent_all), group, near)
    mid = lax.all_to_all(mid, "mp", 0, 0, tiled=True)
    mid, *both_parts = tie(mid, *both_parts)
    both_w = in_order(both_parts, data_index // group)
    units = jnp.transpose(units, (1, 2, 0, 3)).reshape(3, unit_count, WIDTH)
    gate_first = lax.all_gather(units[0], "mp", axis=0)
    gate_pad = jnp.zeros((padded - hidden_units, WIDTH), bf16)
    tree = spread(mid, "dp", group, near)
    tree, both_w, output_w = tie(tree, both_w, output_w)
    tree, gate_first = tie(tree, gate_first)
    query_w = both_w[:, :, :query_rows].reshape(data_count * query_rows, -1)
    keyval_w = both_w[:, :, query_rows:].reshape(data_count * keyval_rows, -1)
    gate_halves = [gate_first, lax.all_gather(units[1], "mp", axis=0)]
    output_parts = far_parts(row_major(columns(output_w)), group, data_count)
    tree = jnp.swapaxes(tree, 0, 1).reshape(length, latent_all)
    tree_parents = jnp.zeros((group, micro, parents.shape[2]), parents.dtype)
    own_parents, normed = tie(parents[:, 0], normed)
    for place in range(group):
        part = own_parents if place == 0 else swap_bit(own_parents, place, data_count)
        tree_parents = lax.dynamic_update_slice(
            tree_parents, part[None], (own_part ^ place, 0, 0)
        )
    tree_parents = tree_parents.reshape(group * micro, -1)
    visible, cosine, sine_part = tree_layout(
        lax.dynamic_index_in_dim(tree_parents, model_index, 0, keepdims=False)
    )
    query_latent = tree[:, :QUERY_RANK]
    keyval_latent = tree[:, QUERY_RANK : QUERY_RANK + LATENT_RANK]
    shared = rotate(
        tree[:, QUERY_RANK + LATENT_RANK :].astype(jnp.float32), cosine, sine_part
    )
    key_lanes = jnp.pad(shared, ((0, 0), (NOPE_DIM, 128 - NOPE_DIM - ROPE_DIM))).astype(bf16)
    bias = jnp.where(visible, 0.0, -1e30).astype(jnp.float32)
    half_rope = ROPE_DIM // 2
    tail_lanes = 128 - NOPE_DIM - ROPE_DIM
    tables = (
        jnp.concatenate(
            [jnp.ones((length, NOPE_DIM)), cosine, cosine, jnp.zeros((length, tail_lanes))], axis=1
        ).astype(jnp.float32),
        jnp.pad(-sine_part, ((0, 0), (NOPE_DIM, half_rope + tail_lanes))),
        jnp.pad(sine_part, ((0, 0), (NOPE_DIM + half_rope, tail_lanes))),
    )
    attended, queries, keyval, peaks = attend(
        query_latent, keyval_latent, query_w, keyval_w, key_lanes, bias, tables, scale_attn, rows_attn
    )
    peak_own = peaks.reshape(heads, 8, 128)[:, 0, 0]

    def heads_near(values):
        parts = values.reshape(model_count, group, share // group, -1)
        parts = lax.all_to_all(parts, "dp", 1, 2, axis_index_groups=near)
        return parts.reshape(model_count, share // group, -1)

    def heads_in(values):
        parts = values.reshape(model_count, share // group, group, -1)
        parts = lax.all_to_all(parts, "dp", 2, 1, axis_index_groups=near)
        return parts.reshape(length, -1)

    grad_out = cotangent.reshape(micro * share, WIDTH).astype(jnp.float32)
    mixed_own, attended, *output_parts = tie(
        (RESIDUAL * grad_out).astype(bf16), attended, *output_parts
    )
    output_w = rows_of(output_parts, group, data_count, data_index)
    mixed_parts = [mixed_own] + [
        swap_bit(mixed_own, bit, data_count) for bit in bits_of(group, data_count)
    ]
    attended, gate_halves[1] = tie(attended, gate_halves[1])
    attended = heads_near(attended)
    attended = lax.all_to_all(attended, "mp", 0, 0, tiled=True)
    down_t, attended, *mixed_parts = tie(units[2], attended, *mixed_parts)
    down_t = lax.all_gather(down_t, "mp", axis=0).reshape(hidden_units, WIDTH)
    attended_own = to_owners(attended, group, near).reshape(micro * share, -1)
    branch = dot_last(attended_own, output_w)
    hidden = tok + RESIDUAL * branch
    normed_two, inverse_two = rms_parts(hidden, gain_two)
    normed_two = normed_two.astype(bf16)

    far_count = data_count // group
    half_rows = micro * share // 2
    order = [
        [(far * group + place, half) for place in range(group) for half in range(2)]
        for far in range(far_count)
    ]

    def joined(values):
        pieces = gather_tokens(values, group, data_count)
        return jnp.concatenate([pieces[key] for keys in order for key in keys], axis=0)

    def parted(values, fillers):
        pieces = {}
        for at, key in enumerate([key for keys in order for key in keys]):
            pieces[key] = values[at * half_rows : (at + 1) * half_rows]
        return scatter_tokens(pieces, group, data_count, group, fillers)

    down_t = jnp.concatenate([down_t, gate_pad], axis=0)
    normed_full, *mixed_parts = tie(joined(normed_two), *mixed_parts)
    early = [0] + [bit // group for bit in bits_of(group, data_count)]
    mixed_parts = [
        mixed_parts[early.index(far)]
        if far in early
        else swap_bit(mixed_parts[0], far * group, data_count)
        for far in range(far_count)
    ]
    mixed_full = blocks_of(mixed_parts, group, data_count)
    gate_t = jnp.concatenate(
        [
            gate_halves[0].reshape(hidden_units, WIDTH),
            gate_pad,
            gate_halves[1].reshape(hidden_units, WIDTH),
            gate_pad,
        ],
        axis=0,
    )
    gateup = dot_last(normed_full, gate_t)
    gate_part = gateup[:, :padded]
    up_part = gateup[:, padded:]
    grad_act = dot_last(mixed_full, down_t)
    sigmoid_gate = jax.nn.sigmoid(gate_part)
    silu_gate = gate_part * sigmoid_gate
    activated = (silu_gate * up_part).astype(bf16)
    grad_gate = grad_act * up_part * sigmoid_gate * (1.0 + gate_part * (1.0 - sigmoid_gate))
    grad_up = grad_act * silu_gate
    grad_gateup = jnp.concatenate([grad_gate, grad_up], axis=1).astype(bf16)
    grad_normed_two, (grad_down_t, grad_gate_t) = parted(
        jnp.dot(grad_gateup, gate_t, preferred_element_type=jnp.float32).astype(bf16),
        [
            dot_first(activated, mixed_full).astype(bf16),
            dot_first(grad_gateup, normed_full).astype(bf16),
        ],
    )
    grad_normed_two = grad_normed_two.astype(jnp.float32)
    grad_down_t = grad_down_t[:hidden_units]

    down_sum = lax.psum_scatter(
        grad_down_t.reshape(model_count, unit_count, WIDTH), "mp", scatter_dimension=0, tiled=True
    )

    grad_hidden = grad_out + rms_back(hidden, inverse_two, gain_two, grad_normed_two)
    grad_gain_two = jnp.sum(grad_normed_two * hidden * inverse_two, axis=0)
    grad_branch = (RESIDUAL * grad_hidden).astype(bf16)
    gate_sum = grad_gate_t.reshape(2, padded, WIDTH)[:, :hidden_units]
    gate_sum = jnp.transpose(
        gate_sum.reshape(2, model_count, unit_count, WIDTH), (1, 0, 2, 3)
    ).reshape(model_count, 2 * unit_count, WIDTH)
    gate_sum = lax.psum_scatter(gate_sum, "mp", scatter_dimension=0, tiled=True)
    grad_attended = jnp.dot(grad_branch, output_w, preferred_element_type=jnp.float32)
    grad_attended = near_parts(
        grad_attended.astype(bf16).reshape(micro, share, -1), group, near
    )
    tail = grad_attended.shape[1] // 2
    early = lax.all_to_all(grad_attended[:, :tail], "mp", 0, 0, tiled=True)
    project_sum = near_sum(
        dot_first(grad_branch, attended_own), group, data_count, data_index
    )
    activated = in_order(list(activated.reshape(data_count, -1, padded)), data_index)
    late, early, activated, project_sum = tie(
        grad_attended[:, tail:], early, activated, project_sum
    )
    late = lax.all_to_all(late, "mp", 0, 0, tiled=True)
    mixed_out = jnp.dot(
        activated.reshape(-1, padded), down_t, preferred_element_type=jnp.float32
    ).astype(bf16)
    mixed_out = lax.psum_scatter(
        mixed_out.reshape(data_count, -1, WIDTH), "dp", scatter_dimension=0, tiled=True
    ).reshape(hidden.shape)
    grad_attended = heads_in(jnp.concatenate([early, late], axis=1))
    project_sum = far_sum(project_sum, group, data_count, data_index)
    grad_query_all, grad_keyval, grad_shared = attend_back(
        queries, keyval, grad_attended, key_lanes, bias, tables, scale_attn, rows_attn
    )
    grad_shared = rotate_back(
        grad_shared[:, NOPE_DIM : NOPE_DIM + ROPE_DIM], cosine, sine_part
    )
    latent_terms = jnp.concatenate(
        [dot_last(grad_query_all, query_w), dot_last(grad_keyval, keyval_w), grad_shared], axis=1
    ).astype(bf16)
    down_sum = jnp.transpose(down_sum.reshape(unit_count, data_count, -1), (1, 0, 2))
    down_sum = lax.all_to_all(down_sum, "dp", 0, 0, tiled=True)
    latent_terms, project_sum, down_sum = tie(latent_terms, project_sum, down_sum)
    down_sum = jnp.transpose(down_sum, (2, 0, 1)).reshape(down_weight.shape)
    layer_out = (hidden + RESIDUAL * mixed_out).astype(bf16)
    parts = latent_terms.reshape(model_count, group, share // group, latent_all)
    parts = lax.all_to_all(parts, "dp", 1, 0, axis_index_groups=near)
    parts = jnp.sum(parts.astype(jnp.float32), axis=0).astype(bf16)
    grad_both = jnp.concatenate(
        [
            dot_first(query_latent, grad_query_all)
            .astype(bf16)
            .reshape(data_count // group, group, query_rows, -1),
            dot_first(keyval_latent, grad_keyval)
            .astype(bf16)
            .reshape(data_count // group, group, keyval_rows, -1),
        ],
        axis=2,
    )
    gate_sum = jnp.transpose(gate_sum.reshape(2 * unit_count, data_count, -1), (1, 0, 2))
    parts, grad_both, gate_sum = tie(
        lax.all_to_all(parts, "mp", 0, 0, tiled=True), grad_both, gate_sum
    )
    gate_sum = lax.all_to_all(gate_sum, "dp", 0, 0, tiled=True)
    project_sum, gate_sum = tie(project_sum, gate_sum)
    gate_sum = jnp.transpose(
        gate_sum.reshape(data_count, 2, unit_count, -1), (3, 1, 0, 2)
    ).reshape(gateup_weight.shape)

    grad_both = far_sum(
        grad_both.reshape(data_count // group, group * (query_rows + keyval_rows), -1),
        group,
        data_count,
        data_index,
    )
    grad_latent_all = (
        to_owners(parts, group, near).reshape(micro * share, latent_all).astype(jnp.float32)
    )

    grad_query_up = grad_latent_all[:, :QUERY_RANK]
    grad_keyval_up = grad_latent_all[:, QUERY_RANK : QUERY_RANK + LATENT_RANK]
    grad_latent = jnp.concatenate(
        [
            rms_back(query_raw, inverse_query, gain_query, grad_query_up),
            rms_back(keyval_raw, inverse_keyval, gain_keyval, grad_keyval_up),
            grad_latent_all[:, QUERY_RANK + LATENT_RANK :],
        ],
        axis=1,
    ).astype(bf16)
    grad_gain_query = jnp.sum(grad_query_up * query_raw * inverse_query, axis=0)
    grad_gain_keyval = jnp.sum(grad_keyval_up * keyval_raw * inverse_keyval, axis=0)
    grad_normed = dot_last(grad_latent, lat_w)
    latent_sum = near_sum(dot_first(normed, grad_latent), group, data_count, data_index)
    input_grad = grad_hidden + rms_back(tok, inverse_one, gain_one, grad_normed)
    grad_gain_one = jnp.sum(grad_normed * tok * inverse_one, axis=0)
    grad_gains = jnp.concatenate(
        [grad_gain_one, grad_gain_two, grad_gain_query, grad_gain_keyval]
    )

    grad_both = lax.all_to_all(
        grad_both.astype(bf16).reshape(group, query_rows + keyval_rows, -1),
        "dp",
        0,
        1,
        axis_index_groups=near,
    )
    grad_both = scatter_columns(
        grad_both.reshape(query_rows + keyval_rows, -1), model_count
    )
    reduced = [
        scatter_columns(
            far_sum(latent_sum, group, data_count, data_index), model_count
        ),
        grad_both[:query_rows]
        .reshape(query_rows, own_heads, 128)[:, :, : NOPE_DIM + ROPE_DIM]
        .reshape(query_weight.shape),
        grad_both[query_rows:],
        scatter_columns(project_sum, model_count),
        gate_sum.astype(jnp.float32),
        down_sum.astype(jnp.float32),
    ]

    peak_row = lax.dynamic_update_slice(
        jnp.full((HEADS,), -1e30, jnp.float32), peak_own, (own_part * heads,)
    )
    small = jnp.concatenate(
        [
            grad_gains.reshape(data_count, -1),
            jnp.broadcast_to(peak_row[None], (data_count, HEADS)),
        ],
        axis=1,
    )
    small = lax.all_to_all(small, "dp", 0, 0, tiled=True)
    gain_count = gains.shape[0]
    small = jnp.concatenate(
        [jnp.sum(small[:, :gain_count], axis=0), jnp.max(small[:, gain_count:], axis=0)]
    )
    cells = ROTATE_ROWS * ROTATE_ROWS
    small = jnp.pad(small, (0, -(gain_count + HEADS) % cells)).reshape(-1, cells)
    grams = jnp.concatenate([gram_of(grad_w) for grad_w in reduced], axis=0)
    gram_count = grams.shape[0]
    packed = spread(
        jnp.concatenate([grams.reshape(gram_count, cells), small], axis=0), "mp", model_count
    )
    grams = jnp.sum(packed[:, :gram_count], axis=0).reshape(grams.shape)
    small = packed[:, gram_count:].reshape(model_count, -1)
    gains_grad = jnp.sum(small[:, :gain_count], axis=0)
    all_peaks = jnp.max(small[:, gain_count : gain_count + HEADS], axis=0)
    threshold = jnp.mean(all_peaks)
    clip_all = jnp.minimum(1.0, threshold / jnp.maximum(all_peaks, 1.0))
    clip_own = lax.dynamic_slice_in_dim(clip_all, model_index * own_heads, own_heads, 0)

    results = [
        layer_out.reshape(tokens.shape),
        input_grad.reshape(tokens.shape),
    ]
    new_stats = []
    start = 0
    for mat_index in range(6):
        stat_m = states[mat_index][2]
        gram_sum = grams[start : start + stat_m.shape[0]]
        start += stat_m.shape[0]
        new_stats.append(BETA_SECOND * stat_m + (1.0 - BETA_SECOND) * gram_sum)
    new_bases = renew_all(new_stats, [state[3] for state in states])
    for mat_index in range(6):
        first_m, second_m, stat_m, basis_m = states[mat_index]
        new_weight, new_first, new_second = rotated_update(
            matrices[mat_index],
            reduced[mat_index],
            first_m,
            second_m,
            basis_m,
            RATES[mat_index],
        )
        if mat_index == 1:
            new_weight = clip_columns(new_weight, clip_own, NOPE_DIM + ROPE_DIM, True)
        if mat_index == 2:
            new_weight = clip_columns(new_weight, clip_own, NOPE_DIM + VALUE_DIM, False)
        results.extend(
            [
                new_weight,
                new_weight.astype(jnp.bfloat16),
                new_first,
                new_second,
                new_stats[mat_index],
                new_bases[mat_index],
            ]
        )
    gains_first_new = BETA_FIRST * gains_first + (1.0 - BETA_FIRST) * gains_grad
    gains_second_new = BETA_SECOND * gains_second + (1.0 - BETA_SECOND) * gains_grad * gains_grad
    gains_step = (
        gains_first_new
        / (1.0 - BETA_FIRST**STEP_COUNT)
        / (jnp.sqrt(gains_second_new / (1.0 - BETA_SECOND**STEP_COUNT)) + ADAM_EPS)
    )
    results.extend(
        [gains - GAIN_RATE * (gains_step + DECAY * gains), gains_first_new, gains_second_new]
    )
    return tuple(results)


def solution(mesh):
    placed = (
        P(None, ("dp", "mp"), None),
        P(None, ("dp", "mp"), None),
        P(None, "dp", None),
        P("dp", "mp"),
        P("dp", "mp"),
        P("dp", "mp"),
        P("dp", None, None),
        P("dp", None, None),
        P("dp", "mp"),
        P("dp", "mp"),
        P("dp", "mp"),
        P("dp", None, None),
        P("dp", None, None),
        P("dp", "mp"),
        P("dp", "mp"),
        P("dp", "mp"),
        P("dp", None, None),
        P("dp", None, None),
        P("dp", "mp"),
        P("dp", "mp"),
        P("dp", "mp"),
        P("dp", None, None),
        P("dp", None, None),
        P("dp", None, "mp"),
        P("dp", None, "mp"),
        P("dp", None, "mp"),
        P("dp", None, None),
        P("dp", None, None),
        P("dp", "mp"),
        P("dp", "mp"),
        P("dp", "mp"),
        P("dp", None, None),
        P("dp", None, None),
        P("dp"),
        P("dp"),
        P("dp"),
    )
    return jax.shard_map(
        on_device,
        mesh=mesh,
        in_specs=placed,
        out_specs=(
            P(None, ("dp", "mp"), None),
            P(None, ("dp", "mp"), None),
            P("dp", "mp"),
            P("dp", "mp"),
            P("dp", "mp"),
            P("dp", "mp"),
            P("dp", None, None),
            P("dp", None, None),
            P("dp", "mp"),
            P("dp", "mp"),
            P("dp", "mp"),
            P("dp", "mp"),
            P("dp", None, None),
            P("dp", None, None),
            P("dp", "mp"),
            P("dp", "mp"),
            P("dp", "mp"),
            P("dp", "mp"),
            P("dp", None, None),
            P("dp", None, None),
            P("dp", "mp"),
            P("dp", "mp"),
            P("dp", "mp"),
            P("dp", "mp"),
            P("dp", None, None),
            P("dp", None, None),
            P("dp", None, "mp"),
            P("dp", None, "mp"),
            P("dp", None, "mp"),
            P("dp", None, "mp"),
            P("dp", None, None),
            P("dp", None, None),
            P("dp", "mp"),
            P("dp", "mp"),
            P("dp", "mp"),
            P("dp", "mp"),
            P("dp", None, None),
            P("dp", None, None),
            P("dp"),
            P("dp"),
            P("dp"),
        ),
        check_vma=False,
    )
```

```python
import functools
import math

import jax
import jax.numpy as jnp
from jax import lax
from jax.experimental import pallas as pl
from jax.experimental.layout import Layout, with_layout_constraint
from jax.experimental.pallas import tpu as pltpu
from jax.sharding import PartitionSpec as P

WIDTH = 2560
HEADS = 40
QUERY_RANK = 768
LATENT_RANK = 256
NOPE_DIM = 64
ROPE_DIM = 32
VALUE_DIM = 64
BLOCK = 128
ROTATE_ROWS = 16
STEP_COUNT = 10


HIGHEST = lax.Precision.HIGHEST
NORM_EPS = 1e-05
RESIDUAL = 1.4 / math.sqrt(62.0)
ROPE_BASE = 10000.0
BETA_FIRST = 0.95
BETA_SECOND = 0.95
ADAM_EPS = 1e-08
DECAY = 0.01
RATES = (0.08, 0.2, 0.25, 3.2, 0.08, 0.56)
GAIN_RATE = 0.8


def rms_parts(values, scale_gain):
    inverse = lax.rsqrt(jnp.mean(values * values, axis=-1, keepdims=True) + NORM_EPS)
    return (values * inverse * scale_gain, inverse)


def rms_back(values, inverse, scale_gain, upstream):
    weighted = upstream * scale_gain
    inner = jnp.mean(weighted * values, axis=-1, keepdims=True)
    return inverse * weighted - values * (inverse * inverse * inverse) * inner


def rotate(values, cosine, sine_part):
    half_dim = values.shape[-1] // 2
    first_half = values[..., :half_dim]
    second_half = values[..., half_dim:]
    return jnp.concatenate(
        [
            first_half * cosine - second_half * sine_part,
            second_half * cosine + first_half * sine_part,
        ],
        axis=-1,
    )


def rotate_back(grad_in, cosine, sine_part):
    half_dim = grad_in.shape[-1] // 2
    first_half = grad_in[..., :half_dim]
    second_half = grad_in[..., half_dim:]
    return jnp.concatenate(
        [
            first_half * cosine + second_half * sine_part,
            second_half * cosine - first_half * sine_part,
        ],
        axis=-1,
    )


def tree_layout(parent):
    block_count = parent.shape[0]
    identity = jnp.eye(block_count, dtype=jnp.float32)
    blocks = jnp.arange(block_count)
    parent_of = ((parent[:, None] == blocks[None, :]) & (blocks[:, None] > 0)).astype(jnp.float32)
    reached = identity
    for unused in range(block_count):
        reached = jnp.minimum(1.0, identity + jnp.dot(parent_of, reached, precision=HIGHEST))
    depths = jnp.sum(reached, axis=1) - 1.0
    length = block_count * BLOCK
    ancestor = (
        jnp.broadcast_to(
            reached[:, None, :, None], (block_count, BLOCK, block_count, BLOCK)
        ).reshape(length, length)
        > 0.5
    )
    tokens_at = jnp.arange(length)
    same_block = tokens_at[:, None] // BLOCK == tokens_at[None, :] // BLOCK
    visible = ancestor & (jnp.logical_not(same_block) | (tokens_at[None, :] <= tokens_at[:, None]))
    position = jnp.repeat(depths, BLOCK) * BLOCK + (tokens_at % BLOCK).astype(jnp.float32)
    frequency = ROPE_BASE ** (-(jnp.arange(ROPE_DIM // 2).astype(jnp.float32) * 2.0 / ROPE_DIM))
    angles = position[:, None] * frequency[None, :]
    return (visible, jnp.cos(angles), jnp.sin(angles))


def dot_first(first_arg, second_arg):
    return lax.dot_general(
        first_arg, second_arg, (((0,), (0,)), ((), ())), preferred_element_type=jnp.float32
    )


def dot_last(first_arg, second_arg):
    return lax.dot_general(
        first_arg, second_arg, (((1,), (1,)), ((), ())), preferred_element_type=jnp.float32
    )


def gram_of(grad_w):
    blocks = grad_w.reshape(grad_w.shape[0] // ROTATE_ROWS, ROTATE_ROWS, -1)
    return jnp.einsum("bic,bjc->bij", blocks, blocks, precision=HIGHEST)


def rotated_update(weight, grad_w, first_m, second_m, basis_m, step_rate):
    blocks = grad_w.reshape(basis_m.shape[0], basis_m.shape[1], -1)
    turned = jnp.einsum("bij,bic->bjc", basis_m, blocks, precision=HIGHEST).reshape(grad_w.shape)
    new_first = BETA_FIRST * first_m + (1.0 - BETA_FIRST) * turned
    new_second = BETA_SECOND * second_m + (1.0 - BETA_SECOND) * turned * turned
    normal_step = (
        new_first
        / (1.0 - BETA_FIRST**STEP_COUNT)
        / (jnp.sqrt(new_second / (1.0 - BETA_SECOND**STEP_COUNT)) + ADAM_EPS)
    )
    rotated_back = jnp.einsum(
        "bij,bjc->bic", basis_m, normal_step.reshape(blocks.shape), precision=HIGHEST
    ).reshape(grad_w.shape)
    new_weight = weight - step_rate * (rotated_back + DECAY * weight)
    return (new_weight, new_first, new_second)


def clip_columns(new_weight, clip_factor, head_width, rope_scaled):
    rows = new_weight.shape[0]
    root_factor = jnp.sqrt(clip_factor)
    tail_factor = clip_factor if rope_scaled else jnp.ones_like(clip_factor)
    column_scale = jnp.concatenate(
        [
            jnp.broadcast_to(root_factor[:, None], (clip_factor.shape[0], NOPE_DIM)),
            jnp.broadcast_to(tail_factor[:, None], (clip_factor.shape[0], head_width - NOPE_DIM)),
        ],
        axis=1,
    )
    return (
        new_weight.reshape(rows, clip_factor.shape[0], head_width) * column_scale[None]
    ).reshape(new_weight.shape)


def groups_of(data_count, group_size):
    near = [[start + i for i in range(group_size)] for start in range(0, data_count, group_size)]
    cross = [[i + start for start in range(0, data_count, group_size)] for i in range(group_size)]
    return near, cross


def near_parts(values, group_size, near):
    micro, count, width = values.shape
    parts = values.reshape(micro, group_size, count // group_size, width)
    parts = lax.all_to_all(parts, "dp", 1, 0, axis_index_groups=near)
    return parts.reshape(group_size * micro, count // group_size, width)


def to_trees(values, group_size, near):
    return lax.all_to_all(near_parts(values, group_size, near), "mp", 0, 0, tiled=True)


def to_owners(values, group_size, near):
    planes, count, width = values.shape
    parts = values.reshape(group_size, planes // group_size, count, width)
    parts = lax.all_to_all(parts, "dp", 0, 1, axis_index_groups=near)
    return parts.reshape(planes // group_size, group_size * count, width)


def spread(values, axis_name, count, groups=None):
    return lax.all_to_all(
        jnp.broadcast_to(values[None], (count,) + values.shape),
        axis_name,
        0,
        0,
        tiled=True,
        axis_index_groups=groups,
    )


def swap_bit(values, bit, data_count):
    return lax.ppermute(values, "dp", [(i, i ^ bit) for i in range(data_count)])


def bits_of(group_size, data_count):
    bits = []
    bit = group_size
    while bit < data_count:
        bits.append(bit)
        bit *= 2
    return bits


def gather_tokens(values, group_size, data_count):
    rows = values.shape[0] // 2
    bits = bits_of(group_size, data_count)
    pieces = {}
    for half in range(2):
        got = {0: values[half * rows : (half + 1) * rows]}
        for bit in bits if half == 0 else bits[::-1]:
            for index in sorted(got):
                got[index ^ bit] = swap_bit(got[index], bit, data_count)
        for index in sorted(got):
            pieces[(index, half)] = got[index]
            for near in range(1, group_size):
                pieces[(index ^ near, half)] = swap_bit(got[index], near, data_count)
    return pieces


def add_low(first_arg, second_arg):
    return (first_arg.astype(jnp.float32) + second_arg.astype(jnp.float32)).astype(jnp.bfloat16)


def scatter_tokens(pieces, group_size, data_count, near_count, fillers):
    bits = bits_of(group_size, data_count)
    fillers = list(fillers)
    held = [{}, {}]
    far = range(0, data_count, group_size)
    sent = {
        (index, half, near): swap_bit(pieces[(index ^ near, half)], near, data_count)
        for half in range(2)
        for index in far
        for near in range(1, near_count)
    }
    keys = sorted(sent)
    fillers[0], *arrived = tie(fillers[0], *[sent[key] for key in keys])
    sent = dict(zip(keys, arrived))
    for half in range(2):
        for index in far:
            total = pieces[(index, half)]
            for near in range(1, near_count):
                total = add_low(total, sent[(index, half, near)])
            held[half][index] = total
    for step in range(len(bits)):
        sent = {}
        for half in range(2):
            bit = bits[step] if half == 0 else bits[::-1][step]
            for index in held[half]:
                if not index & bit:
                    sent[(index, half)] = swap_bit(held[half][index ^ bit], bit, data_count)
        keys = sorted(sent)
        if step + 1 < len(fillers):
            fillers[step + 1], *arrived = tie(fillers[step + 1], *[sent[key] for key in keys])
            sent = dict(zip(keys, arrived))
        held = [
            {
                index: add_low(held[half][index], sent[(index, half)])
                for index in held[half]
                if (index, half) in sent
            }
            for half in range(2)
        ]
    return jnp.concatenate([held[half][0] for half in range(2)], axis=0), fillers


def spread_planes(values, model_count, model_index):
    out = jnp.zeros((model_count,) + values.shape, values.dtype)
    for shift in range(model_count):
        part = values
        if shift:
            part = lax.ppermute(
                values, "mp", [(i, (i + shift) % model_count) for i in range(model_count)]
            )
        place = (model_index + model_count - shift) % model_count
        out = lax.dynamic_update_slice(out, part[None], (place,) + (0,) * values.ndim)
    return out


def row_major(values):
    return with_layout_constraint(values, Layout(major_to_minor=tuple(range(values.ndim))))


def far_parts(block, group_size, data_count):
    return [block] + [
        swap_bit(block, far, data_count) for far in range(group_size, data_count, group_size)
    ]


def in_order(parts, own):
    out = jnp.zeros((len(parts),) + parts[0].shape, parts[0].dtype)
    for index, part in enumerate(parts):
        out = lax.dynamic_update_slice(out, part[None], (own ^ index,) + (0,) * part.ndim)
    return row_major(out)


def rows_of(parts, group_size, data_count, data_index):
    far = in_order(parts, data_index // group_size)
    own = data_index % group_size
    out = jnp.zeros((len(parts), group_size) + parts[0].shape, far.dtype)
    for near in range(group_size):
        part = far if near == 0 else swap_bit(far, near, data_count)
        out = lax.dynamic_update_slice(out, part[:, None], (0, own ^ near, 0, 0))
    return out.reshape((data_count * parts[0].shape[0],) + parts[0].shape[1:])


def blocks_of(parts, group_size, data_count):
    blocks = []
    for part in parts:
        blocks.append(part)
        for near in range(1, group_size):
            blocks.append(swap_bit(part, near, data_count))
    return jnp.concatenate(blocks, axis=0)


def scatter_blocks(values, group_size, data_count):
    parts = values.reshape(data_count // group_size, group_size, -1, values.shape[-1])
    total = parts[:, 0].astype(jnp.float32)
    for near in range(1, group_size):
        total = total + swap_bit(parts[:, near], near, data_count).astype(jnp.float32)
    total = total.astype(jnp.bfloat16)
    result = total[0].astype(jnp.float32)
    for far in range(1, data_count // group_size):
        result = result + swap_bit(total[far], far * group_size, data_count).astype(jnp.float32)
    return result


def tie(*values):
    return lax.optimization_barrier(values)


def far_shares(parts, group_size, data_count, data_index):
    own = data_index // group_size
    shares = []
    for far in range(data_count // group_size):
        part = lax.dynamic_index_in_dim(parts, own ^ far, 0, keepdims=False)
        shares.append(swap_bit(part, far * group_size, data_count) if far else part)
    return shares


def sum_of(shares):
    return sum((share.astype(jnp.float32) for share in shares[1:]), shares[0].astype(jnp.float32))


def far_sum(parts, group_size, data_count, data_index):
    return sum_of(far_shares(parts, group_size, data_count, data_index))


def near_sum(grad_w, group_size, data_count, data_index):
    own = data_index % group_size
    parts = grad_w.astype(jnp.bfloat16).reshape(
        data_count // group_size, group_size, -1, grad_w.shape[-1]
    )

    def part_of(near):
        return lax.dynamic_index_in_dim(parts, own ^ near, 1, keepdims=False)

    total = part_of(0).astype(jnp.float32)
    for near in range(1, group_size):
        total = total + swap_bit(part_of(near), near, data_count).astype(jnp.float32)
    return total.astype(jnp.bfloat16)


def scatter_columns(grad_w, model_count):
    rows, width = grad_w.shape
    parts = grad_w.astype(jnp.bfloat16).reshape(rows, model_count, width // model_count)
    parts = lax.all_to_all(jnp.swapaxes(parts, 0, 1), "mp", 0, 0, tiled=True)
    return jnp.sum(parts.astype(jnp.float32), axis=0)


def basis_kernel(stat_ref, basis_ref, out_ref):
    size = stat_ref.shape[0]
    columns = jnp.zeros(stat_ref.shape, jnp.float32)
    for j in range(size):
        columns = columns + basis_ref[j][:, None, :] * stat_ref[j][None, :, :]
    for j in range(size):
        column = columns[j]
        norm = jnp.sum(column * column, axis=0, keepdims=True)
        column = column * lax.rsqrt(norm)
        out_ref[j] = column
        shares = jnp.sum(columns * column[None], axis=1, keepdims=True)
        columns = columns - shares * column[None]


def renew_all(stats, bases):
    counts = [stat_m.shape[0] for stat_m in stats]
    total = sum(counts)
    padded = -(-total // 128) * 128
    stat_t = jnp.concatenate([jnp.transpose(s, (2, 1, 0)) for s in stats], axis=2)
    basis_t = jnp.concatenate([jnp.transpose(b, (1, 2, 0)) for b in bases], axis=2)
    pad = ((0, 0), (0, 0), (0, padded - total))
    stat_t = jnp.pad(stat_t, pad, constant_values=1.0)
    basis_t = jnp.pad(basis_t, pad, constant_values=1.0)
    out = pl.pallas_call(
        basis_kernel,
        out_shape=jax.ShapeDtypeStruct((ROTATE_ROWS, ROTATE_ROWS, padded), jnp.float32),
    )(stat_t, basis_t)
    results = []
    start = 0
    for count in counts:
        results.append(jnp.transpose(out[:, :, start : start + count], (2, 1, 0)))
        start += count
    return results


LOG2E = 1.4426950408889634


def exp_rows(query, keys, bias, scale):
    scores = lax.dot_general(
        query, keys, (((1,), (1,)), ((), ())), preferred_element_type=jnp.float32
    )
    scores = scores * (scale * LOG2E) + bias
    top = jnp.max(scores, axis=-1, keepdims=True)
    raised = jnp.exp2(scores - top)
    return raised, top, 1.0 / jnp.sum(raised, axis=-1, keepdims=True)


def attend_kernel(
    scale,
    rows,
    query_latent_ref,
    keyval_latent_ref,
    query_w_ref,
    keyval_w_ref,
    key_ref,
    bias_ref,
    cos_ref,
    left_ref,
    right_ref,
    out_ref,
    query_ref,
    keyval_ref,
    peak_ref,
):
    bf16 = jnp.bfloat16
    length = key_ref.shape[0]
    raw = jnp.dot(query_latent_ref[...], query_w_ref[...], preferred_element_type=jnp.float32)
    both = jnp.dot(keyval_latent_ref[...], keyval_w_ref[...], preferred_element_type=jnp.float32)
    keyval_ref[...] = both.astype(bf16)
    lane = lax.broadcasted_iota(jnp.int32, (1, 128), 1)
    for head in range(2):
        at = slice(head * 128, head * 128 + 128)
        part = raw[:, at]
        query_ref[:, at] = (
            part * cos_ref[...]
            + pltpu.roll(part, 128 - ROPE_DIM // 2, 1) * left_ref[...]
            + pltpu.roll(part, ROPE_DIM // 2, 1) * right_ref[...]
        ).astype(bf16)
    for first in range(0, length, rows):
        last = first + rows
        outs = []
        for head in range(2):
            at = slice(head * 128, head * 128 + 128)
            keyval = keyval_ref[:last, at]
            keys = jnp.where(lane < NOPE_DIM, keyval, key_ref[:last, :])
            raised, top, inverse = exp_rows(
                query_ref[first:last, at], keys, bias_ref[first:last, :last], scale
            )
            outs.append(
                jnp.dot(raised.astype(bf16), keyval, preferred_element_type=jnp.float32) * inverse
            )
            tops = jnp.max(top) * (1.0 / LOG2E)
            spot = slice(head * 8, head * 8 + 8)
            if first == 0:
                peak_ref[0, spot, :] = jnp.full((8, 128), tops, jnp.float32)
            else:
                peak_ref[0, spot, :] = jnp.maximum(peak_ref[0, spot, :], tops)
        out_ref[first:last, :] = jnp.where(
            lane < VALUE_DIM, pltpu.roll(outs[0], VALUE_DIM, 1), outs[1]
        ).astype(bf16)


def attend_back_kernel(
    scale,
    rows,
    query_ref,
    keyval_ref,
    grad_ref,
    key_ref,
    bias_ref,
    cos_ref,
    left_ref,
    right_ref,
    query_out_ref,
    keyval_out_ref,
    shared_out_ref,
    pair_ref,
    total_ref,
):
    bf16 = jnp.bfloat16
    length = key_ref.shape[0]
    lane = lax.broadcasted_iota(jnp.int32, (1, 128), 1)
    low_lanes = lane < NOPE_DIM

    @pl.when(pl.program_id(0) == 0)
    def clear():
        total_ref[...] = jnp.zeros_like(total_ref)

    for head in range(2):
        at = slice(head * 128, head * 128 + 128)
        pair_ref[...] = jnp.zeros_like(pair_ref)
        for first in range(0, length, rows):
            last = first + rows
            keyval = keyval_ref[:last, at]
            keys = jnp.where(low_lanes, keyval, key_ref[:last, :])
            query = query_ref[first:last, at]
            grad = grad_ref[first:last, :].astype(jnp.float32)
            if head == 0:
                grad = pltpu.roll(grad, VALUE_DIM, 1)
            grad = jnp.where(low_lanes, 0.0, grad).astype(bf16)
            raised, _, inverse = exp_rows(query, keys, bias_ref[first:last, :last], scale)
            probs = raised * inverse
            grad_probs = lax.dot_general(
                grad, keyval, (((1,), (1,)), ((), ())), preferred_element_type=jnp.float32
            )
            inner = jnp.sum(probs * grad_probs, axis=-1, keepdims=True)
            grad_scores = (probs * (grad_probs - inner)).astype(bf16)
            part = jnp.dot(grad_scores, keys, preferred_element_type=jnp.float32) * scale
            query_out_ref[first:last, at] = (
                part * cos_ref[first:last, :]
                - pltpu.roll(part, 128 - ROPE_DIM // 2, 1) * left_ref[first:last, :]
                - pltpu.roll(part, ROPE_DIM // 2, 1) * right_ref[first:last, :]
            ).astype(bf16)
            zero = jnp.zeros_like(query)
            left = jnp.concatenate([grad_scores, probs.astype(bf16)], axis=0)
            right = jnp.concatenate(
                [
                    jnp.concatenate(
                        [jnp.where(low_lanes, query, zero), jnp.where(low_lanes, zero, query)],
                        axis=1,
                    ),
                    jnp.concatenate([grad, zero], axis=1),
                ],
                axis=0,
            )
            both = lax.dot_general(
                left, right, (((0,), (0,)), ((), ())), preferred_element_type=jnp.float32
            )
            pair_ref[:last, :] += both[:, :128]
            total_ref[:last, :] += both[:, 128:]
        keyval_out_ref[:, at] = (pair_ref[...] * jnp.where(low_lanes, scale, 1.0)).astype(bf16)

    @pl.when(pl.program_id(0) == pl.num_programs(0) - 1)
    def finish():
        shared_out_ref[...] = total_ref[...] * scale


def attend_cost(length, steps, products):
    return pl.CostEstimate(
        flops=int(products * 2 * steps * 2 * length * length * 256),
        bytes_accessed=steps * length * 256 * 8,
        transcendentals=steps * 2 * length * length,
    )


def resident(shape):
    return pl.BlockSpec(shape, lambda step: (0,) * len(shape))


def attend(query_latent, keyval_latent, query_w, keyval_w, key_lanes, bias, tables, scale, rows):
    length = bias.shape[0]
    steps = query_w.shape[1] // 256
    wide = jax.ShapeDtypeStruct((length, steps * 256), jnp.bfloat16)
    column = lambda width: pl.BlockSpec((length, width), lambda step: (0, step))
    return pl.pallas_call(
        functools.partial(attend_kernel, scale, rows),
        grid=(steps,),
        in_specs=[
            resident(query_latent.shape),
            resident(keyval_latent.shape),
            pl.BlockSpec((query_w.shape[0], 256), lambda step: (0, step)),
            pl.BlockSpec((keyval_w.shape[0], 256), lambda step: (0, step)),
            resident(key_lanes.shape),
            resident(bias.shape),
        ]
        + [resident(table.shape) for table in tables],
        out_specs=[
            column(128),
            column(256),
            column(256),
            pl.BlockSpec((1, 16, 128), lambda step: (step, 0, 0)),
        ],
        out_shape=[
            jax.ShapeDtypeStruct((length, steps * 128), jnp.bfloat16),
            wide,
            wide,
            jax.ShapeDtypeStruct((steps, 16, 128), jnp.float32),
        ],
        compiler_params=pltpu.CompilerParams(vmem_limit_bytes=56 * 1024 * 1024),
        cost_estimate=attend_cost(length, steps, 2.0),
    )(query_latent, keyval_latent, query_w, keyval_w, key_lanes, bias, *tables)


def attend_back(queries, keyval, grad, key_lanes, bias, tables, scale, rows):
    length = bias.shape[0]
    steps = queries.shape[1] // 256
    wide = jax.ShapeDtypeStruct(queries.shape, jnp.bfloat16)
    column = lambda width: pl.BlockSpec((length, width), lambda step: (0, step))
    return pl.pallas_call(
        functools.partial(attend_back_kernel, scale, rows),
        grid=(steps,),
        in_specs=[
            column(256),
            column(256),
            column(128),
            resident(key_lanes.shape),
            resident(bias.shape),
        ]
        + [resident(table.shape) for table in tables],
        out_specs=[column(256), column(256), resident((length, 128))],
        out_shape=[wide, wide, jax.ShapeDtypeStruct((length, 128), jnp.float32)],
        scratch_shapes=[
            pltpu.VMEM((length, 128), jnp.float32),
            pltpu.VMEM((length, 128), jnp.float32),
        ],
        compiler_params=pltpu.CompilerParams(vmem_limit_bytes=56 * 1024 * 1024),
        cost_estimate=attend_cost(length, steps, 4.0),
    )(queries, keyval, grad, key_lanes, bias, *tables)


def on_device(
    tokens,
    cotangent,
    parents,
    latent_weight,
    latent_first,
    latent_second,
    latent_stat,
    latent_basis,
    query_weight,
    query_first,
    query_second,
    query_stat,
    query_basis,
    keyval_weight,
    keyval_first,
    keyval_second,
    keyval_stat,
    keyval_basis,
    project_weight,
    project_first,
    project_second,
    project_stat,
    project_basis,
    gateup_weight,
    gateup_first,
    gateup_second,
    gateup_stat,
    gateup_basis,
    down_weight,
    down_first,
    down_second,
    down_stat,
    down_basis,
    gains,
    gains_first,
    gains_second,
):
    matrices = (
        latent_weight,
        query_weight,
        keyval_weight,
        project_weight,
        gateup_weight,
        down_weight,
    )
    states = (
        (latent_first, latent_second, latent_stat, latent_basis),
        (query_first, query_second, query_stat, query_basis),
        (keyval_first, keyval_second, keyval_stat, keyval_basis),
        (project_first, project_second, project_stat, project_basis),
        (gateup_first, gateup_second, gateup_stat, gateup_basis),
        (down_first, down_second, down_stat, down_basis),
    )
    bf16 = jnp.bfloat16
    data_count = lax.axis_size("dp")
    model_count = lax.axis_size("mp")
    micro, share, _ = tokens.shape
    group = model_count // micro
    near, cross = groups_of(data_count, group)
    data_index = lax.axis_index("dp")
    model_index = lax.axis_index("mp")
    own_part = data_index % group
    length = share * model_count
    heads = HEADS // group
    scale_attn = float(NOPE_DIM + ROPE_DIM) ** (-0.5)
    rows_attn = min(512, length)
    own_heads = query_weight.shape[1] // (NOPE_DIM + ROPE_DIM)
    latent_all = latent_weight.shape[1] * model_count

    def columns(far):
        return jnp.swapaxes(far, 0, 1).reshape(far.shape[1], -1)

    def exchange_units(values):
        return lax.all_to_all(values, "dp", 0, 0, tiled=True)

    query_rows = query_weight.shape[0]
    keyval_rows = keyval_weight.shape[0]
    unit_count = down_weight.shape[1] // data_count
    hidden_units = unit_count * model_count
    padded = -(-hidden_units // 128) * 128
    gain_all = spread(gains.astype(bf16), "dp", data_count)
    output_w = lax.all_gather(project_weight.astype(bf16), "mp", axis=0)
    lat_w = spread_planes(row_major(latent_weight.astype(bf16)), model_count, model_index)
    query_pad = jnp.pad(
        query_weight.astype(bf16).reshape(query_rows, own_heads, NOPE_DIM + ROPE_DIM),
        ((0, 0), (0, 0), (0, 128 - NOPE_DIM - ROPE_DIM)),
    ).reshape(query_rows, own_heads * 128)
    both_w = jnp.concatenate([query_pad, keyval_weight.astype(bf16)], axis=0)
    both_w, lat_w = tie(row_major(both_w), lat_w)
    both_w = spread_planes(both_w, model_count, model_index)
    units = jnp.concatenate(
        [
            jnp.transpose(
                gateup_weight.astype(bf16).reshape(-1, 2, data_count, unit_count), (2, 1, 3, 0)
            ),
            jnp.transpose(
                down_weight.astype(bf16).reshape(-1, 1, data_count, unit_count), (2, 1, 3, 0)
            ),
        ],
        axis=1,
    )
    units = exchange_units(units)
    lat_w = far_parts(row_major(columns(lat_w)), group, data_count)
    both_w, units, *lat_w = tie(columns(both_w), units, *lat_w)
    both_w = both_w.reshape(query_rows + keyval_rows, group, -1)
    both_w = lax.all_to_all(both_w, "dp", 1, 0, axis_index_groups=near)
    both_parts = far_parts(row_major(both_w), group, data_count)
    lat_w = rows_of(lat_w, group, data_count, data_index)
    gain_all = gain_all.reshape(-1).astype(jnp.float32)
    gain_one = gain_all[:WIDTH]
    gain_two = gain_all[WIDTH : 2 * WIDTH]
    gain_query = gain_all[2 * WIDTH : 2 * WIDTH + QUERY_RANK]
    gain_keyval = gain_all[2 * WIDTH + QUERY_RANK :]

    tok = tokens.reshape(micro * share, WIDTH).astype(jnp.float32)
    normed, inverse_one = rms_parts(tok, gain_one)
    normed = normed.astype(bf16)
    latent = jnp.dot(normed, lat_w, preferred_element_type=jnp.float32).astype(bf16)
    latent = latent.astype(jnp.float32)
    query_raw = latent[:, :QUERY_RANK]
    keyval_raw = latent[:, QUERY_RANK : QUERY_RANK + LATENT_RANK]
    key_rope = latent[:, QUERY_RANK + LATENT_RANK :]
    query_normed, inverse_query = rms_parts(query_raw, gain_query)
    keyval_normed, inverse_keyval = rms_parts(keyval_raw, gain_keyval)
    sent = jnp.concatenate([query_normed, keyval_normed, key_rope], axis=1).astype(bf16)

    mid = near_parts(sent.reshape(micro, share, latent_all), group, near)
    mid = lax.all_to_all(mid, "mp", 0, 0, tiled=True)
    mid, *both_parts = tie(mid, *both_parts)
    both_w = in_order(both_parts, data_index // group)
    units = jnp.transpose(units, (1, 2, 0, 3)).reshape(3, unit_count, WIDTH)
    gate_first = lax.all_gather(units[0], "mp", axis=0)
    gate_pad = jnp.zeros((padded - hidden_units, WIDTH), bf16)
    tree = spread(mid, "dp", group, near)
    tree, both_w, output_w = tie(tree, both_w, output_w)
    tree, gate_first = tie(tree, gate_first)
    query_w = both_w[:, :, :query_rows].reshape(data_count * query_rows, -1)
    keyval_w = both_w[:, :, query_rows:].reshape(data_count * keyval_rows, -1)
    gate_halves = [gate_first, lax.all_gather(units[1], "mp", axis=0)]
    output_parts = far_parts(row_major(columns(output_w)), group, data_count)
    tree = jnp.swapaxes(tree, 0, 1).reshape(length, latent_all)
    tree_parents = jnp.zeros((group, micro, parents.shape[2]), parents.dtype)
    own_parents, normed = tie(parents[:, 0], normed)
    for place in range(group):
        part = own_parents if place == 0 else swap_bit(own_parents, place, data_count)
        tree_parents = lax.dynamic_update_slice(
            tree_parents, part[None], (own_part ^ place, 0, 0)
        )
    tree_parents = tree_parents.reshape(group * micro, -1)
    visible, cosine, sine_part = tree_layout(
        lax.dynamic_index_in_dim(tree_parents, model_index, 0, keepdims=False)
    )
    query_latent = tree[:, :QUERY_RANK]
    keyval_latent = tree[:, QUERY_RANK : QUERY_RANK + LATENT_RANK]
    shared = rotate(
        tree[:, QUERY_RANK + LATENT_RANK :].astype(jnp.float32), cosine, sine_part
    )
    key_lanes = jnp.pad(shared, ((0, 0), (NOPE_DIM, 128 - NOPE_DIM - ROPE_DIM))).astype(bf16)
    bias = jnp.where(visible, 0.0, -1e30).astype(jnp.float32)
    half_rope = ROPE_DIM // 2
    tail_lanes = 128 - NOPE_DIM - ROPE_DIM
    tables = (
        jnp.concatenate(
            [jnp.ones((length, NOPE_DIM)), cosine, cosine, jnp.zeros((length, tail_lanes))], axis=1
        ).astype(jnp.float32),
        jnp.pad(-sine_part, ((0, 0), (NOPE_DIM, half_rope + tail_lanes))),
        jnp.pad(sine_part, ((0, 0), (NOPE_DIM + half_rope, tail_lanes))),
    )
    attended, queries, keyval, peaks = attend(
        query_latent, keyval_latent, query_w, keyval_w, key_lanes, bias, tables, scale_attn, rows_attn
    )
    peak_own = peaks.reshape(heads, 8, 128)[:, 0, 0]

    def heads_near(values):
        parts = values.reshape(model_count, group, share // group, -1)
        parts = lax.all_to_all(parts, "dp", 1, 2, axis_index_groups=near)
        return parts.reshape(model_count, share // group, -1)

    def heads_in(values):
        parts = values.reshape(model_count, share // group, group, -1)
        parts = lax.all_to_all(parts, "dp", 2, 1, axis_index_groups=near)
        return parts.reshape(length, -1)

    grad_out = cotangent.reshape(micro * share, WIDTH).astype(jnp.float32)
    mixed_own, attended = tie((RESIDUAL * grad_out).astype(bf16), attended)
    mixed_parts = [mixed_own] + [
        swap_bit(mixed_own, bit, data_count) for bit in bits_of(group, data_count)
    ]
    attended, gate_halves[1] = tie(attended, gate_halves[1])
    attended, *output_parts = tie(heads_near(attended), *output_parts)
    middle = attended.shape[1] // 2
    early = lax.all_to_all(attended[:, :middle], "mp", 0, 0, tiled=True)
    late, early, *output_parts = tie(attended[:, middle:], early, *output_parts)
    late = lax.all_to_all(late, "mp", 0, 0, tiled=True)
    output_w = rows_of(output_parts, group, data_count, data_index)
    attended = jnp.concatenate([early, late], axis=1)
    down_t, attended = tie(units[2], attended)
    down_t = lax.all_gather(down_t, "mp", axis=0).reshape(hidden_units, WIDTH)
    attended_own = to_owners(attended, group, near).reshape(micro * share, -1)
    attended_own, *mixed_parts = tie(attended_own, *mixed_parts)
    branch = dot_last(attended_own, output_w)
    hidden = tok + RESIDUAL * branch
    normed_two, inverse_two = rms_parts(hidden, gain_two)
    normed_two = normed_two.astype(bf16)

    far_count = data_count // group
    half_rows = micro * share // 2
    order = [
        [(far * group + place, half) for place in range(group) for half in range(2)]
        for far in range(far_count)
    ]

    def joined(values):
        pieces = gather_tokens(values, group, data_count)
        return jnp.concatenate([pieces[key] for keys in order for key in keys], axis=0)

    def parted(values, fillers):
        pieces = {}
        for at, key in enumerate([key for keys in order for key in keys]):
            pieces[key] = values[at * half_rows : (at + 1) * half_rows]
        return scatter_tokens(pieces, group, data_count, group, fillers)

    down_t = jnp.concatenate([down_t, gate_pad], axis=0)
    normed_full, *mixed_parts = tie(joined(normed_two), *mixed_parts)
    sent_far = [0] + [bit // group for bit in bits_of(group, data_count)]
    mixed_parts = [
        mixed_parts[sent_far.index(far)]
        if far in sent_far
        else swap_bit(mixed_parts[0], far * group, data_count)
        for far in range(far_count)
    ]
    mixed_full = blocks_of(mixed_parts, group, data_count)
    gate_t = jnp.concatenate(
        [
            gate_halves[0].reshape(hidden_units, WIDTH),
            gate_pad,
            gate_halves[1].reshape(hidden_units, WIDTH),
            gate_pad,
        ],
        axis=0,
    )
    gateup = dot_last(normed_full, gate_t)
    gate_part = gateup[:, :padded]
    up_part = gateup[:, padded:]
    grad_act = dot_last(mixed_full, down_t)
    sigmoid_gate = jax.nn.sigmoid(gate_part)
    silu_gate = gate_part * sigmoid_gate
    activated = (silu_gate * up_part).astype(bf16)
    grad_gate = grad_act * up_part * sigmoid_gate * (1.0 + gate_part * (1.0 - sigmoid_gate))
    grad_up = grad_act * silu_gate
    grad_gateup = jnp.concatenate([grad_gate, grad_up], axis=1).astype(bf16)
    grad_normed_two, (grad_down_t, grad_gate_t) = parted(
        jnp.dot(grad_gateup, gate_t, preferred_element_type=jnp.float32).astype(bf16),
        [
            dot_first(activated, mixed_full).astype(bf16),
            dot_first(grad_gateup, normed_full).astype(bf16),
        ],
    )
    grad_normed_two = grad_normed_two.astype(jnp.float32)
    grad_down_t = grad_down_t[:hidden_units]

    down_sum = lax.psum_scatter(
        grad_down_t.reshape(model_count, unit_count, WIDTH), "mp", scatter_dimension=0, tiled=True
    )

    grad_hidden = grad_out + rms_back(hidden, inverse_two, gain_two, grad_normed_two)
    grad_gain_two = jnp.sum(grad_normed_two * hidden * inverse_two, axis=0)
    grad_branch = (RESIDUAL * grad_hidden).astype(bf16)
    gate_sum = grad_gate_t.reshape(2, padded, WIDTH)[:, :hidden_units]
    gate_sum = jnp.transpose(
        gate_sum.reshape(2, model_count, unit_count, WIDTH), (1, 0, 2, 3)
    ).reshape(model_count, 2 * unit_count, WIDTH)
    gate_sum = lax.psum_scatter(gate_sum, "mp", scatter_dimension=0, tiled=True)
    grad_attended = jnp.dot(grad_branch, output_w, preferred_element_type=jnp.float32)
    grad_attended, grad_branch = tie(
        near_parts(grad_attended.astype(bf16).reshape(micro, share, -1), group, near), grad_branch
    )
    tail = grad_attended.shape[1] // 2
    early = lax.all_to_all(grad_attended[:, :tail], "mp", 0, 0, tiled=True)
    project_sum = near_sum(
        dot_first(grad_branch, attended_own), group, data_count, data_index
    )
    activated = in_order(list(activated.reshape(data_count, -1, padded)), data_index)
    late, early, activated, project_sum = tie(
        grad_attended[:, tail:], early, activated, project_sum
    )
    late = lax.all_to_all(late, "mp", 0, 0, tiled=True)
    mixed_out = jnp.dot(
        activated.reshape(-1, padded), down_t, preferred_element_type=jnp.float32
    ).astype(bf16)
    mixed_out = lax.psum_scatter(
        mixed_out.reshape(data_count, -1, WIDTH), "dp", scatter_dimension=0, tiled=True
    ).reshape(hidden.shape)
    grad_attended = heads_in(jnp.concatenate([early, late], axis=1))
    project_shares = far_shares(project_sum, group, data_count, data_index)
    grad_query_all, grad_keyval, grad_shared = attend_back(
        queries, keyval, grad_attended, key_lanes, bias, tables, scale_attn, rows_attn
    )
    grad_query_all, *project_shares = tie(grad_query_all, *project_shares)
    project_sum = sum_of(project_shares)
    grad_shared = rotate_back(
        grad_shared[:, NOPE_DIM : NOPE_DIM + ROPE_DIM], cosine, sine_part
    )
    latent_terms = jnp.concatenate(
        [dot_last(grad_query_all, query_w), dot_last(grad_keyval, keyval_w), grad_shared], axis=1
    ).astype(bf16)
    down_sum = jnp.transpose(down_sum.reshape(unit_count, data_count, -1), (1, 0, 2))
    down_sum = lax.all_to_all(down_sum, "dp", 0, 0, tiled=True)
    latent_terms, project_sum, down_sum = tie(latent_terms, project_sum, down_sum)
    down_sum = jnp.transpose(down_sum, (2, 0, 1)).reshape(down_weight.shape)
    layer_out = (hidden + RESIDUAL * mixed_out).astype(bf16)
    parts = latent_terms.reshape(model_count, group, share // group, latent_all)
    parts = lax.all_to_all(parts, "dp", 1, 0, axis_index_groups=near)
    parts = jnp.sum(parts.astype(jnp.float32), axis=0).astype(bf16)
    grad_both = jnp.concatenate(
        [
            dot_first(query_latent, grad_query_all)
            .astype(bf16)
            .reshape(data_count // group, group, query_rows, -1),
            dot_first(keyval_latent, grad_keyval)
            .astype(bf16)
            .reshape(data_count // group, group, keyval_rows, -1),
        ],
        axis=2,
    )
    gate_sum = jnp.transpose(gate_sum.reshape(2 * unit_count, data_count, -1), (1, 0, 2))
    parts, grad_both, gate_sum = tie(
        lax.all_to_all(parts, "mp", 0, 0, tiled=True), grad_both, gate_sum
    )
    gate_sum = lax.all_to_all(gate_sum, "dp", 0, 0, tiled=True)
    project_sum, gate_sum = tie(project_sum, gate_sum)
    gate_sum = jnp.transpose(
        gate_sum.reshape(data_count, 2, unit_count, -1), (3, 1, 0, 2)
    ).reshape(gateup_weight.shape)

    grad_both = far_sum(
        grad_both.reshape(data_count // group, group * (query_rows + keyval_rows), -1),
        group,
        data_count,
        data_index,
    )
    grad_latent_all = (
        to_owners(parts, group, near).reshape(micro * share, latent_all).astype(jnp.float32)
    )

    grad_query_up = grad_latent_all[:, :QUERY_RANK]
    grad_keyval_up = grad_latent_all[:, QUERY_RANK : QUERY_RANK + LATENT_RANK]
    grad_latent = jnp.concatenate(
        [
            rms_back(query_raw, inverse_query, gain_query, grad_query_up),
            rms_back(keyval_raw, inverse_keyval, gain_keyval, grad_keyval_up),
            grad_latent_all[:, QUERY_RANK + LATENT_RANK :],
        ],
        axis=1,
    ).astype(bf16)
    grad_gain_query = jnp.sum(grad_query_up * query_raw * inverse_query, axis=0)
    grad_gain_keyval = jnp.sum(grad_keyval_up * keyval_raw * inverse_keyval, axis=0)
    grad_normed = dot_last(grad_latent, lat_w)
    latent_sum = near_sum(dot_first(normed, grad_latent), group, data_count, data_index)
    input_grad = grad_hidden + rms_back(tok, inverse_one, gain_one, grad_normed)
    grad_gain_one = jnp.sum(grad_normed * tok * inverse_one, axis=0)
    grad_gains = jnp.concatenate(
        [grad_gain_one, grad_gain_two, grad_gain_query, grad_gain_keyval]
    )

    grad_both = lax.all_to_all(
        grad_both.astype(bf16).reshape(group, query_rows + keyval_rows, -1),
        "dp",
        0,
        1,
        axis_index_groups=near,
    )
    grad_both = scatter_columns(
        grad_both.reshape(query_rows + keyval_rows, -1), model_count
    )
    reduced = [
        scatter_columns(
            far_sum(latent_sum, group, data_count, data_index), model_count
        ),
        grad_both[:query_rows]
        .reshape(query_rows, own_heads, 128)[:, :, : NOPE_DIM + ROPE_DIM]
        .reshape(query_weight.shape),
        grad_both[query_rows:],
        scatter_columns(project_sum, model_count),
        gate_sum.astype(jnp.float32),
        down_sum.astype(jnp.float32),
    ]

    peak_row = lax.dynamic_update_slice(
        jnp.full((HEADS,), -1e30, jnp.float32), peak_own, (own_part * heads,)
    )
    small = jnp.concatenate(
        [
            grad_gains.reshape(data_count, -1),
            jnp.broadcast_to(peak_row[None], (data_count, HEADS)),
        ],
        axis=1,
    )
    small = lax.all_to_all(small, "dp", 0, 0, tiled=True)
    gain_count = gains.shape[0]
    small = jnp.concatenate(
        [jnp.sum(small[:, :gain_count], axis=0), jnp.max(small[:, gain_count:], axis=0)]
    )
    cells = ROTATE_ROWS * ROTATE_ROWS
    small = jnp.pad(small, (0, -(gain_count + HEADS) % cells)).reshape(-1, cells)
    grams = jnp.concatenate([gram_of(grad_w) for grad_w in reduced], axis=0)
    gram_count = grams.shape[0]
    packed = spread(
        jnp.concatenate([grams.reshape(gram_count, cells), small], axis=0), "mp", model_count
    )
    grams = jnp.sum(packed[:, :gram_count], axis=0).reshape(grams.shape)
    small = packed[:, gram_count:].reshape(model_count, -1)
    gains_grad = jnp.sum(small[:, :gain_count], axis=0)
    all_peaks = jnp.max(small[:, gain_count : gain_count + HEADS], axis=0)
    threshold = jnp.mean(all_peaks)
    clip_all = jnp.minimum(1.0, threshold / jnp.maximum(all_peaks, 1.0))
    clip_own = lax.dynamic_slice_in_dim(clip_all, model_index * own_heads, own_heads, 0)

    results = [
        layer_out.reshape(tokens.shape),
        input_grad.reshape(tokens.shape),
    ]
    new_stats = []
    start = 0
    for mat_index in range(6):
        stat_m = states[mat_index][2]
        gram_sum = grams[start : start + stat_m.shape[0]]
        start += stat_m.shape[0]
        new_stats.append(BETA_SECOND * stat_m + (1.0 - BETA_SECOND) * gram_sum)
    new_bases = renew_all(new_stats, [state[3] for state in states])
    for mat_index in range(6):
        first_m, second_m, stat_m, basis_m = states[mat_index]
        new_weight, new_first, new_second = rotated_update(
            matrices[mat_index],
            reduced[mat_index],
            first_m,
            second_m,
            basis_m,
            RATES[mat_index],
        )
        if mat_index == 1:
            new_weight = clip_columns(new_weight, clip_own, NOPE_DIM + ROPE_DIM, True)
        if mat_index == 2:
            new_weight = clip_columns(new_weight, clip_own, NOPE_DIM + VALUE_DIM, False)
        results.extend(
            [
                new_weight,
                new_weight.astype(jnp.bfloat16),
                new_first,
                new_second,
                new_stats[mat_index],
                new_bases[mat_index],
            ]
        )
    gains_first_new = BETA_FIRST * gains_first + (1.0 - BETA_FIRST) * gains_grad
    gains_second_new = BETA_SECOND * gains_second + (1.0 - BETA_SECOND) * gains_grad * gains_grad
    gains_step = (
        gains_first_new
        / (1.0 - BETA_FIRST**STEP_COUNT)
        / (jnp.sqrt(gains_second_new / (1.0 - BETA_SECOND**STEP_COUNT)) + ADAM_EPS)
    )
    results.extend(
        [gains - GAIN_RATE * (gains_step + DECAY * gains), gains_first_new, gains_second_new]
    )
    return tuple(results)


def solution(mesh):
    placed = (
        P(None, ("dp", "mp"), None),
        P(None, ("dp", "mp"), None),
        P(None, "dp", None),
        P("dp", "mp"),
        P("dp", "mp"),
        P("dp", "mp"),
        P("dp", None, None),
        P("dp", None, None),
        P("dp", "mp"),
        P("dp", "mp"),
        P("dp", "mp"),
        P("dp", None, None),
        P("dp", None, None),
        P("dp", "mp"),
        P("dp", "mp"),
        P("dp", "mp"),
        P("dp", None, None),
        P("dp", None, None),
        P("dp", "mp"),
        P("dp", "mp"),
        P("dp", "mp"),
        P("dp", None, None),
        P("dp", None, None),
        P("dp", None, "mp"),
        P("dp", None, "mp"),
        P("dp", None, "mp"),
        P("dp", None, None),
        P("dp", None, None),
        P("dp", "mp"),
        P("dp", "mp"),
        P("dp", "mp"),
        P("dp", None, None),
        P("dp", None, None),
        P("dp"),
        P("dp"),
        P("dp"),
    )
    return jax.shard_map(
        on_device,
        mesh=mesh,
        in_specs=placed,
        out_specs=(
            P(None, ("dp", "mp"), None),
            P(None, ("dp", "mp"), None),
            P("dp", "mp"),
            P("dp", "mp"),
            P("dp", "mp"),
            P("dp", "mp"),
            P("dp", None, None),
            P("dp", None, None),
            P("dp", "mp"),
            P("dp", "mp"),
            P("dp", "mp"),
            P("dp", "mp"),
            P("dp", None, None),
            P("dp", None, None),
            P("dp", "mp"),
            P("dp", "mp"),
            P("dp", "mp"),
            P("dp", "mp"),
            P("dp", None, None),
            P("dp", None, None),
            P("dp", "mp"),
            P("dp", "mp"),
            P("dp", "mp"),
            P("dp", "mp"),
            P("dp", None, None),
            P("dp", None, None),
            P("dp", None, "mp"),
            P("dp", None, "mp"),
            P("dp", None, "mp"),
            P("dp", None, "mp"),
            P("dp", None, None),
            P("dp", None, None),
            P("dp", "mp"),
            P("dp", "mp"),
            P("dp", "mp"),
            P("dp", "mp"),
            P("dp", None, None),
            P("dp", None, None),
            P("dp"),
            P("dp"),
            P("dp"),
        ),
        check_vma=False,
    )
```

```python
import functools
import math

import jax
import jax.numpy as jnp
from jax import lax
from jax.experimental import pallas as pl
from jax.experimental.layout import Layout, with_layout_constraint
from jax.experimental.pallas import tpu as pltpu
from jax.sharding import PartitionSpec as P

WIDTH = 2560
HEADS = 40
QUERY_RANK = 768
LATENT_RANK = 256
NOPE_DIM = 64
ROPE_DIM = 32
VALUE_DIM = 64
BLOCK = 128
ROTATE_ROWS = 16
STEP_COUNT = 10


HIGHEST = lax.Precision.HIGHEST
NORM_EPS = 1e-05
RESIDUAL = 1.4 / math.sqrt(62.0)
ROPE_BASE = 10000.0
BETA_FIRST = 0.95
BETA_SECOND = 0.95
ADAM_EPS = 1e-08
DECAY = 0.01
RATES = (0.08, 0.2, 0.25, 3.2, 0.08, 0.56)
GAIN_RATE = 0.8


def rms_parts(values, scale_gain):
    inverse = lax.rsqrt(jnp.mean(values * values, axis=-1, keepdims=True) + NORM_EPS)
    return (values * inverse * scale_gain, inverse)


def rms_back(values, inverse, scale_gain, upstream):
    weighted = upstream * scale_gain
    inner = jnp.mean(weighted * values, axis=-1, keepdims=True)
    return inverse * weighted - values * (inverse * inverse * inverse) * inner


def rotate(values, cosine, sine_part):
    half_dim = values.shape[-1] // 2
    first_half = values[..., :half_dim]
    second_half = values[..., half_dim:]
    return jnp.concatenate(
        [
            first_half * cosine - second_half * sine_part,
            second_half * cosine + first_half * sine_part,
        ],
        axis=-1,
    )


def rotate_back(grad_in, cosine, sine_part):
    half_dim = grad_in.shape[-1] // 2
    first_half = grad_in[..., :half_dim]
    second_half = grad_in[..., half_dim:]
    return jnp.concatenate(
        [
            first_half * cosine + second_half * sine_part,
            second_half * cosine - first_half * sine_part,
        ],
        axis=-1,
    )


def tree_layout(parent):
    block_count = parent.shape[0]
    identity = jnp.eye(block_count, dtype=jnp.float32)
    blocks = jnp.arange(block_count)
    parent_of = ((parent[:, None] == blocks[None, :]) & (blocks[:, None] > 0)).astype(jnp.float32)
    reached = identity
    for unused in range(block_count):
        reached = jnp.minimum(1.0, identity + jnp.dot(parent_of, reached, precision=HIGHEST))
    depths = jnp.sum(reached, axis=1) - 1.0
    length = block_count * BLOCK
    ancestor = (
        jnp.broadcast_to(
            reached[:, None, :, None], (block_count, BLOCK, block_count, BLOCK)
        ).reshape(length, length)
        > 0.5
    )
    tokens_at = jnp.arange(length)
    same_block = tokens_at[:, None] // BLOCK == tokens_at[None, :] // BLOCK
    visible = ancestor & (jnp.logical_not(same_block) | (tokens_at[None, :] <= tokens_at[:, None]))
    position = jnp.repeat(depths, BLOCK) * BLOCK + (tokens_at % BLOCK).astype(jnp.float32)
    frequency = ROPE_BASE ** (-(jnp.arange(ROPE_DIM // 2).astype(jnp.float32) * 2.0 / ROPE_DIM))
    angles = position[:, None] * frequency[None, :]
    return (visible, jnp.cos(angles), jnp.sin(angles))


def dot_first(first_arg, second_arg):
    return lax.dot_general(
        first_arg, second_arg, (((0,), (0,)), ((), ())), preferred_element_type=jnp.float32
    )


def dot_last(first_arg, second_arg):
    return lax.dot_general(
        first_arg, second_arg, (((1,), (1,)), ((), ())), preferred_element_type=jnp.float32
    )


def gram_of(grad_w):
    blocks = grad_w.reshape(grad_w.shape[0] // ROTATE_ROWS, ROTATE_ROWS, -1)
    return jnp.einsum("bic,bjc->bij", blocks, blocks, precision=HIGHEST)


def rotated_update(weight, grad_w, first_m, second_m, basis_m, step_rate):
    blocks = grad_w.reshape(basis_m.shape[0], basis_m.shape[1], -1)
    turned = jnp.einsum("bij,bic->bjc", basis_m, blocks, precision=HIGHEST).reshape(grad_w.shape)
    new_first = BETA_FIRST * first_m + (1.0 - BETA_FIRST) * turned
    new_second = BETA_SECOND * second_m + (1.0 - BETA_SECOND) * turned * turned
    normal_step = (
        new_first
        / (1.0 - BETA_FIRST**STEP_COUNT)
        / (jnp.sqrt(new_second / (1.0 - BETA_SECOND**STEP_COUNT)) + ADAM_EPS)
    )
    rotated_back = jnp.einsum(
        "bij,bjc->bic", basis_m, normal_step.reshape(blocks.shape), precision=HIGHEST
    ).reshape(grad_w.shape)
    new_weight = weight - step_rate * (rotated_back + DECAY * weight)
    return (new_weight, new_first, new_second)


def clip_columns(new_weight, clip_factor, head_width, rope_scaled):
    rows = new_weight.shape[0]
    root_factor = jnp.sqrt(clip_factor)
    tail_factor = clip_factor if rope_scaled else jnp.ones_like(clip_factor)
    column_scale = jnp.concatenate(
        [
            jnp.broadcast_to(root_factor[:, None], (clip_factor.shape[0], NOPE_DIM)),
            jnp.broadcast_to(tail_factor[:, None], (clip_factor.shape[0], head_width - NOPE_DIM)),
        ],
        axis=1,
    )
    return (
        new_weight.reshape(rows, clip_factor.shape[0], head_width) * column_scale[None]
    ).reshape(new_weight.shape)


def groups_of(data_count, group_size):
    near = [[start + i for i in range(group_size)] for start in range(0, data_count, group_size)]
    cross = [[i + start for start in range(0, data_count, group_size)] for i in range(group_size)]
    return near, cross


def near_parts(values, group_size, near):
    micro, count, width = values.shape
    parts = values.reshape(micro, group_size, count // group_size, width)
    parts = lax.all_to_all(parts, "dp", 1, 0, axis_index_groups=near)
    return parts.reshape(group_size * micro, count // group_size, width)


def to_trees(values, group_size, near):
    return lax.all_to_all(near_parts(values, group_size, near), "mp", 0, 0, tiled=True)


def to_owners(values, group_size, near):
    planes, count, width = values.shape
    parts = values.reshape(group_size, planes // group_size, count, width)
    parts = lax.all_to_all(parts, "dp", 0, 1, axis_index_groups=near)
    return parts.reshape(planes // group_size, group_size * count, width)


def spread(values, axis_name, count, groups=None):
    return lax.all_to_all(
        jnp.broadcast_to(values[None], (count,) + values.shape),
        axis_name,
        0,
        0,
        tiled=True,
        axis_index_groups=groups,
    )


def swap_bit(values, bit, data_count):
    return lax.ppermute(values, "dp", [(i, i ^ bit) for i in range(data_count)])


def bits_of(group_size, data_count):
    bits = []
    bit = group_size
    while bit < data_count:
        bits.append(bit)
        bit *= 2
    return bits


def gather_tokens(values, group_size, data_count):
    rows = values.shape[0] // 2
    bits = bits_of(group_size, data_count)
    pieces = {}
    for half in range(2):
        got = {0: values[half * rows : (half + 1) * rows]}
        for bit in bits if half == 0 else bits[::-1]:
            for index in sorted(got):
                got[index ^ bit] = swap_bit(got[index], bit, data_count)
        for index in sorted(got):
            pieces[(index, half)] = got[index]
            for near in range(1, group_size):
                pieces[(index ^ near, half)] = swap_bit(got[index], near, data_count)
    return pieces


def add_low(first_arg, second_arg):
    return (first_arg.astype(jnp.float32) + second_arg.astype(jnp.float32)).astype(jnp.bfloat16)


def scatter_tokens(pieces, group_size, data_count, near_count, fillers):
    bits = bits_of(group_size, data_count)
    fillers = list(fillers)
    held = [{}, {}]
    far = range(0, data_count, group_size)
    sent = {
        (index, half, near): swap_bit(pieces[(index ^ near, half)], near, data_count)
        for half in range(2)
        for index in far
        for near in range(1, near_count)
    }
    keys = sorted(sent)
    fillers[0], *arrived = tie(fillers[0], *[sent[key] for key in keys])
    sent = dict(zip(keys, arrived))
    for half in range(2):
        for index in far:
            total = pieces[(index, half)]
            for near in range(1, near_count):
                total = add_low(total, sent[(index, half, near)])
            held[half][index] = total
    for step in range(len(bits)):
        sent = {}
        for half in range(2):
            bit = bits[step] if half == 0 else bits[::-1][step]
            for index in held[half]:
                if not index & bit:
                    sent[(index, half)] = swap_bit(held[half][index ^ bit], bit, data_count)
        keys = sorted(sent)
        if step + 1 < len(fillers):
            fillers[step + 1], *arrived = tie(fillers[step + 1], *[sent[key] for key in keys])
            sent = dict(zip(keys, arrived))
        held = [
            {
                index: add_low(held[half][index], sent[(index, half)])
                for index in held[half]
                if (index, half) in sent
            }
            for half in range(2)
        ]
    return jnp.concatenate([held[half][0] for half in range(2)], axis=0), fillers


def spread_planes(values, model_count, model_index):
    out = jnp.zeros((model_count,) + values.shape, values.dtype)
    for shift in range(model_count):
        part = values
        if shift:
            part = lax.ppermute(
                values, "mp", [(i, (i + shift) % model_count) for i in range(model_count)]
            )
        place = (model_index + model_count - shift) % model_count
        out = lax.dynamic_update_slice(out, part[None], (place,) + (0,) * values.ndim)
    return out


def row_major(values):
    return with_layout_constraint(values, Layout(major_to_minor=tuple(range(values.ndim))))


def far_parts(block, group_size, data_count):
    return [block] + [
        swap_bit(block, far, data_count) for far in range(group_size, data_count, group_size)
    ]


def in_order(parts, own):
    out = jnp.zeros((len(parts),) + parts[0].shape, parts[0].dtype)
    for index, part in enumerate(parts):
        out = lax.dynamic_update_slice(out, part[None], (own ^ index,) + (0,) * part.ndim)
    return row_major(out)


def rows_of(parts, group_size, data_count, data_index):
    far = in_order(parts, data_index // group_size)
    own = data_index % group_size
    out = jnp.zeros((len(parts), group_size) + parts[0].shape, far.dtype)
    for near in range(group_size):
        part = far if near == 0 else swap_bit(far, near, data_count)
        out = lax.dynamic_update_slice(out, part[:, None], (0, own ^ near, 0, 0))
    return out.reshape((data_count * parts[0].shape[0],) + parts[0].shape[1:])


def blocks_of(parts, group_size, data_count):
    blocks = []
    for part in parts:
        blocks.append(part)
        for near in range(1, group_size):
            blocks.append(swap_bit(part, near, data_count))
    return jnp.concatenate(blocks, axis=0)


def scatter_blocks(values, group_size, data_count):
    parts = values.reshape(data_count // group_size, group_size, -1, values.shape[-1])
    total = parts[:, 0].astype(jnp.float32)
    for near in range(1, group_size):
        total = total + swap_bit(parts[:, near], near, data_count).astype(jnp.float32)
    total = total.astype(jnp.bfloat16)
    result = total[0].astype(jnp.float32)
    for far in range(1, data_count // group_size):
        result = result + swap_bit(total[far], far * group_size, data_count).astype(jnp.float32)
    return result


def tie(*values):
    return lax.optimization_barrier(values)


def far_shares(parts, group_size, data_count, data_index):
    own = data_index // group_size
    shares = []
    for far in range(data_count // group_size):
        part = lax.dynamic_index_in_dim(parts, own ^ far, 0, keepdims=False)
        shares.append(swap_bit(part, far * group_size, data_count) if far else part)
    return shares


def sum_of(shares):
    return sum((share.astype(jnp.float32) for share in shares[1:]), shares[0].astype(jnp.float32))


def far_sum(parts, group_size, data_count, data_index):
    return sum_of(far_shares(parts, group_size, data_count, data_index))


def near_sum(grad_w, group_size, data_count, data_index):
    own = data_index % group_size
    parts = grad_w.astype(jnp.bfloat16).reshape(
        data_count // group_size, group_size, -1, grad_w.shape[-1]
    )

    def part_of(near):
        return lax.dynamic_index_in_dim(parts, own ^ near, 1, keepdims=False)

    total = part_of(0).astype(jnp.float32)
    for near in range(1, group_size):
        total = total + swap_bit(part_of(near), near, data_count).astype(jnp.float32)
    return total.astype(jnp.bfloat16)


def scatter_columns(grad_w, model_count):
    rows, width = grad_w.shape
    parts = grad_w.astype(jnp.bfloat16).reshape(rows, model_count, width // model_count)
    parts = lax.all_to_all(jnp.swapaxes(parts, 0, 1), "mp", 0, 0, tiled=True)
    return jnp.sum(parts.astype(jnp.float32), axis=0)


def basis_kernel(stat_ref, basis_ref, out_ref):
    size = stat_ref.shape[0]
    columns = jnp.zeros(stat_ref.shape, jnp.float32)
    for j in range(size):
        columns = columns + basis_ref[j][:, None, :] * stat_ref[j][None, :, :]
    for j in range(size):
        column = columns[j]
        norm = jnp.sum(column * column, axis=0, keepdims=True)
        column = column * lax.rsqrt(norm)
        out_ref[j] = column
        shares = jnp.sum(columns * column[None], axis=1, keepdims=True)
        columns = columns - shares * column[None]


def renew_all(stats, bases):
    counts = [stat_m.shape[0] for stat_m in stats]
    total = sum(counts)
    padded = -(-total // 128) * 128
    stat_t = jnp.concatenate([jnp.transpose(s, (2, 1, 0)) for s in stats], axis=2)
    basis_t = jnp.concatenate([jnp.transpose(b, (1, 2, 0)) for b in bases], axis=2)
    pad = ((0, 0), (0, 0), (0, padded - total))
    stat_t = jnp.pad(stat_t, pad, constant_values=1.0)
    basis_t = jnp.pad(basis_t, pad, constant_values=1.0)
    out = pl.pallas_call(
        basis_kernel,
        out_shape=jax.ShapeDtypeStruct((ROTATE_ROWS, ROTATE_ROWS, padded), jnp.float32),
    )(stat_t, basis_t)
    results = []
    start = 0
    for count in counts:
        results.append(jnp.transpose(out[:, :, start : start + count], (2, 1, 0)))
        start += count
    return results


LOG2E = 1.4426950408889634


def exp_rows(query, keys, bias, scale):
    scores = lax.dot_general(
        query, keys, (((1,), (1,)), ((), ())), preferred_element_type=jnp.float32
    )
    scores = scores * (scale * LOG2E) + bias
    top = jnp.max(scores, axis=-1, keepdims=True)
    raised = jnp.exp2(scores - top)
    return raised, top, 1.0 / jnp.sum(raised, axis=-1, keepdims=True)


def attend_kernel(
    scale,
    rows,
    query_latent_ref,
    keyval_latent_ref,
    query_w_ref,
    keyval_w_ref,
    key_ref,
    bias_ref,
    cos_ref,
    left_ref,
    right_ref,
    out_ref,
    query_ref,
    keyval_ref,
    peak_ref,
):
    bf16 = jnp.bfloat16
    length = key_ref.shape[0]
    raw = jnp.dot(query_latent_ref[...], query_w_ref[...], preferred_element_type=jnp.float32)
    both = jnp.dot(keyval_latent_ref[...], keyval_w_ref[...], preferred_element_type=jnp.float32)
    keyval_ref[...] = both.astype(bf16)
    lane = lax.broadcasted_iota(jnp.int32, (1, 128), 1)
    for head in range(2):
        at = slice(head * 128, head * 128 + 128)
        part = raw[:, at]
        query_ref[:, at] = (
            part * cos_ref[...]
            + pltpu.roll(part, 128 - ROPE_DIM // 2, 1) * left_ref[...]
            + pltpu.roll(part, ROPE_DIM // 2, 1) * right_ref[...]
        ).astype(bf16)
    for first in range(0, length, rows):
        last = first + rows
        outs = []
        for head in range(2):
            at = slice(head * 128, head * 128 + 128)
            keyval = keyval_ref[:last, at]
            keys = jnp.where(lane < NOPE_DIM, keyval, key_ref[:last, :])
            raised, top, inverse = exp_rows(
                query_ref[first:last, at], keys, bias_ref[first:last, :last], scale
            )
            outs.append(
                jnp.dot(raised.astype(bf16), keyval, preferred_element_type=jnp.float32) * inverse
            )
            tops = jnp.max(top) * (1.0 / LOG2E)
            spot = slice(head * 8, head * 8 + 8)
            if first == 0:
                peak_ref[0, spot, :] = jnp.full((8, 128), tops, jnp.float32)
            else:
                peak_ref[0, spot, :] = jnp.maximum(peak_ref[0, spot, :], tops)
        out_ref[first:last, :] = jnp.where(
            lane < VALUE_DIM, pltpu.roll(outs[0], VALUE_DIM, 1), outs[1]
        ).astype(bf16)


def attend_back_kernel(
    scale,
    rows,
    query_ref,
    keyval_ref,
    grad_ref,
    key_ref,
    bias_ref,
    cos_ref,
    left_ref,
    right_ref,
    query_out_ref,
    keyval_out_ref,
    shared_out_ref,
    pair_ref,
    total_ref,
):
    bf16 = jnp.bfloat16
    length = key_ref.shape[0]
    lane = lax.broadcasted_iota(jnp.int32, (1, 128), 1)
    low_lanes = lane < NOPE_DIM

    @pl.when(pl.program_id(0) == 0)
    def clear():
        total_ref[...] = jnp.zeros_like(total_ref)

    for head in range(2):
        at = slice(head * 128, head * 128 + 128)
        pair_ref[...] = jnp.zeros_like(pair_ref)
        for first in range(0, length, rows):
            last = first + rows
            keyval = keyval_ref[:last, at]
            keys = jnp.where(low_lanes, keyval, key_ref[:last, :])
            query = query_ref[first:last, at]
            grad = grad_ref[first:last, :].astype(jnp.float32)
            if head == 0:
                grad = pltpu.roll(grad, VALUE_DIM, 1)
            grad = jnp.where(low_lanes, 0.0, grad).astype(bf16)
            raised, _, inverse = exp_rows(query, keys, bias_ref[first:last, :last], scale)
            probs = raised * inverse
            grad_probs = lax.dot_general(
                grad, keyval, (((1,), (1,)), ((), ())), preferred_element_type=jnp.float32
            )
            inner = jnp.sum(probs * grad_probs, axis=-1, keepdims=True)
            grad_scores = (probs * (grad_probs - inner)).astype(bf16)
            part = jnp.dot(grad_scores, keys, preferred_element_type=jnp.float32) * scale
            query_out_ref[first:last, at] = (
                part * cos_ref[first:last, :]
                - pltpu.roll(part, 128 - ROPE_DIM // 2, 1) * left_ref[first:last, :]
                - pltpu.roll(part, ROPE_DIM // 2, 1) * right_ref[first:last, :]
            ).astype(bf16)
            zero = jnp.zeros_like(query)
            left = jnp.concatenate([grad_scores, probs.astype(bf16)], axis=0)
            right = jnp.concatenate(
                [
                    jnp.concatenate(
                        [jnp.where(low_lanes, query, zero), jnp.where(low_lanes, zero, query)],
                        axis=1,
                    ),
                    jnp.concatenate([grad, zero], axis=1),
                ],
                axis=0,
            )
            both = lax.dot_general(
                left, right, (((0,), (0,)), ((), ())), preferred_element_type=jnp.float32
            )
            pair_ref[:last, :] += both[:, :128]
            total_ref[:last, :] += both[:, 128:]
        keyval_out_ref[:, at] = (pair_ref[...] * jnp.where(low_lanes, scale, 1.0)).astype(bf16)

    @pl.when(pl.program_id(0) == pl.num_programs(0) - 1)
    def finish():
        shared_out_ref[...] = total_ref[...] * scale


def attend_cost(length, steps, products):
    return pl.CostEstimate(
        flops=int(products * 2 * steps * 2 * length * length * 256),
        bytes_accessed=steps * length * 256 * 8,
        transcendentals=steps * 2 * length * length,
    )


def resident(shape):
    return pl.BlockSpec(shape, lambda step: (0,) * len(shape))


def attend(query_latent, keyval_latent, query_w, keyval_w, key_lanes, bias, tables, scale, rows):
    length = bias.shape[0]
    steps = query_w.shape[1] // 256
    wide = jax.ShapeDtypeStruct((length, steps * 256), jnp.bfloat16)
    column = lambda width: pl.BlockSpec((length, width), lambda step: (0, step))
    return pl.pallas_call(
        functools.partial(attend_kernel, scale, rows),
        grid=(steps,),
        in_specs=[
            resident(query_latent.shape),
            resident(keyval_latent.shape),
            pl.BlockSpec((query_w.shape[0], 256), lambda step: (0, step)),
            pl.BlockSpec((keyval_w.shape[0], 256), lambda step: (0, step)),
            resident(key_lanes.shape),
            resident(bias.shape),
        ]
        + [resident(table.shape) for table in tables],
        out_specs=[
            column(128),
            column(256),
            column(256),
            pl.BlockSpec((1, 16, 128), lambda step: (step, 0, 0)),
        ],
        out_shape=[
            jax.ShapeDtypeStruct((length, steps * 128), jnp.bfloat16),
            wide,
            wide,
            jax.ShapeDtypeStruct((steps, 16, 128), jnp.float32),
        ],
        compiler_params=pltpu.CompilerParams(vmem_limit_bytes=56 * 1024 * 1024),
        cost_estimate=attend_cost(length, steps, 2.0),
    )(query_latent, keyval_latent, query_w, keyval_w, key_lanes, bias, *tables)


def attend_back(queries, keyval, grad, key_lanes, bias, tables, scale, rows):
    length = bias.shape[0]
    steps = queries.shape[1] // 256
    wide = jax.ShapeDtypeStruct(queries.shape, jnp.bfloat16)
    column = lambda width: pl.BlockSpec((length, width), lambda step: (0, step))
    return pl.pallas_call(
        functools.partial(attend_back_kernel, scale, rows),
        grid=(steps,),
        in_specs=[
            column(256),
            column(256),
            column(128),
            resident(key_lanes.shape),
            resident(bias.shape),
        ]
        + [resident(table.shape) for table in tables],
        out_specs=[column(256), column(256), resident((length, 128))],
        out_shape=[wide, wide, jax.ShapeDtypeStruct((length, 128), jnp.float32)],
        scratch_shapes=[
            pltpu.VMEM((length, 128), jnp.float32),
            pltpu.VMEM((length, 128), jnp.float32),
        ],
        compiler_params=pltpu.CompilerParams(vmem_limit_bytes=56 * 1024 * 1024),
        cost_estimate=attend_cost(length, steps, 4.0),
    )(queries, keyval, grad, key_lanes, bias, *tables)


def on_device(
    tokens,
    cotangent,
    parents,
    latent_weight,
    latent_first,
    latent_second,
    latent_stat,
    latent_basis,
    query_weight,
    query_first,
    query_second,
    query_stat,
    query_basis,
    keyval_weight,
    keyval_first,
    keyval_second,
    keyval_stat,
    keyval_basis,
    project_weight,
    project_first,
    project_second,
    project_stat,
    project_basis,
    gateup_weight,
    gateup_first,
    gateup_second,
    gateup_stat,
    gateup_basis,
    down_weight,
    down_first,
    down_second,
    down_stat,
    down_basis,
    gains,
    gains_first,
    gains_second,
):
    matrices = (
        latent_weight,
        query_weight,
        keyval_weight,
        project_weight,
        gateup_weight,
        down_weight,
    )
    states = (
        (latent_first, latent_second, latent_stat, latent_basis),
        (query_first, query_second, query_stat, query_basis),
        (keyval_first, keyval_second, keyval_stat, keyval_basis),
        (project_first, project_second, project_stat, project_basis),
        (gateup_first, gateup_second, gateup_stat, gateup_basis),
        (down_first, down_second, down_stat, down_basis),
    )
    bf16 = jnp.bfloat16
    data_count = lax.axis_size("dp")
    model_count = lax.axis_size("mp")
    micro, share, _ = tokens.shape
    group = model_count // micro
    near, cross = groups_of(data_count, group)
    data_index = lax.axis_index("dp")
    model_index = lax.axis_index("mp")
    own_part = data_index % group
    length = share * model_count
    heads = HEADS // group
    scale_attn = float(NOPE_DIM + ROPE_DIM) ** (-0.5)
    rows_attn = min(512, length)
    own_heads = query_weight.shape[1] // (NOPE_DIM + ROPE_DIM)
    latent_all = latent_weight.shape[1] * model_count

    def columns(far):
        return jnp.swapaxes(far, 0, 1).reshape(far.shape[1], -1)

    def exchange_units(values):
        return lax.all_to_all(values, "dp", 0, 0, tiled=True)

    query_rows = query_weight.shape[0]
    keyval_rows = keyval_weight.shape[0]
    unit_count = down_weight.shape[1] // data_count
    hidden_units = unit_count * model_count
    padded = -(-hidden_units // 128) * 128
    gain_all = spread(gains.astype(bf16), "dp", data_count)
    output_w = lax.all_gather(project_weight.astype(bf16), "mp", axis=0)
    lat_w = spread_planes(row_major(latent_weight.astype(bf16)), model_count, model_index)
    query_pad = jnp.pad(
        query_weight.astype(bf16).reshape(query_rows, own_heads, NOPE_DIM + ROPE_DIM),
        ((0, 0), (0, 0), (0, 128 - NOPE_DIM - ROPE_DIM)),
    ).reshape(query_rows, own_heads * 128)
    both_w = jnp.concatenate([query_pad, keyval_weight.astype(bf16)], axis=0)
    both_w, lat_w = tie(row_major(both_w), lat_w)
    both_w = spread_planes(both_w, model_count, model_index)
    units = jnp.concatenate(
        [
            jnp.transpose(
                gateup_weight.astype(bf16).reshape(-1, 2, data_count, unit_count), (2, 1, 3, 0)
            ),
            jnp.transpose(
                down_weight.astype(bf16).reshape(-1, 1, data_count, unit_count), (2, 1, 3, 0)
            ),
        ],
        axis=1,
    )
    units = exchange_units(units)
    lat_w = far_parts(row_major(columns(lat_w)), group, data_count)
    both_w, units, *lat_w = tie(columns(both_w), units, *lat_w)
    both_w = both_w.reshape(query_rows + keyval_rows, group, -1)
    both_w = lax.all_to_all(both_w, "dp", 1, 0, axis_index_groups=near)
    both_parts = far_parts(row_major(both_w), group, data_count)
    lat_w = rows_of(lat_w, group, data_count, data_index)
    gain_all = gain_all.reshape(-1).astype(jnp.float32)
    gain_one = gain_all[:WIDTH]
    gain_two = gain_all[WIDTH : 2 * WIDTH]
    gain_query = gain_all[2 * WIDTH : 2 * WIDTH + QUERY_RANK]
    gain_keyval = gain_all[2 * WIDTH + QUERY_RANK :]

    tok = tokens.reshape(micro * share, WIDTH).astype(jnp.float32)
    normed, inverse_one = rms_parts(tok, gain_one)
    normed = normed.astype(bf16)
    latent = jnp.dot(normed, lat_w, preferred_element_type=jnp.float32).astype(bf16)
    latent = latent.astype(jnp.float32)
    query_raw = latent[:, :QUERY_RANK]
    keyval_raw = latent[:, QUERY_RANK : QUERY_RANK + LATENT_RANK]
    key_rope = latent[:, QUERY_RANK + LATENT_RANK :]
    query_normed, inverse_query = rms_parts(query_raw, gain_query)
    keyval_normed, inverse_keyval = rms_parts(keyval_raw, gain_keyval)
    sent = jnp.concatenate([query_normed, keyval_normed, key_rope], axis=1).astype(bf16)

    mid = near_parts(sent.reshape(micro, share, latent_all), group, near)
    mid = lax.all_to_all(mid, "mp", 0, 0, tiled=True)
    mid, *both_parts = tie(mid, *both_parts)
    both_w = in_order(both_parts, data_index // group)
    units = jnp.transpose(units, (1, 2, 0, 3)).reshape(3, unit_count, WIDTH)
    gate_first = lax.all_gather(units[0], "mp", axis=0)
    gate_pad = jnp.zeros((padded - hidden_units, WIDTH), bf16)
    tree = spread(mid, "dp", group, near)
    tree, both_w, output_w = tie(tree, both_w, output_w)
    tree, gate_first = tie(tree, gate_first)
    query_w = both_w[:, :, :query_rows].reshape(data_count * query_rows, -1)
    keyval_w = both_w[:, :, query_rows:].reshape(data_count * keyval_rows, -1)
    gate_halves = [gate_first, lax.all_gather(units[1], "mp", axis=0)]
    output_parts = far_parts(row_major(columns(output_w)), group, data_count)
    tree = jnp.swapaxes(tree, 0, 1).reshape(length, latent_all)
    tree_parents = jnp.zeros((group, micro, parents.shape[2]), parents.dtype)
    own_parents, normed = tie(parents[:, 0], normed)
    for place in range(group):
        part = own_parents if place == 0 else swap_bit(own_parents, place, data_count)
        tree_parents = lax.dynamic_update_slice(
            tree_parents, part[None], (own_part ^ place, 0, 0)
        )
    tree_parents = tree_parents.reshape(group * micro, -1)
    visible, cosine, sine_part = tree_layout(
        lax.dynamic_index_in_dim(tree_parents, model_index, 0, keepdims=False)
    )
    query_latent = tree[:, :QUERY_RANK]
    keyval_latent = tree[:, QUERY_RANK : QUERY_RANK + LATENT_RANK]
    shared = rotate(
        tree[:, QUERY_RANK + LATENT_RANK :].astype(jnp.float32), cosine, sine_part
    )
    key_lanes = jnp.pad(shared, ((0, 0), (NOPE_DIM, 128 - NOPE_DIM - ROPE_DIM))).astype(bf16)
    bias = jnp.where(visible, 0.0, -1e30).astype(jnp.float32)
    half_rope = ROPE_DIM // 2
    tail_lanes = 128 - NOPE_DIM - ROPE_DIM
    tables = (
        jnp.concatenate(
            [jnp.ones((length, NOPE_DIM)), cosine, cosine, jnp.zeros((length, tail_lanes))], axis=1
        ).astype(jnp.float32),
        jnp.pad(-sine_part, ((0, 0), (NOPE_DIM, half_rope + tail_lanes))),
        jnp.pad(sine_part, ((0, 0), (NOPE_DIM + half_rope, tail_lanes))),
    )
    attended, queries, keyval, peaks = attend(
        query_latent, keyval_latent, query_w, keyval_w, key_lanes, bias, tables, scale_attn, rows_attn
    )
    peak_own = peaks.reshape(heads, 8, 128)[:, 0, 0]

    def heads_near(values):
        parts = values.reshape(model_count, group, share // group, -1)
        parts = lax.all_to_all(parts, "dp", 1, 2, axis_index_groups=near)
        return parts.reshape(model_count, share // group, -1)

    def heads_in(values):
        parts = values.reshape(model_count, share // group, group, -1)
        parts = lax.all_to_all(parts, "dp", 2, 1, axis_index_groups=near)
        return parts.reshape(length, -1)

    grad_out = cotangent.reshape(micro * share, WIDTH).astype(jnp.float32)
    mixed_own, attended = tie((RESIDUAL * grad_out).astype(bf16), attended)
    mixed_parts = [mixed_own] + [
        swap_bit(mixed_own, bit, data_count) for bit in bits_of(group, data_count)
    ]
    attended, gate_halves[1] = tie(attended, gate_halves[1])
    attended, *output_parts = tie(heads_near(attended), *output_parts)
    middle = attended.shape[1] // 2
    early = lax.all_to_all(attended[:, :middle], "mp", 0, 0, tiled=True)
    late, early, *output_parts = tie(attended[:, middle:], early, *output_parts)
    late = lax.all_to_all(late, "mp", 0, 0, tiled=True)
    output_w = rows_of(output_parts, group, data_count, data_index)
    attended = jnp.concatenate([early, late], axis=1)
    down_t, attended = tie(units[2], attended)
    down_t = lax.all_gather(down_t, "mp", axis=0).reshape(hidden_units, WIDTH)
    attended_own = to_owners(attended, group, near).reshape(micro * share, -1)
    attended_own, *mixed_parts = tie(attended_own, *mixed_parts)
    branch = dot_last(attended_own, output_w)
    hidden = tok + RESIDUAL * branch
    normed_two, inverse_two = rms_parts(hidden, gain_two)
    normed_two = normed_two.astype(bf16)

    far_count = data_count // group
    half_rows = micro * share // 2
    order = [
        [(far * group + place, half) for place in range(group) for half in range(2)]
        for far in range(far_count)
    ]

    def joined(values):
        pieces = gather_tokens(values, group, data_count)
        return jnp.concatenate([pieces[key] for keys in order for key in keys], axis=0)

    def parted(values, fillers):
        pieces = {}
        for at, key in enumerate([key for keys in order for key in keys]):
            pieces[key] = values[at * half_rows : (at + 1) * half_rows]
        return scatter_tokens(pieces, group, data_count, group, fillers)

    down_t = jnp.concatenate([down_t, gate_pad], axis=0)
    normed_full, *mixed_parts = tie(joined(normed_two), *mixed_parts)
    sent_far = [0] + [bit // group for bit in bits_of(group, data_count)]
    mixed_parts = [
        mixed_parts[sent_far.index(far)]
        if far in sent_far
        else swap_bit(mixed_parts[0], far * group, data_count)
        for far in range(far_count)
    ]
    mixed_full = blocks_of(mixed_parts, group, data_count)
    gate_t = jnp.concatenate(
        [
            gate_halves[0].reshape(hidden_units, WIDTH),
            gate_pad,
            gate_halves[1].reshape(hidden_units, WIDTH),
            gate_pad,
        ],
        axis=0,
    )
    gateup = dot_last(normed_full, gate_t)
    gate_part = gateup[:, :padded]
    up_part = gateup[:, padded:]
    grad_act = dot_last(mixed_full, down_t)
    sigmoid_gate = jax.nn.sigmoid(gate_part)
    silu_gate = gate_part * sigmoid_gate
    activated = (silu_gate * up_part).astype(bf16)
    grad_gate = grad_act * up_part * sigmoid_gate * (1.0 + gate_part * (1.0 - sigmoid_gate))
    grad_up = grad_act * silu_gate
    grad_gateup = jnp.concatenate([grad_gate, grad_up], axis=1).astype(bf16)
    grad_normed_two, (grad_down_t, grad_gate_t) = parted(
        jnp.dot(grad_gateup, gate_t, preferred_element_type=jnp.float32).astype(bf16),
        [
            dot_first(activated, mixed_full).astype(bf16),
            dot_first(grad_gateup, normed_full).astype(bf16),
        ],
    )
    grad_normed_two = grad_normed_two.astype(jnp.float32)
    grad_down_t = grad_down_t[:hidden_units]

    down_sum = lax.psum_scatter(
        grad_down_t.reshape(model_count, unit_count, WIDTH), "mp", scatter_dimension=0, tiled=True
    )

    grad_hidden = grad_out + rms_back(hidden, inverse_two, gain_two, grad_normed_two)
    grad_gain_two = jnp.sum(grad_normed_two * hidden * inverse_two, axis=0)
    grad_branch = (RESIDUAL * grad_hidden).astype(bf16)
    gate_sum = grad_gate_t.reshape(2, padded, WIDTH)[:, :hidden_units]
    gate_sum = jnp.transpose(
        gate_sum.reshape(2, model_count, unit_count, WIDTH), (1, 0, 2, 3)
    ).reshape(model_count, 2 * unit_count, WIDTH)
    grad_attended = jnp.dot(grad_branch, output_w, preferred_element_type=jnp.float32)
    grad_attended, grad_branch = tie(
        near_parts(grad_attended.astype(bf16).reshape(micro, share, -1), group, near), grad_branch
    )
    tail = grad_attended.shape[1] // 2
    early = lax.all_to_all(grad_attended[:, :tail], "mp", 0, 0, tiled=True)
    project_sum = near_sum(
        dot_first(grad_branch, attended_own), group, data_count, data_index
    )
    activated = in_order(list(activated.reshape(data_count, -1, padded)), data_index)
    late, early, activated, project_sum = tie(
        grad_attended[:, tail:], early, activated, project_sum
    )
    late = lax.all_to_all(late, "mp", 0, 0, tiled=True)
    mixed_out = jnp.dot(
        activated.reshape(-1, padded), down_t, preferred_element_type=jnp.float32
    ).astype(bf16)
    mixed_out = lax.psum_scatter(
        mixed_out.reshape(data_count, -1, WIDTH), "dp", scatter_dimension=0, tiled=True
    ).reshape(hidden.shape)
    grad_attended, gate_sum = tie(
        heads_in(jnp.concatenate([early, late], axis=1)), gate_sum
    )
    gate_sum = lax.psum_scatter(gate_sum, "mp", scatter_dimension=0, tiled=True)
    project_shares = far_shares(project_sum, group, data_count, data_index)
    grad_query_all, grad_keyval, grad_shared = attend_back(
        queries, keyval, grad_attended, key_lanes, bias, tables, scale_attn, rows_attn
    )
    grad_query_all, *project_shares = tie(grad_query_all, *project_shares)
    project_sum = sum_of(project_shares)
    grad_shared = rotate_back(
        grad_shared[:, NOPE_DIM : NOPE_DIM + ROPE_DIM], cosine, sine_part
    )
    latent_terms = jnp.concatenate(
        [dot_last(grad_query_all, query_w), dot_last(grad_keyval, keyval_w), grad_shared], axis=1
    ).astype(bf16)
    down_sum = jnp.transpose(down_sum.reshape(unit_count, data_count, -1), (1, 0, 2))
    down_sum = lax.all_to_all(down_sum, "dp", 0, 0, tiled=True)
    latent_terms, project_sum, down_sum = tie(latent_terms, project_sum, down_sum)
    down_sum = jnp.transpose(down_sum, (2, 0, 1)).reshape(down_weight.shape)
    layer_out = (hidden + RESIDUAL * mixed_out).astype(bf16)
    parts = latent_terms.reshape(model_count, group, share // group, latent_all)
    parts = lax.all_to_all(parts, "dp", 1, 0, axis_index_groups=near)
    parts = jnp.sum(parts.astype(jnp.float32), axis=0).astype(bf16)
    grad_both = jnp.concatenate(
        [
            dot_first(query_latent, grad_query_all)
            .astype(bf16)
            .reshape(data_count // group, group, query_rows, -1),
            dot_first(keyval_latent, grad_keyval)
            .astype(bf16)
            .reshape(data_count // group, group, keyval_rows, -1),
        ],
        axis=2,
    )
    gate_sum = jnp.transpose(gate_sum.reshape(2 * unit_count, data_count, -1), (1, 0, 2))
    parts, grad_both = tie(lax.all_to_all(parts, "mp", 0, 0, tiled=True), grad_both)
    gate_sum = lax.all_to_all(gate_sum, "dp", 0, 0, tiled=True)
    gate_sum = jnp.transpose(
        gate_sum.reshape(data_count, 2, unit_count, -1), (3, 1, 0, 2)
    ).reshape(gateup_weight.shape)

    grad_both = far_sum(
        grad_both.reshape(data_count // group, group * (query_rows + keyval_rows), -1),
        group,
        data_count,
        data_index,
    )
    grad_latent_all = (
        to_owners(parts, group, near).reshape(micro * share, latent_all).astype(jnp.float32)
    )

    grad_query_up = grad_latent_all[:, :QUERY_RANK]
    grad_keyval_up = grad_latent_all[:, QUERY_RANK : QUERY_RANK + LATENT_RANK]
    grad_latent = jnp.concatenate(
        [
            rms_back(query_raw, inverse_query, gain_query, grad_query_up),
            rms_back(keyval_raw, inverse_keyval, gain_keyval, grad_keyval_up),
            grad_latent_all[:, QUERY_RANK + LATENT_RANK :],
        ],
        axis=1,
    ).astype(bf16)
    grad_gain_query = jnp.sum(grad_query_up * query_raw * inverse_query, axis=0)
    grad_gain_keyval = jnp.sum(grad_keyval_up * keyval_raw * inverse_keyval, axis=0)
    grad_normed = dot_last(grad_latent, lat_w)
    latent_sum = near_sum(dot_first(normed, grad_latent), group, data_count, data_index)
    input_grad = grad_hidden + rms_back(tok, inverse_one, gain_one, grad_normed)
    grad_gain_one = jnp.sum(grad_normed * tok * inverse_one, axis=0)
    grad_gains = jnp.concatenate(
        [grad_gain_one, grad_gain_two, grad_gain_query, grad_gain_keyval]
    )

    grad_both = lax.all_to_all(
        grad_both.astype(bf16).reshape(group, query_rows + keyval_rows, -1),
        "dp",
        0,
        1,
        axis_index_groups=near,
    )
    grad_both = scatter_columns(
        grad_both.reshape(query_rows + keyval_rows, -1), model_count
    )
    reduced = [
        scatter_columns(
            far_sum(latent_sum, group, data_count, data_index), model_count
        ),
        grad_both[:query_rows]
        .reshape(query_rows, own_heads, 128)[:, :, : NOPE_DIM + ROPE_DIM]
        .reshape(query_weight.shape),
        grad_both[query_rows:],
        scatter_columns(project_sum, model_count),
        gate_sum.astype(jnp.float32),
        down_sum.astype(jnp.float32),
    ]

    peak_row = lax.dynamic_update_slice(
        jnp.full((HEADS,), -1e30, jnp.float32), peak_own, (own_part * heads,)
    )
    small = jnp.concatenate(
        [
            grad_gains.reshape(data_count, -1),
            jnp.broadcast_to(peak_row[None], (data_count, HEADS)),
        ],
        axis=1,
    )
    small = lax.all_to_all(small, "dp", 0, 0, tiled=True)
    gain_count = gains.shape[0]
    small = jnp.concatenate(
        [jnp.sum(small[:, :gain_count], axis=0), jnp.max(small[:, gain_count:], axis=0)]
    )
    cells = ROTATE_ROWS * ROTATE_ROWS
    small = jnp.pad(small, (0, -(gain_count + HEADS) % cells)).reshape(-1, cells)
    grams = jnp.concatenate([gram_of(grad_w) for grad_w in reduced], axis=0)
    gram_count = grams.shape[0]
    packed = spread(
        jnp.concatenate([grams.reshape(gram_count, cells), small], axis=0), "mp", model_count
    )
    grams = jnp.sum(packed[:, :gram_count], axis=0).reshape(grams.shape)
    small = packed[:, gram_count:].reshape(model_count, -1)
    gains_grad = jnp.sum(small[:, :gain_count], axis=0)
    all_peaks = jnp.max(small[:, gain_count : gain_count + HEADS], axis=0)
    threshold = jnp.mean(all_peaks)
    clip_all = jnp.minimum(1.0, threshold / jnp.maximum(all_peaks, 1.0))
    clip_own = lax.dynamic_slice_in_dim(clip_all, model_index * own_heads, own_heads, 0)

    results = [
        layer_out.reshape(tokens.shape),
        input_grad.reshape(tokens.shape),
    ]
    new_stats = []
    start = 0
    for mat_index in range(6):
        stat_m = states[mat_index][2]
        gram_sum = grams[start : start + stat_m.shape[0]]
        start += stat_m.shape[0]
        new_stats.append(BETA_SECOND * stat_m + (1.0 - BETA_SECOND) * gram_sum)
    new_bases = renew_all(new_stats, [state[3] for state in states])
    for mat_index in range(6):
        first_m, second_m, stat_m, basis_m = states[mat_index]
        new_weight, new_first, new_second = rotated_update(
            matrices[mat_index],
            reduced[mat_index],
            first_m,
            second_m,
            basis_m,
            RATES[mat_index],
        )
        if mat_index == 1:
            new_weight = clip_columns(new_weight, clip_own, NOPE_DIM + ROPE_DIM, True)
        if mat_index == 2:
            new_weight = clip_columns(new_weight, clip_own, NOPE_DIM + VALUE_DIM, False)
        results.extend(
            [
                new_weight,
                new_weight.astype(jnp.bfloat16),
                new_first,
                new_second,
                new_stats[mat_index],
                new_bases[mat_index],
            ]
        )
    gains_first_new = BETA_FIRST * gains_first + (1.0 - BETA_FIRST) * gains_grad
    gains_second_new = BETA_SECOND * gains_second + (1.0 - BETA_SECOND) * gains_grad * gains_grad
    gains_step = (
        gains_first_new
        / (1.0 - BETA_FIRST**STEP_COUNT)
        / (jnp.sqrt(gains_second_new / (1.0 - BETA_SECOND**STEP_COUNT)) + ADAM_EPS)
    )
    results.extend(
        [gains - GAIN_RATE * (gains_step + DECAY * gains), gains_first_new, gains_second_new]
    )
    return tuple(results)


def solution(mesh):
    placed = (
        P(None, ("dp", "mp"), None),
        P(None, ("dp", "mp"), None),
        P(None, "dp", None),
        P("dp", "mp"),
        P("dp", "mp"),
        P("dp", "mp"),
        P("dp", None, None),
        P("dp", None, None),
        P("dp", "mp"),
        P("dp", "mp"),
        P("dp", "mp"),
        P("dp", None, None),
        P("dp", None, None),
        P("dp", "mp"),
        P("dp", "mp"),
        P("dp", "mp"),
        P("dp", None, None),
        P("dp", None, None),
        P("dp", "mp"),
        P("dp", "mp"),
        P("dp", "mp"),
        P("dp", None, None),
        P("dp", None, None),
        P("dp", None, "mp"),
        P("dp", None, "mp"),
        P("dp", None, "mp"),
        P("dp", None, None),
        P("dp", None, None),
        P("dp", "mp"),
        P("dp", "mp"),
        P("dp", "mp"),
        P("dp", None, None),
        P("dp", None, None),
        P("dp"),
        P("dp"),
        P("dp"),
    )
    return jax.shard_map(
        on_device,
        mesh=mesh,
        in_specs=placed,
        out_specs=(
            P(None, ("dp", "mp"), None),
            P(None, ("dp", "mp"), None),
            P("dp", "mp"),
            P("dp", "mp"),
            P("dp", "mp"),
            P("dp", "mp"),
            P("dp", None, None),
            P("dp", None, None),
            P("dp", "mp"),
            P("dp", "mp"),
            P("dp", "mp"),
            P("dp", "mp"),
            P("dp", None, None),
            P("dp", None, None),
            P("dp", "mp"),
            P("dp", "mp"),
            P("dp", "mp"),
            P("dp", "mp"),
            P("dp", None, None),
            P("dp", None, None),
            P("dp", "mp"),
            P("dp", "mp"),
            P("dp", "mp"),
            P("dp", "mp"),
            P("dp", None, None),
            P("dp", None, None),
            P("dp", None, "mp"),
            P("dp", None, "mp"),
            P("dp", None, "mp"),
            P("dp", None, "mp"),
            P("dp", None, None),
            P("dp", None, None),
            P("dp", "mp"),
            P("dp", "mp"),
            P("dp", "mp"),
            P("dp", "mp"),
            P("dp", None, None),
            P("dp", None, None),
            P("dp"),
            P("dp"),
            P("dp"),
        ),
        check_vma=False,
    )
```
